1024 devices in a mesh: sec: 128 (over y, z_hi, x, core), row: 8 (over z_lo).
Axes of the slice: x: 4, y: 4, z: 32 (z_hi: 4, z_lo: 8; z = z_hi * 8 + z_lo), core: 2. Of those that a mesh axis runs over, the one named last changes fastest.
Arguments:
- first_pts: float32 [4, 256, 16, 32, 2, 128], P(None, 'sec', 'row'), may hold values from -1 to 1
- second_pts: float32 [4, 256, 16, 32, 2, 128], P(None, 'sec', 'row'), may hold values from -1 to 1
- counts: int32 [4, 256, 16, 32], P(None, 'sec', 'row'), may hold values from 32 to 128, as said below
Outputs:
- affines: float32 [6, 256, 16, 32], P(None, 'sec', 'row')
- residual: float32 [4, 256, 16, 32, 2, 128], P(None, 'sec', 'row')
The draws below stay inside these ranges and needn't reach their ends.
Inputs may be any that keep to these rules, and one draw needn't show every extreme that they name: `counts`: points 0 to the count minus one of a pair are live, the rest are padding.
All inputs are finite; a program needn't handle non-finite values.
Results may differ from the reference program's by a relative error of at most 0.035.
Values sent between devices are 32-bit elements; how exact they have to be, the bound alone decides.
No kernel may reach another device: no remote copies, remote signals or barrier semaphores. Data moves between devices by JAX's collectives and lax.ppermute only.
A program may use at most 64 MiB of HBM per device.

```python
import jax
import jax.numpy as jnp
from jax import lax

COLS = 32
P_SIZE = 128
ITERS = 4
NSEC = 256
NROWS = 16


def draw_counts(key, part):
    base_counts = jax.random.randint(jax.random.fold_in(key, 11), (4, NSEC, NROWS, COLS), P_SIZE // 4, P_SIZE + 1)
    chosen = jax.random.randint(jax.random.fold_in(key, 12), (NSEC,), 0, COLS)
    chosen_cell = jnp.arange(COLS)[None, None, None, :] == chosen[None, :, None, None]
    kind_zero = jnp.arange(4)[:, None, None, None] == 0
    row_zero = jnp.arange(NROWS)[None, None, :, None] == 0
    return jnp.where(chosen_cell & kind_zero & row_zero, P_SIZE, base_counts).astype(jnp.int32)


def levels(key, extent, shards, low, high):
    factor_of = 1.0
    for dim, blocks in shards:
        draws = jax.random.uniform(jax.random.fold_in(jax.random.fold_in(key, 6), dim), (blocks,), jnp.float32, low / len(shards), high / len(shards))
        factor_of = factor_of * jnp.repeat(jnp.exp(draws), extent[dim] // blocks).reshape((-1,) + (1,) * (len(extent) - 1 - dim))
    return factor_of


def setup_inputs(seed: int = 0) -> dict:
    splits = jax.random.split(jax.random.key(seed), 4)
    first_pts = jnp.clip(jax.random.uniform(splits[0], (4, NSEC, NROWS, COLS, 2, P_SIZE), jnp.float32, -1.0, 1.0) * levels(splits[0], (4, NSEC, NROWS, COLS, 2, P_SIZE), ((1, 128), (2, 8)), -0.4, 0.0), -1.0, 1.0)
    second_pts = jnp.clip(jax.random.uniform(splits[1], (4, NSEC, NROWS, COLS, 2, P_SIZE), jnp.float32, -1.0, 1.0) * levels(splits[1], (4, NSEC, NROWS, COLS, 2, P_SIZE), ((1, 128), (2, 8)), -0.4, 0.0), -1.0, 1.0)
    counts = draw_counts(jax.random.fold_in(splits[3], 71), 0)
    return {"first_pts": first_pts, "second_pts": second_pts, "counts": counts}


reg_root = (0.7, 0.7, 0.3, 0.7, 0.7, 0.3)
kind_moves = ((2, 1), (1, 1), (0, 1), (0, 2))


def transform(affine, points):
    coord_x = points[..., 0, :]
    coord_y = points[..., 1, :]
    factor = [affine[number][..., None] for number in range(6)]
    return jnp.stack([factor[0] * coord_x + factor[1] * coord_y + factor[2],
                      factor[3] * coord_x + factor[4] * coord_y + factor[5]], axis=-2)


def moments(errors, points):
    err_x = errors[..., 0, :]
    err_y = errors[..., 1, :]
    pos_x = points[..., 0, :]
    pos_y = points[..., 1, :]
    return jnp.stack([jnp.sum(err_x * pos_x, -1), jnp.sum(err_x * pos_y, -1), jnp.sum(err_x, -1),
                      jnp.sum(err_y * pos_x, -1), jnp.sum(err_y * pos_y, -1), jnp.sum(err_y, -1)], 0)


def toward(values, axis_no, offset):
    length = values.shape[axis_no]
    kept = lax.slice_in_dim(values, offset, length, axis=axis_no)
    zeros = jnp.zeros_like(lax.slice_in_dim(values, 0, offset, axis=axis_no))
    return jnp.concatenate([kept, zeros], axis=axis_no)


def away(values, axis_no, offset):
    length = values.shape[axis_no]
    kept = lax.slice_in_dim(values, 0, length - offset, axis=axis_no)
    zeros = jnp.zeros_like(lax.slice_in_dim(values, 0, offset, axis=axis_no))
    return jnp.concatenate([zeros, kept], axis=axis_no)


def inner(list_a, reg_a, list_b, reg_b):
    summed = jnp.sum(reg_a * reg_b)
    for kind_no in range(4):
        summed = summed + jnp.sum(list_a[kind_no] * list_b[kind_no])
    return summed


def reference(first_pts, second_pts, counts):
    n_sec = counts.shape[1]
    n_row = counts.shape[2]
    n_col = counts.shape[3]
    width = first_pts.shape[-1]
    live = jnp.arange(width)[None, None, None, None, :] < counts[..., None]
    sec_ids = jnp.arange(n_sec)[:, None, None]
    row_ids = jnp.arange(n_row)[None, :, None]
    col_ids = jnp.arange(n_col)[None, None, :]
    valid = [col_ids < n_col - 1, row_ids < n_row - 1, sec_ids < n_sec - 1, sec_ids < n_sec - 2]
    masks = [jnp.where(live[kind_no] & valid[kind_no][..., None], 1.0, 0.0).astype(jnp.float32)[..., None, :]
             for kind_no in range(4)]
    root = jnp.array(reg_root, jnp.float32)[:, None, None, None]

    def forward(affine):
        result = []
        for kind_no in range(4):
            axis_no, offset = kind_moves[kind_no]
            image = toward(transform(affine, second_pts[kind_no]), axis_no, offset)
            result.append(masks[kind_no] * (transform(affine, first_pts[kind_no]) - image))
        return result

    def backward(errors, reg_part):
        summed = root * reg_part
        for kind_no in range(4):
            axis_no, offset = kind_moves[kind_no]
            moved = away(errors[kind_no], axis_no, offset)
            summed = summed + moments(errors[kind_no], first_pts[kind_no]) - moments(moved, second_pts[kind_no])
        return summed

    ones = jnp.ones((1, n_sec, n_row, n_col), jnp.float32)
    identity = jnp.array([1.0, 0.0, 0.0, 0.0, 1.0, 0.0], jnp.float32)[:, None, None, None] * ones
    resid = forward(-identity)
    resid_reg = jnp.zeros((6, n_sec, n_row, n_col), jnp.float32)
    search = backward(resid, resid_reg)
    image = forward(search)
    image_reg = root * search
    gamma = jnp.sum(search * search)
    curv = inner(image, image_reg, image, image_reg)
    direction = search
    along = image
    along_reg = image_reg
    solution = jnp.zeros((6, n_sec, n_row, n_col), jnp.float32)
    for sweep in range(ITERS):
        alpha = gamma / curv
        solution = solution + alpha * direction
        resid = [resid[kind_no] - alpha * along[kind_no] for kind_no in range(4)]
        resid_reg = resid_reg - alpha * along_reg
        if sweep < ITERS - 1:
            search = backward(resid, resid_reg)
            image = forward(search)
            image_reg = root * search
            gamma_new = jnp.sum(search * search)
            omega = inner(image, image_reg, image, image_reg)
            cross = inner(image, image_reg, along, along_reg)
            beta = gamma_new / gamma
            direction = search + beta * direction
            along = [image[kind_no] + beta * along[kind_no] for kind_no in range(4)]
            along_reg = image_reg + beta * along_reg
            curv = omega + 2.0 * beta * cross + beta * beta * curv
            gamma = gamma_new
    return solution, jnp.stack(resid, 0)
```

```python
import functools

import jax
import jax.numpy as jnp
from jax import lax
from jax.experimental import pallas as pl
from jax.experimental.pallas import tpu as pltpu
from jax.sharding import Mesh
from jax.sharding import PartitionSpec as P

ITERS = 4
SPAN = 1024.0
SHIFT = 512.0
HALF = SHIFT / SPAN
SQUARES = (0.49, 0.49, 0.09)
SYM = ((0, 0), (0, 1), (0, 2), (1, 1), (1, 2), (2, 2))
SEC_AXES = ("y", "zhi", "x", "core")
GROUP = ("x", "core")
OTHERS = ("y", "zhi", "row")

ROWS = 80
AT_C = 12
AT_LOW = 48
AT_SEND = 57


def sym_at(a, b):
    return SYM.index((min(a, b), max(a, b)))


def roll(value, shift, axis):
    size = value.shape[axis]
    return pltpu.roll(value, shift % size, axis)


def lane_bits(shape):
    lane = lax.broadcasted_iota(jnp.int32, shape, len(shape) - 1)
    return (lane // 32) % 2 == 0, lane < 64


def block_sums(first, second, live):
    u, v = first
    p, q = second
    dx = p - u
    dy = q - v

    def red(z):
        return jnp.sum(z, axis=0, keepdims=True)

    su, sv, sp, sq, n = red(u), red(v), red(p), red(q), red(live)
    F = [red(u * u), red(u * v), su, red(v * v), sv, n]
    G = [red(p * p), red(p * q), sp, red(q * q), sq, n]
    C = [red(u * p), red(u * q), su, red(v * p), red(v * q), sv, sp, sq, n]
    tx, ty = red(dx), red(dy)
    s1 = [red(dx * u), red(dx * v), tx, red(dy * u), red(dy * v), ty]
    s2 = [red(dx * p), red(dx * q), tx, red(dy * p), red(dy * q), ty]
    return F, G, C, s1, s2


def gram_kernel(flags, f_ref, g_ref, counts_ref, up_ref, next_ref, low_ref, packet, kept):
    row_zero, sec_zero = lane_bits((1, 128))
    lane = lax.broadcasted_iota(jnp.int32, (1, 128), 1)
    last_row = flags[0] == 1
    last_sec = flags[1] == 1

    def pair_rows(ref, start, count, comp):
        return ref[pl.ds(2 * start + comp, count, stride=2), :]

    def own(ref, kind):
        return [pair_rows(ref, kind * 128, 128, comp).T for comp in range(2)]

    counts = counts_ref[...].astype(jnp.float32)
    zero = jnp.zeros((1, 128), jnp.float32)
    alive = [
        jnp.where(lane % 32 == 31, zero, counts[0:1]),
        jnp.where(jnp.logical_and(jnp.logical_not(row_zero), last_row), zero, counts[1:2]),
        jnp.where(jnp.logical_and(jnp.logical_not(sec_zero), last_sec), zero, counts[2:3]),
        jnp.where(last_sec, zero, counts[3:4]),
    ]
    point = lax.broadcasted_iota(jnp.int32, (128, 128), 0).astype(jnp.float32)

    def masked(points, count):
        live = jnp.where(point < count, 1.0, 0.0)
        return [z * live for z in points], live

    def second_of(kind):
        if kind == 0:
            return [roll(z, -1, 1) for z in own(g_ref, 0)]
        out = []
        for comp in range(2):
            if kind == 1:
                parts = [
                    pair_rows(g_ref, 128 + 32, 32, comp),
                    pair_rows(next_ref, 0, 32, comp),
                    pair_rows(g_ref, 128 + 96, 32, comp),
                    pair_rows(next_ref, 32, 32, comp),
                ]
            elif kind == 2:
                parts = [pair_rows(g_ref, 256 + 64, 64, comp), pair_rows(up_ref, 0, 64, comp)]
            else:
                parts = [pair_rows(up_ref, 64, 128, comp)]
            out.append(jnp.concatenate(parts, axis=0).T)
        return out

    D = [zero] * 6
    S = [zero] * 6
    unit = 1.0 / SPAN

    def put(row, value):
        packet[row : row + 1, :] = value

    for kind in range(4):
        first, live = masked(own(f_ref, kind), alive[kind])
        second, _ = masked(second_of(kind), alive[kind])
        kept[5 * kind] = first[0]
        kept[5 * kind + 1] = first[1]
        kept[5 * kind + 2] = second[0]
        kept[5 * kind + 3] = second[1]
        kept[5 * kind + 4] = live
        F, G, C, s1, s2 = block_sums(first, second, live)
        D = [a + b for a, b in zip(D, F)]
        S = [a + b for a, b in zip(S, s1)]
        for i in range(9):
            put(AT_C + 9 * kind + i, C[i] * unit)
        if kind == 0:
            D = [a + roll(b, 1, 1) for a, b in zip(D, G)]
            S = [a - roll(b, 1, 1) for a, b in zip(S, s2)]
        elif kind == 1:
            D = [a + jnp.where(row_zero, zero, roll(b, 32, 1)) for a, b in zip(D, G)]
            S = [a - jnp.where(row_zero, zero, roll(b, 32, 1)) for a, b in zip(S, s2)]
        elif kind == 2:
            D = [a + jnp.where(sec_zero, zero, roll(b, 64, 1)) for a, b in zip(D, G)]
            S = [a - jnp.where(sec_zero, zero, roll(b, 64, 1)) for a, b in zip(S, s2)]
        if kind >= 2:
            base = AT_SEND + 9 * (kind - 2)
            put(base, G[0] * unit)
            put(base + 1, G[1] * unit)
            put(base + 2, G[3] * unit)
            for i in range(6):
                put(base + 3 + i, s2[i])

    low_count = jnp.where(row_zero, zero, low_ref[128:129, :])
    first = []
    second = []
    for comp in range(2):
        low = [pair_rows(low_ref, 32 * sec, 32, comp) for sec in range(2)]
        first.append(jnp.concatenate([low[0], low[0], low[1], low[1]], axis=0).T)
        mine = [pair_rows(g_ref, 128 + 64 * sec, 32, comp) for sec in range(2)]
        second.append(jnp.concatenate([mine[0], mine[0], mine[1], mine[1]], axis=0).T)
    first, live = masked(first, low_count)
    second, _ = masked(second, low_count)
    F, G, C, s1, s2 = block_sums(first, second, live)
    for i in range(9):
        put(AT_LOW + i, C[i] * unit)
    D = [a + jnp.where(row_zero, roll(b, -32, 1), zero) for a, b in zip(D, G)]
    S = [a - jnp.where(row_zero, roll(b, -32, 1), zero) for a, b in zip(S, s2)]

    for i in range(6):
        a, b = SYM[i]
        put(i, D[i] * unit + ((SQUARES[a] - SHIFT) * unit if a == b else 0.0))
        put(6 + i, S[i])
    for row in range(AT_SEND + 18, ROWS):
        put(row, zero)


def from_above(value):
    return roll(value, -1, 0)


def from_below(value):
    return roll(value, 1, 0)


def seconds_of(value, value_next, bits):
    row_zero, sec_zero = bits
    half = roll(value, 64, 1)
    return [
        roll(value, -1, 1),
        jnp.where(row_zero, roll(value, -32, 1), roll(value_next, 32, 1)),
        jnp.where(sec_zero, half, from_above(half)),
        from_above(value),
    ]


def window_kernel(got, blocks, start):
    n_dev = got.shape[0] // (2 * ROWS)

    def row(i):
        parts = []
        for slot, dev in [(1, d) for d in range(n_dev // 2, n_dev)] + [(0, d) for d in range(n_dev)] + [
            (1, d) for d in range(n_dev // 2)
        ]:
            at = (dev * 2 + slot) * ROWS + i
            parts.append(got[at : at + 1, :])
        return jnp.concatenate(parts, axis=0)

    row_zero, sec_zero = lane_bits((2 * n_dev, 128))
    zero = jnp.zeros((2 * n_dev, 128), jnp.float32)
    C = {(k, i): row(AT_C + 9 * k + i) for k in range(4) for i in range(9)}
    for (k, i), value in C.items():
        blocks[6 + 9 * k + i] = value
    for i in range(9):
        blocks[42 + i] = row(AT_LOW + i)

    def pushed(kind, value):
        if kind == 2:
            return from_below(jnp.where(sec_zero, roll(value, 64, 1), zero))
        return from_below(value)

    D = [row(i) for i in range(6)]
    S = [row(6 + i) for i in range(6)]
    for kind in (2, 3):
        base = AT_SEND + 9 * (kind - 2)
        G = [row(base), row(base + 1), C[kind, 6], row(base + 2), C[kind, 7], C[kind, 8]]
        D = [a + pushed(kind, b) for a, b in zip(D, G)]
        S = [a - pushed(kind, row(base + 3 + i)) for i, a in enumerate(S)]
    for i in range(6):
        blocks[i] = D[i]
        start[i] = S[i]


def apply_kernel(blocks, v_ref, next_ref, low_ref, out):
    shape = v_ref.shape[1:]
    bits = lane_bits(shape)
    row_zero, sec_zero = bits
    v = [v_ref[i] for i in range(6)]
    after = [seconds_of(v[i], next_ref[i], bits) for i in range(6)]
    total = [None] * 6
    for half in range(2):
        a = v[3 * half : 3 * half + 3]
        for i in range(3):
            total[3 * half + i] = sum(blocks[sym_at(i, j)] * a[j] for j in range(3))
    for kind in range(4):
        C = [[blocks[6 + 9 * kind + 3 * i + j] for j in range(3)] for i in range(3)]
        for half in range(2):
            a = v[3 * half : 3 * half + 3]
            b = [after[3 * half + j][kind] for j in range(3)]
            for i in range(3):
                total[3 * half + i] -= C[i][0] * b[0] + C[i][1] * b[1] + C[i][2] * b[2]
            for j in range(3):
                t = C[0][j] * a[0] + C[1][j] * a[1] + C[2][j] * a[2]
                if kind == 0:
                    t = roll(t, 1, 1)
                elif kind == 1:
                    low = [low_ref[3 * half + i] for i in range(3)]
                    t_low = sum(blocks[42 + 3 * i + j] * low[i] for i in range(3))
                    t = jnp.where(row_zero, roll(t_low, -32, 1), roll(t, 32, 1))
                elif kind == 2:
                    t = roll(t, 64, 1)
                    t = jnp.where(sec_zero, from_below(t), t)
                else:
                    t = from_below(t)
                total[3 * half + j] -= t
    for i in range(6):
        out[i] = total[i]


def moments_kernel(blocks, v0, v1, v2, v3, next_ref, out):
    shape = v3.shape[1:]
    bits = lane_bits(shape)
    quarter = shape[0] // 4
    dev = lax.broadcasted_iota(jnp.int32, shape, 0)
    inside = jnp.logical_and(dev >= quarter, dev < 3 * quarter)
    vs = [[ref[i] for i in range(6)] for ref in (v0, v1, v2, v3)]

    def dot(left, right):
        return sum(a * b for a, b in zip(left, right))

    products = [dot(vs[n // 2], vs[n - n // 2]) for n in range(7)]
    energy = 0.0
    after = [seconds_of(vs[3][i], next_ref[i], bits) for i in range(6)]
    for half in range(2):
        a = vs[3][3 * half : 3 * half + 3]
        for i in range(3):
            inner = sum(blocks[sym_at(i, j)] * a[j] for j in range(3))
            for kind in range(4):
                cross = sum(blocks[6 + 9 * kind + 3 * i + j] * after[3 * half + j][kind] for j in range(3))
                inner = inner - 2.0 * cross
            energy = energy + a[i] * inner
    products.append(energy)
    lane = lax.broadcasted_iota(jnp.int32, (1, 128), 1)
    packed = jnp.zeros((1, 128), jnp.float32)
    for n, value in enumerate(products):
        value = jnp.where(inside, value, 0.0)
        value = jnp.sum(jnp.sum(value, axis=0, keepdims=True), axis=1, keepdims=True)
        packed = jnp.where(lane == n, value, packed)
    out[...] = packed


def coefficients(moments):
    zero = jnp.zeros_like(moments[0])

    def inner(s, p, offset):
        total = zero
        for i, a in enumerate(s):
            for j, b in enumerate(p):
                total = total + a * b * moments[i + j + offset]
        return total

    def energy(p):
        return inner(p, p, 1) + HALF * inner(p, p, 0)

    s = [zero + 1.0]
    p = [zero + 1.0]
    x = [zero] * ITERS
    gamma = inner(s, s, 0)
    for sweep in range(ITERS):
        alpha = gamma / energy(p)
        x = [x[i] + (alpha * p[i] if i < len(p) else 0.0) for i in range(ITERS)]
        if sweep < ITERS - 1:
            image = [(p[i - 1] if i else 0.0) + (HALF * p[i] if i < len(p) else 0.0) for i in range(len(p) + 1)]
            s = [(s[i] if i < len(s) else 0.0) - alpha * image[i] for i in range(len(image))]
            gamma_new = inner(s, s, 0)
            beta = gamma_new / gamma
            p = [s[i] + (beta * p[i] if i < len(p) else 0.0) for i in range(len(s))]
            gamma = gamma_new
    return [value * (1.0 / SPAN) for value in x]


def finish_kernel(place, sums, v0, v1, v2, v3, n0, n1, n2, n3, kept, affines, residual):
    total = jnp.sum(sums[...], axis=0, keepdims=True)
    lane = lax.broadcasted_iota(jnp.int32, (1, 128), 1)
    moments = [jnp.sum(jnp.where(lane == n, total, 0.0), axis=1, keepdims=True) for n in range(8)]
    weights = coefficients(moments)
    at = place[0]
    row_zero, sec_zero = lane_bits((1, 128))

    def mix(refs, i, dev):
        return sum(w * ref[i, pl.ds(dev, 1), :] for w, ref in zip(weights, refs))

    vs = (v0, v1, v2, v3)
    x = [mix(vs, i, at) for i in range(6)]
    above = [mix(vs, i, at + 1) for i in range(6)]
    beside = [mix((n0, n1, n2, n3), i, at) for i in range(6)]
    for i in range(6):
        affines[i : i + 1, :] = x[i]
    for kind in range(4):
        if kind == 0:
            b = [roll(z, -1, 1) for z in x]
        elif kind == 1:
            b = [jnp.where(row_zero, roll(z, -32, 1), roll(w, 32, 1)) for z, w in zip(x, beside)]
        elif kind == 2:
            b = [jnp.where(sec_zero, roll(z, 64, 1), roll(w, 64, 1)) for z, w in zip(x, above)]
        else:
            b = above
        u, v, p, q, live = (kept[5 * kind + i] for i in range(5))
        for comp in range(2):
            o = 3 * comp
            r = (p - u) if comp == 0 else (q - v)
            r = r - (x[o] * u + x[o + 1] * v) + (b[o] * p + b[o + 1] * q) - live * (x[o + 2] - b[o + 2])
            residual[pl.ds(kind * 256 + comp, 128, stride=2), :] = r.T


def shape_of(*shape):
    return jax.ShapeDtypeStruct(shape, jnp.float32)


def call(kernel, outs, *args, scalars=0, interpret=False):
    spaces = [pl.BlockSpec(memory_space=pltpu.SMEM)] * scalars
    spaces += [pl.BlockSpec(memory_space=pltpu.VMEM)] * (len(args) - scalars)
    many = isinstance(outs, (list, tuple))
    out_specs = [pl.BlockSpec(memory_space=pltpu.VMEM) for _ in outs] if many else pl.BlockSpec(memory_space=pltpu.VMEM)
    return pl.pallas_call(kernel, out_shape=outs, in_specs=spaces, out_specs=out_specs, interpret=interpret)(*args)


def shifted(value, axes, steps):
    count = lax.axis_size(axes)
    pairs = [(i, i + steps) for i in range(count) if 0 <= i + steps < count]
    return lax.ppermute(value, axes, pairs)


def per_device(interpret, first_pts, second_pts, counts):
    run = functools.partial(call, interpret=interpret)
    n_sec = lax.axis_size(SEC_AXES)
    n_dev = lax.axis_size(GROUP)
    n_group = n_sec // n_dev
    sec = lax.axis_index(SEC_AXES)
    member = lax.axis_index(GROUP)
    f = first_pts.reshape(1024, 128)
    g = second_pts.reshape(1024, 128)
    lives = counts.reshape(4, 128)

    up = shifted(jnp.concatenate([g[512:640], g[768:1024]], axis=0), SEC_AXES, -1)
    beside = shifted(jnp.concatenate([g[256:320], g[384:448]], axis=0), "row", -1)
    odd = jnp.concatenate(
        [f[320:384], f[448:512], jnp.broadcast_to(lives[1:2].astype(jnp.float32), (8, 128))], axis=0
    )
    low = shifted(odd, "row", 1)
    flags = jnp.stack(
        [
            (lax.axis_index("row") == lax.axis_size("row") - 1).astype(jnp.int32),
            (sec == n_sec - 1).astype(jnp.int32),
        ]
    )
    packet, kept = run(gram_kernel, [shape_of(ROWS, 128), shape_of(20, 128, 128)], flags, f, g, lives, up, beside, low, scalars=1)

    half = n_dev // 2
    pairs = []
    for group in range(n_group):
        for dev in range(n_dev):
            source = group + (1 if dev < half else -1)
            if 0 <= source < n_group:
                pairs.append((source * n_dev + dev, group * n_dev + dev))
    other = lax.ppermute(packet, SEC_AXES, pairs)
    mine = jnp.concatenate([packet, other], axis=0)
    got = lax.all_to_all(jnp.broadcast_to(mine[None], (n_dev, 2 * ROWS, 128)), GROUP, 0, 0, tiled=False)
    blocks, v0 = run(
        window_kernel, [shape_of(51, 2 * n_dev, 128), shape_of(6, 2 * n_dev, 128)], got.reshape(n_dev * 2 * ROWS, 128)
    )
    vs = [v0]
    nexts = []
    for step in range(ITERS - 1):
        v = vs[-1]
        nexts.append(shifted(v, "row", -1))
        lows = shifted(v, "row", 1)
        vs.append(run(apply_kernel, shape_of(*v.shape), blocks, v, nexts[-1], lows))
    nexts.append(shifted(vs[-1], "row", -1))
    part = run(moments_kernel, shape_of(1, 128), blocks, *vs, nexts[-1])
    n_other = lax.axis_size(OTHERS)
    sums = lax.all_to_all(jnp.broadcast_to(part[None], (n_other, 1, 128)), OTHERS, 0, 0, tiled=False)
    place = (member + n_dev // 2).astype(jnp.int32).reshape(1)
    affines, residual = run(
        finish_kernel,
        [shape_of(6, 128), shape_of(1024, 128)],
        place,
        sums.reshape(n_other, 128),
        *vs,
        *nexts,
        kept,
        scalars=1,
    )
    return affines.reshape((6,) + counts.shape[1:]), residual.reshape(first_pts.shape)


def split_mesh(mesh):
    n_row = mesh.shape["row"]
    return Mesh(mesh.devices.reshape(4, 4, 4, 2, n_row), SEC_AXES + ("row",))


def solution(mesh, inner=None, interpret=False):
    inner = inner or split_mesh(mesh)
    in_specs = (
        P(None, SEC_AXES, "row", None, None, None),
        P(None, SEC_AXES, "row", None, None, None),
        P(None, SEC_AXES, "row", None),
    )
    out_specs = (P(None, SEC_AXES, "row", None), P(None, SEC_AXES, "row", None, None, None))
    return jax.shard_map(
        functools.partial(per_device, interpret), mesh=inner, in_specs=in_specs, out_specs=out_specs, check_vma=False
    )
```

```python
import functools

import jax
import jax.numpy as jnp
from jax import lax
from jax.experimental import pallas as pl
from jax.experimental.pallas import tpu as pltpu
from jax.sharding import Mesh
from jax.sharding import PartitionSpec as P

ITERS = 4
SPAN = 1024.0
SHIFT = 512.0
HALF = SHIFT / SPAN
SQUARES = (0.49, 0.49, 0.09)
SYM = ((0, 0), (0, 1), (0, 2), (1, 1), (1, 2), (2, 2))
SEC_AXES = ("y", "zhi", "x", "core")
GROUP = ("x", "core")
OTHERS = ("y", "zhi", "row")

ROWS = 72
AT_C = 12
AT_SEND = 48
USED = 66
AT_E = 66
AT_E2 = 132
DOUBLE = 160
BEYOND = [AT_C + 9 + i for i in range(9)] + [6 + i for i in range(6)]
BEYOND += [AT_SEND + 3 + i for i in range(6)] + [AT_SEND + 12 + i for i in range(6)]


def sym_at(a, b):
    return SYM.index((min(a, b), max(a, b)))


def roll(value, shift, axis):
    size = value.shape[axis]
    return pltpu.roll(value, shift % size, axis)


def lane_bits(shape):
    lane = lax.broadcasted_iota(jnp.int32, shape, len(shape) - 1)
    return (lane // 32) % 2 == 0, lane < 64


def counts_row(ref, kind):
    cells = [ref[kind, sec, row : row + 1, :] for sec in range(2) for row in range(2)]
    return jnp.concatenate(cells, axis=1).astype(jnp.float32)


def block_sums(first, second, live):
    u, v = first
    p, q = second
    dx = p - u
    dy = q - v

    def red(z):
        return jnp.sum(z, axis=0, keepdims=True)

    su, sv, sp, sq, n = red(u), red(v), red(p), red(q), red(live)
    F = [red(u * u), red(u * v), su, red(v * v), sv, n]
    G = [red(p * p), red(p * q), sp, red(q * q), sq, n]
    C = [red(u * p), red(u * q), su, red(v * p), red(v * q), sv, sp, sq, n]
    tx, ty = red(dx), red(dy)
    s1 = [red(dx * u), red(dx * v), tx, red(dy * u), red(dy * v), ty]
    s2 = [red(dx * p), red(dx * q), tx, red(dy * p), red(dy * q), ty]
    return F, G, C, s1, s2


def gram_kernel(flags, f_ref, g_ref, counts_ref, up_ref, next_ref, low_ref, packet, kept):
    row_zero, sec_zero = lane_bits((1, 128))
    lane = lax.broadcasted_iota(jnp.int32, (1, 128), 1)
    last_row = flags[0] == 1
    last_sec = flags[1] == 1

    def pair_rows(ref, start, count, comp):
        return ref[pl.ds(2 * start + comp, count, stride=2), :]

    def own(ref, kind):
        return [pair_rows(ref, kind * 128, 128, comp).T for comp in range(2)]

    zero = jnp.zeros((1, 128), jnp.float32)
    counts = [counts_row(counts_ref, kind) for kind in range(4)]
    alive = [
        jnp.where(lane % 32 == 31, zero, counts[0]),
        jnp.where(jnp.logical_and(jnp.logical_not(row_zero), last_row), zero, counts[1]),
        jnp.where(jnp.logical_and(jnp.logical_not(sec_zero), last_sec), zero, counts[2]),
        jnp.where(last_sec, zero, counts[3]),
    ]
    point = lax.broadcasted_iota(jnp.int32, (128, 128), 0).astype(jnp.float32)

    def masked(points, count):
        live = jnp.where(point < count, 1.0, 0.0)
        return [z * live for z in points], live

    def second_of(kind):
        if kind == 0:
            return [roll(z, -1, 1) for z in own(g_ref, 0)]
        out = []
        for comp in range(2):
            if kind == 1:
                parts = [
                    pair_rows(g_ref, 128 + 32, 32, comp),
                    pair_rows(next_ref, 0, 32, comp),
                    pair_rows(g_ref, 128 + 96, 32, comp),
                    pair_rows(next_ref, 32, 32, comp),
                ]
            elif kind == 2:
                parts = [pair_rows(g_ref, 256 + 64, 64, comp), pair_rows(up_ref, 0, 64, comp)]
            else:
                parts = [pair_rows(up_ref, 64, 128, comp)]
            out.append(jnp.concatenate(parts, axis=0).T)
        return out

    D = [zero] * 6
    S = [zero] * 6
    unit = 1.0 / SPAN

    def put(row, value):
        packet[row : row + 1, :] = value

    for kind in range(4):
        first, live = masked(own(f_ref, kind), alive[kind])
        second, _ = masked(second_of(kind), alive[kind])
        kept[5 * kind] = first[0]
        kept[5 * kind + 1] = first[1]
        kept[5 * kind + 2] = second[0]
        kept[5 * kind + 3] = second[1]
        kept[5 * kind + 4] = live
        F, G, C, s1, s2 = block_sums(first, second, live)
        D = [a + b for a, b in zip(D, F)]
        S = [a + b for a, b in zip(S, s1)]
        for i in range(9):
            put(AT_C + 9 * kind + i, C[i] * unit)
        if kind == 0:
            D = [a + roll(b, 1, 1) for a, b in zip(D, G)]
            S = [a - roll(b, 1, 1) for a, b in zip(S, s2)]
        elif kind == 1:
            D = [a + jnp.where(row_zero, zero, roll(b, 32, 1)) for a, b in zip(D, G)]
            S = [a - jnp.where(row_zero, zero, roll(b, 32, 1)) for a, b in zip(S, s2)]
        elif kind == 2:
            D = [a + jnp.where(sec_zero, zero, roll(b, 64, 1)) for a, b in zip(D, G)]
            S = [a - jnp.where(sec_zero, zero, roll(b, 64, 1)) for a, b in zip(S, s2)]
        if kind >= 2:
            base = AT_SEND + 9 * (kind - 2)
            put(base, G[0] * unit)
            put(base + 1, G[1] * unit)
            put(base + 2, G[3] * unit)
            for i in range(6):
                put(base + 3 + i, s2[i])

    low_count = jnp.where(row_zero, zero, low_ref[128:129, :])
    first = []
    second = []
    for comp in range(2):
        low = [pair_rows(low_ref, 32 * sec, 32, comp) for sec in range(2)]
        first.append(jnp.concatenate([low[0], low[0], low[1], low[1]], axis=0).T)
        mine = [pair_rows(g_ref, 128 + 64 * sec, 32, comp) for sec in range(2)]
        second.append(jnp.concatenate([mine[0], mine[0], mine[1], mine[1]], axis=0).T)
    first, live = masked(first, low_count)
    second, _ = masked(second, low_count)
    F, G, C, s1, s2 = block_sums(first, second, live)
    D = [a + jnp.where(row_zero, roll(b, -32, 1), zero) for a, b in zip(D, G)]
    S = [a - jnp.where(row_zero, roll(b, -32, 1), zero) for a, b in zip(S, s2)]

    for i in range(6):
        a, b = SYM[i]
        put(i, D[i] * unit + ((SQUARES[a] - SHIFT) * unit if a == b else 0.0))
        put(6 + i, S[i])
    for row in range(AT_SEND + 18, ROWS):
        put(row, zero)


def from_above(value):
    return roll(value, -1, 0)


def from_below(value):
    return roll(value, 1, 0)


def pack_up_kernel(g_ref, up, sems):
    copies = [
        pltpu.make_async_copy(g_ref.at[pl.ds(512, 128)], up.at[pl.ds(0, 128)], sems.at[0]),
        pltpu.make_async_copy(g_ref.at[pl.ds(768, 256)], up.at[pl.ds(128, 256)], sems.at[1]),
    ]
    for copy in copies:
        copy.start()
    for copy in copies:
        copy.wait()


def pack_rows_kernel(f_ref, g_ref, counts_ref, beside, odd, sems):
    copies = [
        pltpu.make_async_copy(g_ref.at[pl.ds(256, 64)], beside.at[pl.ds(0, 64)], sems.at[0]),
        pltpu.make_async_copy(g_ref.at[pl.ds(384, 64)], beside.at[pl.ds(64, 64)], sems.at[1]),
        pltpu.make_async_copy(f_ref.at[pl.ds(320, 64)], odd.at[pl.ds(0, 64)], sems.at[2]),
        pltpu.make_async_copy(f_ref.at[pl.ds(448, 64)], odd.at[pl.ds(64, 64)], sems.at[3]),
    ]
    for copy in copies:
        copy.start()
    odd[128:136, :] = jnp.broadcast_to(counts_row(counts_ref, 1), (8, 128))
    for copy in copies:
        copy.wait()


def merge_kernel(both, above, below, out):
    row_zero, _ = lane_bits((1, 128))
    for part in range(2):
        at = part * ROWS
        to = part * DOUBLE
        out[to : to + USED, :] = both[at : at + USED, :]
        a = above[at : at + USED, :]
        b = below[at : at + USED, :]
        out[to + AT_E : to + AT_E + USED, :] = jnp.where(row_zero, a, b)
        for i, source in enumerate(BEYOND):
            out[to + AT_E2 + i : to + AT_E2 + i + 1, :] = jnp.where(
                row_zero, b[source : source + 1], a[source : source + 1]
            )
        out[to + AT_E2 + len(BEYOND) : to + DOUBLE, :] = jnp.zeros((DOUBLE - AT_E2 - len(BEYOND), 128), jnp.float32)


class Window:
    def __init__(self, load, n_dev):
        self.load = load
        self.bits = lane_bits((2 * n_dev, 128))

    def seconds(self, v, row_values):
        row_zero, sec_zero = self.bits
        half = roll(v, 64, 1)
        return [
            roll(v, -1, 1),
            row_values,
            jnp.where(sec_zero, half, from_above(half)),
            from_above(v),
        ]

    def row_pairs(self, v, e, e2):
        row_zero, _ = self.bits
        forth, back = roll(v, 32, 1), roll(v, -32, 1)
        own = jnp.where(row_zero, back, roll(e, 32, 1))
        side = jnp.where(row_zero, roll(e2, -32, 1), forth)
        return own, side

    def c(self, side, kind, i, j):
        return self.load(side * 42 + 6 + 9 * kind + 3 * i + j)

    def d(self, side, i, j):
        return self.load(side * 42 + sym_at(i, j))

    def c_e2(self, i, j):
        return self.load(84 + 3 * i + j)

    def transposed(self, c, a):
        return [c(0, j) * a[0] + c(1, j) * a[1] + c(2, j) * a[2] for j in range(3)]

    def apply(self, v, e, e2, sides):
        row_zero, sec_zero = self.bits
        outs = ([None] * 6, [None] * 6)
        for half in range(2):
            span = slice(3 * half, 3 * half + 3)
            sets = (v[span], e[span])
            beyond = e2[span]
            pairs = [self.row_pairs(*z) for z in zip(v[span], e[span], beyond)]
            t_row = [self.transposed(functools.partial(self.c, side, 1), sets[side]) for side in range(2)]
            for side in sides:
                a = sets[side]
                after = [self.seconds(a[j], pairs[j][side]) for j in range(3)]
                total = []
                for i in range(3):
                    y = sum(self.d(side, i, j) * a[j] for j in range(3))
                    for kind in range(4):
                        y = y - sum(self.c(side, kind, i, j) * after[j][kind] for j in range(3))
                    total.append(y)
                col = self.transposed(functools.partial(self.c, side, 0), a)
                one = self.transposed(functools.partial(self.c, side, 2), a)
                two = self.transposed(functools.partial(self.c, side, 3), a)
                if side == 1:
                    outer = self.transposed(self.c_e2, beyond)
                for j in range(3):
                    t = roll(one[j], 64, 1)
                    y = total[j] - roll(col[j], 1, 1) - jnp.where(sec_zero, from_below(t), t) - from_below(two[j])
                    if side == 0:
                        y = y - jnp.where(row_zero, roll(t_row[1][j], -32, 1), roll(t_row[0][j], 32, 1))
                    else:
                        y = y - jnp.where(row_zero, roll(t_row[0][j], -32, 1), roll(outer[j], 32, 1))
                    outs[side][3 * half + j] = y
        return outs


def window_kernel(got, blocks, v0, e0, v1, e1, v2):
    n_dev = got.shape[0] // (2 * DOUBLE)
    row_zero, sec_zero = lane_bits((2 * n_dev, 128))
    zero = jnp.zeros((2 * n_dev, 128), jnp.float32)

    def row(i):
        return jnp.concatenate(
            [got[pl.ds(slot * DOUBLE + i, n_dev, stride=2 * DOUBLE), :] for slot in range(2)], axis=0
        )

    def pushed(kind, value):
        if kind == 2:
            return from_below(jnp.where(sec_zero, roll(value, 64, 1), zero))
        return from_below(value)

    starts = []
    for side, at in enumerate((0, AT_E)):
        for i in range(36):
            blocks[side * 42 + 6 + i] = row(at + AT_C + i)
        D = [row(at + i) for i in range(6)]
        S = [row(at + 6 + i) for i in range(6)]
        for kind in (2, 3):
            base = at + AT_SEND + 9 * (kind - 2)
            last = [blocks[side * 42 + 6 + 9 * kind + i] for i in (6, 7, 8)]
            G = [row(base), row(base + 1), last[0], row(base + 2), last[1], last[2]]
            D = [a + pushed(kind, b) for a, b in zip(D, G)]
            S = [a - pushed(kind, row(base + 3 + i)) for i, a in enumerate(S)]
        for i in range(6):
            blocks[side * 42 + i] = D[i]
        starts.append(S)
    for i in range(9):
        blocks[84 + i] = row(AT_E2 + i)
    outer = [
        row(AT_E2 + 9 + i) - pushed(2, row(AT_E2 + 15 + i)) - pushed(3, row(AT_E2 + 21 + i)) for i in range(6)
    ]
    window = Window(lambda i: blocks[i], n_dev)
    v, e = starts
    w, f = window.apply(v, e, outer, (0, 1))
    last, _ = window.apply(w, f, f, (0,))
    for i in range(6):
        v0[i] = v[i]
        e0[i] = e[i]
        v1[i] = w[i]
        e1[i] = f[i]
        v2[i] = last[i]


def moments_kernel(blocks, v0, v1, v2, above, below, e2, v3, e3, out):
    shape = v2.shape[1:]
    n_dev = shape[0] // 2
    bits = lane_bits(shape)
    row_zero, _ = bits
    window = Window(lambda i: blocks[i], n_dev)
    v = [v2[i] for i in range(6)]
    side = [jnp.where(row_zero, above[i], below[i]) for i in range(6)]
    outer = [jnp.where(row_zero, below[i], above[i]) for i in range(6)]
    w, f = window.apply(v, side, outer, (0, 1))
    for i in range(6):
        e2[i] = side[i]
        v3[i] = w[i]
        e3[i] = f[i]
    vs = [[v0[i] for i in range(6)], [v1[i] for i in range(6)], v, w]

    def dot(left, right):
        return sum(a[:n_dev] * b[:n_dev] for a, b in zip(left, right))

    products = [dot(vs[n // 2], vs[n - n // 2]) for n in range(7)]
    energy = 0.0
    for half in range(2):
        a = w[3 * half : 3 * half + 3]
        b = f[3 * half : 3 * half + 3]
        after = [window.seconds(a[j], jnp.where(row_zero, roll(a[j], -32, 1), roll(b[j], 32, 1))) for j in range(3)]
        for i in range(3):
            inner = sum(window.d(0, i, j) * a[j] for j in range(3))
            for kind in range(4):
                inner = inner - 2.0 * sum(window.c(0, kind, i, j) * after[j][kind] for j in range(3))
            energy = energy + a[i][:n_dev] * inner[:n_dev]
    products.append(energy)
    lane = lax.broadcasted_iota(jnp.int32, (1, 128), 1)
    packed = jnp.zeros((1, 128), jnp.float32)
    for n, value in enumerate(products):
        value = jnp.sum(jnp.sum(value, axis=0, keepdims=True), axis=1, keepdims=True)
        packed = jnp.where(lane == n, value, packed)
    out[...] = packed


def coefficients(moments):
    zero = jnp.zeros_like(moments[0])

    def inner(s, p, offset):
        total = zero
        for i, a in enumerate(s):
            for j, b in enumerate(p):
                total = total + a * b * moments[i + j + offset]
        return total

    def energy(p):
        return inner(p, p, 1) + HALF * inner(p, p, 0)

    s = [zero + 1.0]
    p = [zero + 1.0]
    x = [zero] * ITERS
    gamma = inner(s, s, 0)
    for sweep in range(ITERS):
        alpha = gamma / energy(p)
        x = [x[i] + (alpha * p[i] if i < len(p) else 0.0) for i in range(ITERS)]
        if sweep < ITERS - 1:
            image = [(p[i - 1] if i else 0.0) + (HALF * p[i] if i < len(p) else 0.0) for i in range(len(p) + 1)]
            s = [(s[i] if i < len(s) else 0.0) - alpha * image[i] for i in range(len(image))]
            gamma_new = inner(s, s, 0)
            beta = gamma_new / gamma
            p = [s[i] + (beta * p[i] if i < len(p) else 0.0) for i in range(len(s))]
            gamma = gamma_new
    return [value * (1.0 / SPAN) for value in x]


def finish_kernel(place, sums, v0, v1, v2, v3, n0, n1, n2, n3, kept, affines, residual):
    total = jnp.sum(sums[...], axis=0, keepdims=True)
    lane = lax.broadcasted_iota(jnp.int32, (1, 128), 1)
    moments = [jnp.sum(jnp.where(lane == n, total, 0.0), axis=1, keepdims=True) for n in range(8)]
    weights = coefficients(moments)
    at = place[2]
    row_zero, sec_zero = lane_bits((1, 128))

    def mix(refs, i, dev):
        return sum(w * ref[i, pl.ds(dev, 1), :] for w, ref in zip(weights, refs))

    vs = (v0, v1, v2, v3)
    x = [mix(vs, i, at) for i in range(6)]
    above = [mix(vs, i, at + 1) for i in range(6)]
    beside = [mix((n0, n1, n2, n3), i, at) for i in range(6)]
    for i in range(6):
        for sec in range(2):
            for row in range(2):
                start = 64 * sec + 32 * row
                affines[i, sec, row : row + 1, :] = x[i][:, start : start + 32]
    for kind in range(4):
        if kind == 0:
            b = [roll(z, -1, 1) for z in x]
        elif kind == 1:
            b = [jnp.where(row_zero, roll(z, -32, 1), roll(w, 32, 1)) for z, w in zip(x, beside)]
        elif kind == 2:
            b = [jnp.where(sec_zero, roll(z, 64, 1), roll(w, 64, 1)) for z, w in zip(x, above)]
        else:
            b = above
        u, v, p, q, live = (kept[5 * kind + i] for i in range(5))
        for comp in range(2):
            o = 3 * comp
            r = (p - u) if comp == 0 else (q - v)
            r = r - (x[o] * u + x[o + 1] * v) + (b[o] * p + b[o + 1] * q) - live * (x[o + 2] - b[o + 2])
            residual[pl.ds(kind * 256 + comp, 128, stride=2), :] = r.T


def shape_of(*shape):
    return jax.ShapeDtypeStruct(shape, jnp.float32)


def call(interpret, kernel, outs, *args, scalars=0, anywhere=0, copies=0, results="vmem"):
    spaces = [pl.BlockSpec(memory_space=pltpu.SMEM)] * scalars
    spaces += [pl.BlockSpec(memory_space=pl.ANY)] * anywhere
    spaces += [pl.BlockSpec(memory_space=pltpu.VMEM)] * (len(args) - scalars - anywhere)
    args = list(args)
    shapes = [shape_of(*out) for out in outs]
    if not interpret:
        for n in range(scalars + anywhere, len(args)):
            if args[n].dtype == jnp.float32:
                args[n] = pltpu.with_memory_space_constraint(args[n], pltpu.VMEM)
        if results == "vmem":
            shapes = [pltpu.VMEM(out, jnp.float32) for out in outs]
    return pl.pallas_call(
        kernel,
        out_shape=shapes,
        in_specs=spaces,
        out_specs=[pl.BlockSpec(memory_space=pltpu.VMEM) for _ in outs],
        scratch_shapes=[pltpu.SemaphoreType.DMA((copies,))] if copies else [],
        interpret=interpret,
    )(*args)


def shifted(value, axes, steps):
    count = lax.axis_size(axes)
    pairs = [(i, i + steps) for i in range(count) if 0 <= i + steps < count]
    return lax.ppermute(value, axes, pairs)


def pack_up(run, g):
    return run(pack_up_kernel, [(384, 128)], g, anywhere=1, copies=2)[0]


def pack_rows(run, f, g, counts):
    return run(pack_rows_kernel, [(128, 128), (136, 128)], f, g, counts, anywhere=2, copies=4)


def per_device(interpret, first_pts, second_pts, counts):
    run = functools.partial(call, interpret)
    n_sec = lax.axis_size(SEC_AXES)
    n_dev = lax.axis_size(GROUP)
    n_group = n_sec // n_dev
    sec = lax.axis_index(SEC_AXES)
    f = first_pts.reshape(1024, 128)
    g = second_pts.reshape(1024, 128)
    flags = jnp.stack(
        [
            (lax.axis_index("row") == lax.axis_size("row") - 1).astype(jnp.int32),
            (sec == n_sec - 1).astype(jnp.int32),
            lax.axis_index(GROUP).astype(jnp.int32),
        ]
    )

    up = shifted(pack_up(run, g), SEC_AXES, -1)
    beside, odd = pack_rows(run, f, g, counts)
    beside = shifted(beside, "row", -1)
    low = shifted(odd, "row", 1)
    packet, kept = run(gram_kernel, [(ROWS, 128), (20, 128, 128)], flags, f, g, counts, up, beside, low, scalars=1)

    half = n_dev // 2
    pairs = []
    for group in range(n_group):
        for dev in range(n_dev):
            source = group + (1 if dev < half else -1)
            if 0 <= source < n_group:
                pairs.append((source * n_dev + dev, group * n_dev + dev))
    other = lax.ppermute(packet, SEC_AXES, pairs)
    both = jnp.concatenate([packet, other], axis=0)
    (mine,) = run(merge_kernel, [(2 * DOUBLE, 128)], both, shifted(both, "row", -1), shifted(both, "row", 1))
    got = lax.all_to_all(jnp.broadcast_to(mine[None], (n_dev, 2 * DOUBLE, 128)), GROUP, 0, 0, tiled=False)
    wide = (6, 2 * n_dev, 128)
    blocks, v0, e0, v1, e1, v2 = run(
        window_kernel, [(93, 2 * n_dev, 128)] + [wide] * 5, got.reshape(n_dev * 2 * DOUBLE, 128)
    )
    e2, v3, e3, part = run(
        moments_kernel,
        [wide, wide, wide, (1, 128)],
        blocks,
        v0,
        v1,
        v2,
        shifted(v2, "row", -1),
        shifted(v2, "row", 1),
    )
    n_other = lax.axis_size(OTHERS)
    sums = lax.all_to_all(jnp.broadcast_to(part[None], (n_other, 1, 128)), OTHERS, 0, 0, tiled=False)
    affines, residual = run(
        finish_kernel,
        [(6,) + counts.shape[1:], (1024, 128)],
        flags,
        sums.reshape(n_other, 128),
        v0,
        v1,
        v2,
        v3,
        e0,
        e1,
        e2,
        e3,
        kept,
        scalars=1,
        results="hbm",
    )
    return affines, residual.reshape(first_pts.shape)


def split_mesh(mesh):
    n_row = mesh.shape["row"]
    return Mesh(mesh.devices.reshape(4, 4, 4, 2, n_row), SEC_AXES + ("row",))


def solution(mesh, inner=None, interpret=False):
    inner = inner or split_mesh(mesh)
    in_specs = (
        P(None, SEC_AXES, "row", None, None, None),
        P(None, SEC_AXES, "row", None, None, None),
        P(None, SEC_AXES, "row", None),
    )
    out_specs = (P(None, SEC_AXES, "row", None), P(None, SEC_AXES, "row", None, None, None))
    return jax.shard_map(
        functools.partial(per_device, interpret), mesh=inner, in_specs=in_specs, out_specs=out_specs, check_vma=False
    )
```

```python
import functools

import jax
import jax.numpy as jnp
from jax import lax
from jax.experimental import pallas as pl
from jax.experimental.pallas import tpu as pltpu
from jax.sharding import Mesh
from jax.sharding import PartitionSpec as P

ITERS = 4
SPAN = 1024.0
SHIFT = 512.0
HALF = SHIFT / SPAN
SQUARES = (0.49, 0.49, 0.09)
SYM = ((0, 0), (0, 1), (0, 2), (1, 1), (1, 2), (2, 2))
SEC_AXES = ("y", "zhi", "x", "core")
GROUP = ("x", "core")
OTHERS = ("y", "zhi", "row")

ROWS = 72
AT_C = 12
AT_SEND = 48
USED = 66
AT_E = 66
AT_E2 = 132
DOUBLE = 160
BEYOND = [AT_C + 9 + i for i in range(9)] + [6 + i for i in range(6)]
BEYOND += [AT_SEND + 3 + i for i in range(6)] + [AT_SEND + 12 + i for i in range(6)]


def sym_at(a, b):
    return SYM.index((min(a, b), max(a, b)))


def roll(value, shift, axis):
    size = value.shape[axis]
    return pltpu.roll(value, shift % size, axis)


def lane_bits(shape):
    lane = lax.broadcasted_iota(jnp.int32, shape, len(shape) - 1)
    return (lane // 32) % 2 == 0, lane < 64


def counts_row(ref, kind):
    cells = [ref[kind, sec, row : row + 1, :] for sec in range(2) for row in range(2)]
    return jnp.concatenate(cells, axis=1).astype(jnp.float32)


def block_sums(first, second, live):
    u, v = first
    p, q = second
    dx = p - u
    dy = q - v

    def red(z):
        return jnp.sum(z, axis=0, keepdims=True)

    su, sv, sp, sq, n = red(u), red(v), red(p), red(q), red(live)
    F = [red(u * u), red(u * v), su, red(v * v), sv, n]
    G = [red(p * p), red(p * q), sp, red(q * q), sq, n]
    C = [red(u * p), red(u * q), su, red(v * p), red(v * q), sv, sp, sq, n]
    tx, ty = red(dx), red(dy)
    s1 = [red(dx * u), red(dx * v), tx, red(dy * u), red(dy * v), ty]
    s2 = [red(dx * p), red(dx * q), tx, red(dy * p), red(dy * q), ty]
    return F, G, C, s1, s2


def gram_kernel(flags, f_ref, g_ref, counts_ref, up_ref, rest_ref, outside_ref, next_ref, low_ref, packet, kept):
    row_zero, sec_zero = lane_bits((1, 128))
    lane = lax.broadcasted_iota(jnp.int32, (1, 128), 1)
    last_row = flags[0] == 1
    last_sec = flags[1] == 1

    def pair_rows(ref, start, count, comp):
        return ref[pl.ds(2 * start + comp, count, stride=2), :]

    def own(ref, kind):
        return [pair_rows(ref, kind * 128, 128, comp).T for comp in range(2)]

    zero = jnp.zeros((1, 128), jnp.float32)
    counts = [counts_row(counts_ref, kind) for kind in range(4)]
    alive = [
        jnp.where(lane % 32 == 31, zero, counts[0]),
        jnp.where(jnp.logical_and(jnp.logical_not(row_zero), last_row), zero, counts[1]),
        jnp.where(jnp.logical_and(jnp.logical_not(sec_zero), last_sec), zero, counts[2]),
        jnp.where(last_sec, zero, counts[3]),
    ]
    point = lax.broadcasted_iota(jnp.int32, (128, 128), 0).astype(jnp.float32)

    def masked(points, count):
        live = jnp.where(point < count, 1.0, 0.0)
        return [z * live for z in points], live

    def second_of(kind):
        if kind == 0:
            return [roll(z, -1, 1) for z in own(g_ref, 0)]
        out = []
        for comp in range(2):
            if kind == 1:
                parts = [
                    pair_rows(g_ref, 128 + 32, 32, comp),
                    pair_rows(next_ref, 0, 32, comp),
                    pair_rows(g_ref, 128 + 96, 32, comp),
                    pair_rows(next_ref, 32, 32, comp),
                ]
            elif kind == 2:
                parts = [pair_rows(g_ref, 256 + 64, 64, comp), pair_rows(up_ref, 0, 64, comp)]
            else:
                rest = pair_rows(rest_ref, 0, 96, comp) + pair_rows(outside_ref, 0, 96, comp)
                parts = [pair_rows(up_ref, 64, 32, comp), rest]
            out.append(jnp.concatenate(parts, axis=0).T)
        return out

    D = [zero] * 6
    S = [zero] * 6
    unit = 1.0 / SPAN

    def put(row, value):
        packet[row : row + 1, :] = value

    for kind in range(4):
        first, live = masked(own(f_ref, kind), alive[kind])
        second, _ = masked(second_of(kind), alive[kind])
        kept[5 * kind] = first[0]
        kept[5 * kind + 1] = first[1]
        kept[5 * kind + 2] = second[0]
        kept[5 * kind + 3] = second[1]
        kept[5 * kind + 4] = live
        F, G, C, s1, s2 = block_sums(first, second, live)
        D = [a + b for a, b in zip(D, F)]
        S = [a + b for a, b in zip(S, s1)]
        for i in range(9):
            put(AT_C + 9 * kind + i, C[i] * unit)
        if kind == 0:
            D = [a + roll(b, 1, 1) for a, b in zip(D, G)]
            S = [a - roll(b, 1, 1) for a, b in zip(S, s2)]
        elif kind == 1:
            D = [a + jnp.where(row_zero, zero, roll(b, 32, 1)) for a, b in zip(D, G)]
            S = [a - jnp.where(row_zero, zero, roll(b, 32, 1)) for a, b in zip(S, s2)]
        elif kind == 2:
            D = [a + jnp.where(sec_zero, zero, roll(b, 64, 1)) for a, b in zip(D, G)]
            S = [a - jnp.where(sec_zero, zero, roll(b, 64, 1)) for a, b in zip(S, s2)]
        if kind >= 2:
            base = AT_SEND + 9 * (kind - 2)
            put(base, G[0] * unit)
            put(base + 1, G[1] * unit)
            put(base + 2, G[3] * unit)
            for i in range(6):
                put(base + 3 + i, s2[i])

    low_count = jnp.where(row_zero, zero, low_ref[128:129, :])
    first = []
    second = []
    for comp in range(2):
        low = [pair_rows(low_ref, 32 * sec, 32, comp) for sec in range(2)]
        first.append(jnp.concatenate([low[0], low[0], low[1], low[1]], axis=0).T)
        mine = [pair_rows(g_ref, 128 + 64 * sec, 32, comp) for sec in range(2)]
        second.append(jnp.concatenate([mine[0], mine[0], mine[1], mine[1]], axis=0).T)
    first, live = masked(first, low_count)
    second, _ = masked(second, low_count)
    F, G, C, s1, s2 = block_sums(first, second, live)
    D = [a + jnp.where(row_zero, roll(b, -32, 1), zero) for a, b in zip(D, G)]
    S = [a - jnp.where(row_zero, roll(b, -32, 1), zero) for a, b in zip(S, s2)]

    for i in range(6):
        a, b = SYM[i]
        put(i, D[i] * unit + ((SQUARES[a] - SHIFT) * unit if a == b else 0.0))
        put(6 + i, S[i])
    for row in range(AT_SEND + 18, ROWS):
        put(row, zero)


def from_above(value):
    return roll(value, -1, 0)


def from_below(value):
    return roll(value, 1, 0)


def pack_up_kernel(g_ref, up, rest, sems):
    copies = [
        pltpu.make_async_copy(g_ref.at[pl.ds(512, 128)], up.at[pl.ds(0, 128)], sems.at[0]),
        pltpu.make_async_copy(g_ref.at[pl.ds(768, 64)], up.at[pl.ds(128, 64)], sems.at[1]),
        pltpu.make_async_copy(g_ref.at[pl.ds(832, 192)], rest, sems.at[2]),
    ]
    for copy in copies:
        copy.start()
    for copy in copies:
        copy.wait()


def pack_rows_kernel(f_ref, g_ref, counts_ref, beside, odd, sems):
    copies = [
        pltpu.make_async_copy(g_ref.at[pl.ds(256, 64)], beside.at[pl.ds(0, 64)], sems.at[0]),
        pltpu.make_async_copy(g_ref.at[pl.ds(384, 64)], beside.at[pl.ds(64, 64)], sems.at[1]),
        pltpu.make_async_copy(f_ref.at[pl.ds(320, 64)], odd.at[pl.ds(0, 64)], sems.at[2]),
        pltpu.make_async_copy(f_ref.at[pl.ds(448, 64)], odd.at[pl.ds(64, 64)], sems.at[3]),
    ]
    for copy in copies:
        copy.start()
    odd[128:136, :] = jnp.broadcast_to(counts_row(counts_ref, 1), (8, 128))
    for copy in copies:
        copy.wait()


def merge_kernel(both, above, below, out):
    row_zero, _ = lane_bits((1, 128))
    for part in range(2):
        at = part * ROWS
        to = part * DOUBLE
        out[to : to + USED, :] = both[at : at + USED, :]
        a = above[at : at + USED, :]
        b = below[at : at + USED, :]
        out[to + AT_E : to + AT_E + USED, :] = jnp.where(row_zero, a, b)
        for i, source in enumerate(BEYOND):
            out[to + AT_E2 + i : to + AT_E2 + i + 1, :] = jnp.where(
                row_zero, b[source : source + 1], a[source : source + 1]
            )
        out[to + AT_E2 + len(BEYOND) : to + DOUBLE, :] = jnp.zeros((DOUBLE - AT_E2 - len(BEYOND), 128), jnp.float32)


class Window:
    def __init__(self, load, n_dev):
        self.load = load
        self.bits = lane_bits((2 * n_dev, 128))

    def seconds(self, v, row_values):
        row_zero, sec_zero = self.bits
        half = roll(v, 64, 1)
        return [
            roll(v, -1, 1),
            row_values,
            jnp.where(sec_zero, half, from_above(half)),
            from_above(v),
        ]

    def row_pairs(self, v, e, e2):
        row_zero, _ = self.bits
        forth, back = roll(v, 32, 1), roll(v, -32, 1)
        own = jnp.where(row_zero, back, roll(e, 32, 1))
        side = jnp.where(row_zero, roll(e2, -32, 1), forth)
        return own, side

    def c(self, side, kind, i, j):
        return self.load(side * 42 + 6 + 9 * kind + 3 * i + j)

    def d(self, side, i, j):
        return self.load(side * 42 + sym_at(i, j))

    def c_e2(self, i, j):
        return self.load(84 + 3 * i + j)

    def transposed(self, c, a):
        return [c(0, j) * a[0] + c(1, j) * a[1] + c(2, j) * a[2] for j in range(3)]

    def apply(self, v, e, e2, sides):
        row_zero, sec_zero = self.bits
        outs = ([None] * 6, [None] * 6)
        for half in range(2):
            span = slice(3 * half, 3 * half + 3)
            sets = (v[span], e[span])
            beyond = e2[span]
            pairs = [self.row_pairs(*z) for z in zip(v[span], e[span], beyond)]
            t_row = [self.transposed(functools.partial(self.c, side, 1), sets[side]) for side in range(2)]
            for side in sides:
                a = sets[side]
                after = [self.seconds(a[j], pairs[j][side]) for j in range(3)]
                total = []
                for i in range(3):
                    y = sum(self.d(side, i, j) * a[j] for j in range(3))
                    for kind in range(4):
                        y = y - sum(self.c(side, kind, i, j) * after[j][kind] for j in range(3))
                    total.append(y)
                col = self.transposed(functools.partial(self.c, side, 0), a)
                one = self.transposed(functools.partial(self.c, side, 2), a)
                two = self.transposed(functools.partial(self.c, side, 3), a)
                if side == 1:
                    outer = self.transposed(self.c_e2, beyond)
                for j in range(3):
                    t = roll(one[j], 64, 1)
                    y = total[j] - roll(col[j], 1, 1) - jnp.where(sec_zero, from_below(t), t) - from_below(two[j])
                    if side == 0:
                        y = y - jnp.where(row_zero, roll(t_row[1][j], -32, 1), roll(t_row[0][j], 32, 1))
                    else:
                        y = y - jnp.where(row_zero, roll(t_row[0][j], -32, 1), roll(outer[j], 32, 1))
                    outs[side][3 * half + j] = y
        return outs


def window_kernel(got, blocks, v0, e0, v1, e1, v2):
    n_dev = got.shape[0] // (2 * DOUBLE)
    row_zero, sec_zero = lane_bits((2 * n_dev, 128))
    zero = jnp.zeros((2 * n_dev, 128), jnp.float32)

    def row(i):
        return jnp.concatenate(
            [got[pl.ds(slot * DOUBLE + i, n_dev, stride=2 * DOUBLE), :] for slot in range(2)], axis=0
        )

    def pushed(kind, value):
        if kind == 2:
            return from_below(jnp.where(sec_zero, roll(value, 64, 1), zero))
        return from_below(value)

    starts = []
    for side, at in enumerate((0, AT_E)):
        for i in range(36):
            blocks[side * 42 + 6 + i] = row(at + AT_C + i)
        D = [row(at + i) for i in range(6)]
        S = [row(at + 6 + i) for i in range(6)]
        for kind in (2, 3):
            base = at + AT_SEND + 9 * (kind - 2)
            last = [blocks[side * 42 + 6 + 9 * kind + i] for i in (6, 7, 8)]
            G = [row(base), row(base + 1), last[0], row(base + 2), last[1], last[2]]
            D = [a + pushed(kind, b) for a, b in zip(D, G)]
            S = [a - pushed(kind, row(base + 3 + i)) for i, a in enumerate(S)]
        for i in range(6):
            blocks[side * 42 + i] = D[i]
        starts.append(S)
    for i in range(9):
        blocks[84 + i] = row(AT_E2 + i)
    outer = [
        row(AT_E2 + 9 + i) - pushed(2, row(AT_E2 + 15 + i)) - pushed(3, row(AT_E2 + 21 + i)) for i in range(6)
    ]
    window = Window(lambda i: blocks[i], n_dev)
    v, e = starts
    w, f = window.apply(v, e, outer, (0, 1))
    last, _ = window.apply(w, f, f, (0,))
    for i in range(6):
        v0[i] = v[i]
        e0[i] = e[i]
        v1[i] = w[i]
        e1[i] = f[i]
        v2[i] = last[i]


def moments_kernel(blocks, v0, v1, v2, above, below, e2, v3, e3, out):
    shape = v2.shape[1:]
    n_dev = shape[0] // 2
    bits = lane_bits(shape)
    row_zero, _ = bits
    window = Window(lambda i: blocks[i], n_dev)
    v = [v2[i] for i in range(6)]
    side = [jnp.where(row_zero, above[i], below[i]) for i in range(6)]
    outer = [jnp.where(row_zero, below[i], above[i]) for i in range(6)]
    w, f = window.apply(v, side, outer, (0, 1))
    for i in range(6):
        e2[i] = side[i]
        v3[i] = w[i]
        e3[i] = f[i]
    vs = [[v0[i] for i in range(6)], [v1[i] for i in range(6)], v, w]

    def dot(left, right):
        return sum(a[:n_dev] * b[:n_dev] for a, b in zip(left, right))

    products = [dot(vs[n // 2], vs[n - n // 2]) for n in range(7)]
    energy = 0.0
    for half in range(2):
        a = w[3 * half : 3 * half + 3]
        b = f[3 * half : 3 * half + 3]
        after = [window.seconds(a[j], jnp.where(row_zero, roll(a[j], -32, 1), roll(b[j], 32, 1))) for j in range(3)]
        for i in range(3):
            inner = sum(window.d(0, i, j) * a[j] for j in range(3))
            for kind in range(4):
                inner = inner - 2.0 * sum(window.c(0, kind, i, j) * after[j][kind] for j in range(3))
            energy = energy + a[i][:n_dev] * inner[:n_dev]
    products.append(energy)
    lane = lax.broadcasted_iota(jnp.int32, (1, 128), 1)
    packed = jnp.zeros((1, 128), jnp.float32)
    for n, value in enumerate(products):
        value = jnp.sum(jnp.sum(value, axis=0, keepdims=True), axis=1, keepdims=True)
        packed = jnp.where(lane == n, value, packed)
    out[...] = packed


def coefficients(moments):
    zero = jnp.zeros_like(moments[0])

    def inner(s, p, offset):
        total = zero
        for i, a in enumerate(s):
            for j, b in enumerate(p):
                total = total + a * b * moments[i + j + offset]
        return total

    def energy(p):
        return inner(p, p, 1) + HALF * inner(p, p, 0)

    s = [zero + 1.0]
    p = [zero + 1.0]
    x = [zero] * ITERS
    gamma = inner(s, s, 0)
    for sweep in range(ITERS):
        alpha = gamma / energy(p)
        x = [x[i] + (alpha * p[i] if i < len(p) else 0.0) for i in range(ITERS)]
        if sweep < ITERS - 1:
            image = [(p[i - 1] if i else 0.0) + (HALF * p[i] if i < len(p) else 0.0) for i in range(len(p) + 1)]
            s = [(s[i] if i < len(s) else 0.0) - alpha * image[i] for i in range(len(image))]
            gamma_new = inner(s, s, 0)
            beta = gamma_new / gamma
            p = [s[i] + (beta * p[i] if i < len(p) else 0.0) for i in range(len(s))]
            gamma = gamma_new
    return [value * (1.0 / SPAN) for value in x]


def finish_kernel(place, sums, v0, v1, v2, v3, n0, n1, n2, n3, kept_hbm, affines, residual_hbm, kept, residual, sems):
    fetches = [
        pltpu.make_async_copy(kept_hbm.at[pl.ds(5 * kind, 5)], kept.at[pl.ds(5 * kind, 5)], sems.at[kind])
        for kind in range(4)
    ]
    for fetch in fetches:
        fetch.start()
    stores = []
    total = jnp.sum(sums[...], axis=0, keepdims=True)
    lane = lax.broadcasted_iota(jnp.int32, (1, 128), 1)
    moments = [jnp.sum(jnp.where(lane == n, total, 0.0), axis=1, keepdims=True) for n in range(8)]
    weights = coefficients(moments)
    at = place[2]
    row_zero, sec_zero = lane_bits((1, 128))

    def mix(refs, i, dev):
        return sum(w * ref[i, pl.ds(dev, 1), :] for w, ref in zip(weights, refs))

    vs = (v0, v1, v2, v3)
    x = [mix(vs, i, at) for i in range(6)]
    above = [mix(vs, i, at + 1) for i in range(6)]
    beside = [mix((n0, n1, n2, n3), i, at) for i in range(6)]
    for i in range(6):
        for sec in range(2):
            for row in range(2):
                start = 64 * sec + 32 * row
                affines[i, sec, row : row + 1, :] = x[i][:, start : start + 32]
    for kind in range(4):
        if kind == 0:
            b = [roll(z, -1, 1) for z in x]
        elif kind == 1:
            b = [jnp.where(row_zero, roll(z, -32, 1), roll(w, 32, 1)) for z, w in zip(x, beside)]
        elif kind == 2:
            b = [jnp.where(sec_zero, roll(z, 64, 1), roll(w, 64, 1)) for z, w in zip(x, above)]
        else:
            b = above
        fetches[kind].wait()
        u, v, p, q, live = (kept[5 * kind + i] for i in range(5))
        for comp in range(2):
            o = 3 * comp
            r = (p - u) if comp == 0 else (q - v)
            r = r - (x[o] * u + x[o + 1] * v) + (b[o] * p + b[o + 1] * q) - live * (x[o + 2] - b[o + 2])
            residual[pl.ds(kind * 256 + comp, 128, stride=2), :] = r.T
        part = pl.ds(kind * 256, 256)
        stores.append(pltpu.make_async_copy(residual.at[part], residual_hbm.at[part], sems.at[4 + kind]))
        stores[-1].start()
    for store in stores:
        store.wait()


def shape_of(*shape):
    return jax.ShapeDtypeStruct(shape, jnp.float32)


def call(interpret, kernel, outs, *args, scalars=0, anywhere=(), copies=0, buffers=(), results=None):
    spaces = []
    args = list(args)
    shapes = [shape_of(*out) for out in outs]
    for n, arg in enumerate(args):
        if n < scalars:
            spaces.append(pl.BlockSpec(memory_space=pltpu.SMEM))
        elif n in anywhere:
            spaces.append(pl.BlockSpec(memory_space=pl.ANY))
        else:
            spaces.append(pl.BlockSpec(memory_space=pltpu.VMEM))
            if arg.dtype == jnp.float32 and not interpret:
                args[n] = pltpu.with_memory_space_constraint(arg, pltpu.VMEM)
    if not results and not interpret:
        shapes = [pltpu.VMEM(out, jnp.float32) for out in outs]
    results = results or [pltpu.VMEM] * len(outs)
    return pl.pallas_call(
        kernel,
        out_shape=shapes,
        in_specs=spaces,
        out_specs=[pl.BlockSpec(memory_space=space) for space in results],
        scratch_shapes=[pltpu.VMEM(b, jnp.float32) for b in buffers]
        + ([pltpu.SemaphoreType.DMA((copies,))] if copies else []),
        interpret=interpret,
    )(*args)


def shifted(value, axes, steps):
    count = lax.axis_size(axes)
    pairs = [(i, i + steps) for i in range(count) if 0 <= i + steps < count]
    return lax.ppermute(value, axes, pairs)


def pack_up(run, g):
    return run(pack_up_kernel, [(192, 128), (192, 128)], g, anywhere=(0,), copies=3)


def pack_rows(run, f, g, counts):
    return run(pack_rows_kernel, [(128, 128), (136, 128)], f, g, counts, anywhere=(0, 1), copies=4)


def per_device(interpret, first_pts, second_pts, counts):
    run = functools.partial(call, interpret)
    n_sec = lax.axis_size(SEC_AXES)
    n_dev = lax.axis_size(GROUP)
    n_group = n_sec // n_dev
    sec = lax.axis_index(SEC_AXES)
    f = first_pts.reshape(1024, 128)
    g = second_pts.reshape(1024, 128)
    flags = jnp.stack(
        [
            (lax.axis_index("row") == lax.axis_size("row") - 1).astype(jnp.int32),
            (sec == n_sec - 1).astype(jnp.int32),
            lax.axis_index(GROUP).astype(jnp.int32),
        ]
    )

    up, rest = pack_up(run, g)
    up = shifted(up, SEC_AXES, -1)
    relay = n_dev - 2
    inside = [(i + 1, i) for i in range(n_sec - 1) if (i + 1) % n_dev]
    to_relay = [(group * n_dev, group * n_dev + relay) for group in range(1, n_group)]
    from_relay = [(group * n_dev + relay, group * n_dev - 1) for group in range(1, n_group)]
    relayed = lax.ppermute(rest, SEC_AXES, to_relay)
    relayed, f_later, g_later = lax.optimization_barrier((relayed, f, g))
    outside = lax.ppermute(relayed, SEC_AXES, from_relay)
    beside, odd, rest = lax.optimization_barrier((*pack_rows(run, f_later, g_later, counts), rest))
    rest = lax.ppermute(rest, SEC_AXES, inside)
    beside = shifted(beside, "row", -1)
    low = shifted(odd, "row", 1)
    packet, kept = run(gram_kernel, [(ROWS, 128), (20, 128, 128)], flags, f, g, counts, up, rest, outside, beside, low, scalars=1)

    half = n_dev // 2
    pairs = []
    for group in range(n_group):
        for dev in range(n_dev):
            source = group + (1 if dev < half else -1)
            if 0 <= source < n_group:
                pairs.append((source * n_dev + dev, group * n_dev + dev))
    other = lax.ppermute(packet, SEC_AXES, pairs)
    both = jnp.concatenate([packet, other], axis=0)
    (mine,) = run(merge_kernel, [(2 * DOUBLE, 128)], both, shifted(both, "row", -1), shifted(both, "row", 1))
    got = lax.all_to_all(jnp.broadcast_to(mine[None], (n_dev, 2 * DOUBLE, 128)), GROUP, 0, 0, tiled=False)
    wide = (6, 2 * n_dev, 128)
    blocks, v0, e0, v1, e1, v2 = run(
        window_kernel, [(93, 2 * n_dev, 128)] + [wide] * 5, got.reshape(n_dev * 2 * DOUBLE, 128)
    )
    e2, v3, e3, part = run(
        moments_kernel,
        [wide, wide, wide, (1, 128)],
        blocks,
        v0,
        v1,
        v2,
        shifted(v2, "row", -1),
        shifted(v2, "row", 1),
    )
    n_other = lax.axis_size(OTHERS)
    sums = lax.all_to_all(jnp.broadcast_to(part[None], (n_other, 1, 128)), OTHERS, 0, 0, tiled=False)
    affines, residual = run(
        finish_kernel,
        [(6,) + counts.shape[1:], (1024, 128)],
        flags,
        sums.reshape(n_other, 128),
        v0,
        v1,
        v2,
        v3,
        e0,
        e1,
        e2,
        e3,
        kept,
        scalars=1,
        anywhere=(10,),
        copies=8,
        buffers=[(20, 128, 128), (1024, 128)],
        results=[pltpu.VMEM, pl.ANY],
    )
    return affines, residual.reshape(first_pts.shape)


def split_mesh(mesh):
    n_row = mesh.shape["row"]
    return Mesh(mesh.devices.reshape(4, 4, 4, 2, n_row), SEC_AXES + ("row",))


def solution(mesh, inner=None, interpret=False):
    inner = inner or split_mesh(mesh)
    in_specs = (
        P(None, SEC_AXES, "row", None, None, None),
        P(None, SEC_AXES, "row", None, None, None),
        P(None, SEC_AXES, "row", None),
    )
    out_specs = (P(None, SEC_AXES, "row", None), P(None, SEC_AXES, "row", None, None, None))
    return jax.shard_map(
        functools.partial(per_device, interpret), mesh=inner, in_specs=in_specs, out_specs=out_specs, check_vma=False
    )
```

```python
import functools

import jax
import jax.numpy as jnp
from jax import lax
from jax.experimental import pallas as pl
from jax.experimental.pallas import tpu as pltpu
from jax.sharding import Mesh
from jax.sharding import PartitionSpec as P

ITERS = 4
SPAN = 1024.0
SHIFT = 512.0
HALF = SHIFT / SPAN
SQUARES = (0.49, 0.49, 0.09)
SYM = ((0, 0), (0, 1), (0, 2), (1, 1), (1, 2), (2, 2))
SEC_AXES = ("y", "zhi", "x", "core")
GROUP = ("x", "core")
OTHERS = ("y", "zhi", "row")

ROWS = 64
AT_C = 12
AT_THREE = 48
AT_TWO = 57
USED = 62
AT_E = 62
AT_E2 = 124
DOUBLE = 144
BEYOND = [6 + i for i in range(6)] + [AT_THREE + 3 + i for i in range(6)] + [AT_TWO + i for i in range(3)]


def sym_at(a, b):
    return SYM.index((min(a, b), max(a, b)))


def roll(value, shift, axis):
    size = value.shape[axis]
    return pltpu.roll(value, shift % size, axis)


def lane_bits(shape):
    lane = lax.broadcasted_iota(jnp.int32, shape, len(shape) - 1)
    return (lane // 32) % 2 == 0, lane < 64


def counts_row(ref, kind):
    cells = [ref[kind, sec, row : row + 1, :] for sec in range(2) for row in range(2)]
    return jnp.concatenate(cells, axis=1).astype(jnp.float32)


def live_counts(flags, counts_ref):
    row_zero, sec_zero = lane_bits((1, 128))
    lane = lax.broadcasted_iota(jnp.int32, (1, 128), 1)
    last_row = flags[0] == 1
    last_sec = flags[1] == 1
    zero = jnp.zeros((1, 128), jnp.float32)
    counts = [counts_row(counts_ref, kind) for kind in range(4)]
    return [
        jnp.where(lane % 32 == 31, zero, counts[0]),
        jnp.where(jnp.logical_and(jnp.logical_not(row_zero), last_row), zero, counts[1]),
        jnp.where(jnp.logical_and(jnp.logical_not(sec_zero), last_sec), zero, counts[2]),
        jnp.where(last_sec, zero, counts[3]),
    ]


def live_points(count):
    point = lax.broadcasted_iota(jnp.int32, (128, 128), 0).astype(jnp.float32)
    return jnp.where(point < count, 1.0, 0.0)


def block_sums(first, second, live):
    u, v = first
    p, q = second
    dx = p - u
    dy = q - v

    def red(z):
        return jnp.sum(z, axis=0, keepdims=True)

    su, sv, sp, sq, n = red(u), red(v), red(p), red(q), red(live)
    F = [red(u * u), red(u * v), su, red(v * v), sv, n]
    G = [red(p * p), red(p * q), sp, red(q * q), sq, n]
    C = [red(u * p), red(u * q), su, red(v * p), red(v * q), sv, sp, sq, n]
    tx, ty = red(dx), red(dy)
    s1 = [red(dx * u), red(dx * v), tx, red(dy * u), red(dy * v), ty]
    s2 = [red(dx * p), red(dx * q), tx, red(dy * p), red(dy * q), ty]
    return F, G, C, s1, s2


def gram_kernel(flags, f_ref, g_ref, counts_ref, up_ref, rest_ref, outside_ref, next_ref, low_ref, packet, kept):
    row_zero, sec_zero = lane_bits((1, 128))

    def pair_rows(ref, start, count, comp):
        return ref[pl.ds(2 * start + comp, count, stride=2), :]

    def own(ref, kind):
        return [pair_rows(ref, kind * 128, 128, comp).T for comp in range(2)]

    zero = jnp.zeros((1, 128), jnp.float32)
    alive = live_counts(flags, counts_ref)

    def masked(points, count):
        live = live_points(count)
        return [z * live for z in points], live

    def second_of(kind):
        if kind == 0:
            return [roll(z, -1, 1) for z in own(g_ref, 0)]
        out = []
        for comp in range(2):
            if kind == 1:
                parts = [
                    pair_rows(g_ref, 128 + 32, 32, comp),
                    pair_rows(next_ref, 0, 32, comp),
                    pair_rows(g_ref, 128 + 96, 32, comp),
                    pair_rows(next_ref, 32, 32, comp),
                ]
            elif kind == 2:
                parts = [pair_rows(g_ref, 256 + 64, 64, comp), pair_rows(up_ref, 0, 64, comp)]
            else:
                rest = pair_rows(rest_ref, 0, 96, comp) + pair_rows(outside_ref, 0, 96, comp)
                parts = [pair_rows(up_ref, 64, 32, comp), rest]
            out.append(jnp.concatenate(parts, axis=0).T)
        return out

    D = [zero] * 6
    S = [zero] * 6
    unit = 1.0 / SPAN

    def put(row, value):
        packet[row : row + 1, :] = value

    for kind in range(4):
        first, live = masked(own(f_ref, kind), alive[kind])
        second, _ = masked(second_of(kind), alive[kind])
        for i, points in enumerate(first + second):
            kept[4 * kind + i] = points
        F, G, C, s1, s2 = block_sums(first, second, live)
        D = [a + b for a, b in zip(D, F)]
        S = [a + b for a, b in zip(S, s1)]
        for i in range(9):
            put(AT_C + 9 * kind + i, C[i] * unit)
        if kind == 0:
            D = [a + roll(b, 1, 1) for a, b in zip(D, G)]
            S = [a - roll(b, 1, 1) for a, b in zip(S, s2)]
        elif kind == 1:
            D = [a + jnp.where(row_zero, zero, roll(b, 32, 1)) for a, b in zip(D, G)]
            S = [a - jnp.where(row_zero, zero, roll(b, 32, 1)) for a, b in zip(S, s2)]
        elif kind == 2:
            D = [a + jnp.where(sec_zero, zero, roll(b, 64, 1)) for a, b in zip(D, G)]
            S = [a - jnp.where(sec_zero, zero, roll(b, 64, 1)) for a, b in zip(S, s2)]
            for i in range(3):
                put(AT_TWO + i, jnp.where(sec_zero, roll(s2[3 + i], 64, 1), s2[i]))
            put(AT_TWO + 3, jnp.where(sec_zero, roll(G[1], 64, 1), G[0]) * unit)
            put(AT_TWO + 4, G[3] * unit)
        else:
            put(AT_THREE, G[0] * unit)
            put(AT_THREE + 1, G[1] * unit)
            put(AT_THREE + 2, G[3] * unit)
            for i in range(6):
                put(AT_THREE + 3 + i, s2[i])

    low_count = jnp.where(row_zero, zero, low_ref[128:129, :])
    first = []
    second = []
    for comp in range(2):
        low = [pair_rows(low_ref, 32 * sec, 32, comp) for sec in range(2)]
        first.append(jnp.concatenate([low[0], low[0], low[1], low[1]], axis=0).T)
        mine = [pair_rows(g_ref, 128 + 64 * sec, 32, comp) for sec in range(2)]
        second.append(jnp.concatenate([mine[0], mine[0], mine[1], mine[1]], axis=0).T)
    first, live = masked(first, low_count)
    second, _ = masked(second, low_count)
    F, G, C, s1, s2 = block_sums(first, second, live)
    D = [a + jnp.where(row_zero, roll(b, -32, 1), zero) for a, b in zip(D, G)]
    S = [a - jnp.where(row_zero, roll(b, -32, 1), zero) for a, b in zip(S, s2)]

    for i in range(6):
        a, b = SYM[i]
        put(i, D[i] * unit + ((SQUARES[a] - SHIFT) * unit if a == b else 0.0))
        put(6 + i, S[i])
    for row in range(USED, ROWS):
        put(row, zero)


def from_above(value):
    return roll(value, -1, 0)


def from_below(value):
    return roll(value, 1, 0)


def pack_up_kernel(g_ref, up, rest, sems):
    copies = [
        pltpu.make_async_copy(g_ref.at[pl.ds(512, 128)], up.at[pl.ds(0, 128)], sems.at[0]),
        pltpu.make_async_copy(g_ref.at[pl.ds(768, 64)], up.at[pl.ds(128, 64)], sems.at[1]),
        pltpu.make_async_copy(g_ref.at[pl.ds(832, 192)], rest, sems.at[2]),
    ]
    for copy in copies:
        copy.start()
    for copy in copies:
        copy.wait()


def pack_rows_kernel(f_ref, g_ref, counts_ref, beside, odd, sems):
    copies = [
        pltpu.make_async_copy(g_ref.at[pl.ds(256, 64)], beside.at[pl.ds(0, 64)], sems.at[0]),
        pltpu.make_async_copy(g_ref.at[pl.ds(384, 64)], beside.at[pl.ds(64, 64)], sems.at[1]),
        pltpu.make_async_copy(f_ref.at[pl.ds(320, 64)], odd.at[pl.ds(0, 64)], sems.at[2]),
        pltpu.make_async_copy(f_ref.at[pl.ds(448, 64)], odd.at[pl.ds(64, 64)], sems.at[3]),
    ]
    for copy in copies:
        copy.start()
    odd[128:136, :] = jnp.broadcast_to(counts_row(counts_ref, 1), (8, 128))
    for copy in copies:
        copy.wait()


def merge_kernel(both, above, below, out):
    row_zero, _ = lane_bits((1, 128))
    for part in range(2):
        at = part * ROWS
        to = part * DOUBLE
        out[to : to + USED, :] = both[at : at + USED, :]
        a = above[at : at + USED, :]
        b = below[at : at + USED, :]
        out[to + AT_E : to + AT_E + USED, :] = jnp.where(row_zero, a, b)
        first = AT_C + 9
        for i in range(5):
            one, two = b[first + i : first + i + 1], b[first + min(5 + i, 8) : first + min(5 + i, 8) + 1]
            out[to + AT_E2 + i : to + AT_E2 + i + 1, :] = jnp.where(row_zero, one, roll(two, 32, 1))
        for i, source in enumerate(BEYOND):
            out[to + AT_E2 + 5 + i : to + AT_E2 + 6 + i, :] = jnp.where(
                row_zero, b[source : source + 1], a[source : source + 1]
            )


class Window:
    def __init__(self, load, n_dev):
        self.load = load
        self.bits = lane_bits((2 * n_dev, 128))

    def seconds(self, v, row_values):
        row_zero, sec_zero = self.bits
        half = roll(v, 64, 1)
        return [
            roll(v, -1, 1),
            row_values,
            jnp.where(sec_zero, half, from_above(half)),
            from_above(v),
        ]

    def row_pairs(self, v, e, e2):
        row_zero, _ = self.bits
        forth, back = roll(v, 32, 1), roll(v, -32, 1)
        own = jnp.where(row_zero, back, roll(e, 32, 1))
        side = jnp.where(row_zero, roll(e2, -32, 1), forth)
        return own, side

    def c(self, side, kind, i, j):
        return self.load(side * 42 + 6 + 9 * kind + 3 * i + j)

    def d(self, side, i, j):
        return self.load(side * 42 + sym_at(i, j))

    def c_e2(self, i, j):
        return self.load(84 + 3 * i + j)

    def transposed(self, c, a):
        return [c(0, j) * a[0] + c(1, j) * a[1] + c(2, j) * a[2] for j in range(3)]

    def apply(self, v, e, e2, sides):
        row_zero, sec_zero = self.bits
        outs = ([None] * 6, [None] * 6)
        for half in range(2):
            span = slice(3 * half, 3 * half + 3)
            sets = (v[span], e[span])
            beyond = e2[span]
            pairs = [self.row_pairs(*z) for z in zip(v[span], e[span], beyond)]
            t_row = [self.transposed(functools.partial(self.c, side, 1), sets[side]) for side in range(2)]
            for side in sides:
                a = sets[side]
                after = [self.seconds(a[j], pairs[j][side]) for j in range(3)]
                total = []
                for i in range(3):
                    y = sum(self.d(side, i, j) * a[j] for j in range(3))
                    for kind in range(4):
                        y = y - sum(self.c(side, kind, i, j) * after[j][kind] for j in range(3))
                    total.append(y)
                col = self.transposed(functools.partial(self.c, side, 0), a)
                one = self.transposed(functools.partial(self.c, side, 2), a)
                two = self.transposed(functools.partial(self.c, side, 3), a)
                if side == 1:
                    outer = self.transposed(self.c_e2, beyond)
                for j in range(3):
                    t = roll(one[j], 64, 1)
                    y = total[j] - roll(col[j], 1, 1) - jnp.where(sec_zero, from_below(t), t) - from_below(two[j])
                    if side == 0:
                        y = y - jnp.where(row_zero, roll(t_row[1][j], -32, 1), roll(t_row[0][j], 32, 1))
                    else:
                        y = y - jnp.where(row_zero, roll(t_row[0][j], -32, 1), roll(outer[j], 32, 1))
                    outs[side][3 * half + j] = y
        return outs


def window_kernel(got, blocks, v0, e0, v1, e1, v2):
    n_dev = got.shape[0] // (2 * DOUBLE)
    row_zero, sec_zero = lane_bits((2 * n_dev, 128))
    zero = jnp.zeros((2 * n_dev, 128), jnp.float32)

    def row(i):
        return jnp.concatenate(
            [got[pl.ds(slot * DOUBLE + i, n_dev, stride=2 * DOUBLE), :] for slot in range(2)], axis=0
        )

    def from_two(value, packed_second=False):
        if not packed_second:
            value = roll(value, 64, 1)
        return from_below(jnp.where(sec_zero, value, zero))

    def s_terms(three, two):
        return [
            from_below(row(three + i)) + from_two(row(two + i % 3), packed_second=i >= 3) for i in range(6)
        ]

    starts = []
    for side, at in enumerate((0, AT_E)):
        base = side * 42
        for i in range(36):
            blocks[base + 6 + i] = row(at + AT_C + i)
        two = [blocks[base + 24 + i] for i in (6, 7, 8)]
        three = [blocks[base + 33 + i] for i in (6, 7, 8)]
        pair, last = row(at + AT_TWO + 3), row(at + AT_TWO + 4)
        G_two = [from_two(z) for z in (pair, pair, two[0], last, two[1], two[2])]
        G_two[1] = from_two(pair, packed_second=True)
        G_three = [row(at + AT_THREE), row(at + AT_THREE + 1), three[0], row(at + AT_THREE + 2), three[1], three[2]]
        for i in range(6):
            blocks[base + i] = row(at + i) + G_two[i] + from_below(G_three[i])
        terms = s_terms(at + AT_THREE + 3, at + AT_TWO)
        starts.append([row(at + 6 + i) - terms[i] for i in range(6)])
    for i in range(5):
        packed = row(AT_E2 + i)
        blocks[84 + i] = packed
        if i < 4:
            blocks[89 + i] = roll(packed, -32, 1)
    terms = s_terms(AT_E2 + 11, AT_E2 + 17)
    outer = [row(AT_E2 + 5 + i) - terms[i] for i in range(6)]
    window = Window(lambda i: blocks[i], n_dev)
    v, e = starts
    w, f = window.apply(v, e, outer, (0, 1))
    last, _ = window.apply(w, f, f, (0,))
    for i in range(6):
        v0[i] = v[i]
        e0[i] = e[i]
        v1[i] = w[i]
        e1[i] = f[i]
        v2[i] = last[i]


def moments_kernel(blocks, v0, v1, v2, above, below, kept_hbm, e2, v3, e3, out, kept, sems):
    fetch = pltpu.make_async_copy(kept_hbm, kept, sems.at[0])
    fetch.start()
    shape = v2.shape[1:]
    n_dev = shape[0] // 2
    bits = lane_bits(shape)
    row_zero, _ = bits
    window = Window(lambda i: blocks[i], n_dev)
    v = [v2[i] for i in range(6)]
    side = [jnp.where(row_zero, above[i], below[i]) for i in range(6)]
    outer = [jnp.where(row_zero, below[i], above[i]) for i in range(6)]
    w, f = window.apply(v, side, outer, (0, 1))
    for i in range(6):
        e2[i] = side[i]
        v3[i] = w[i]
        e3[i] = f[i]
    vs = [[v0[i] for i in range(6)], [v1[i] for i in range(6)], v, w]

    def dot(left, right):
        return sum(a[:n_dev] * b[:n_dev] for a, b in zip(left, right))

    products = [dot(vs[n // 2], vs[n - n // 2]) for n in range(7)]
    energy = 0.0
    for half in range(2):
        a = w[3 * half : 3 * half + 3]
        b = f[3 * half : 3 * half + 3]
        after = [window.seconds(a[j], jnp.where(row_zero, roll(a[j], -32, 1), roll(b[j], 32, 1))) for j in range(3)]
        for i in range(3):
            inner = sum(window.d(0, i, j) * a[j] for j in range(3))
            for kind in range(4):
                inner = inner - 2.0 * sum(window.c(0, kind, i, j) * after[j][kind] for j in range(3))
            energy = energy + a[i][:n_dev] * inner[:n_dev]
    products.append(energy)
    lane = lax.broadcasted_iota(jnp.int32, (1, 128), 1)
    packed = jnp.zeros((1, 128), jnp.float32)
    for n, value in enumerate(products):
        value = jnp.sum(jnp.sum(value, axis=0, keepdims=True), axis=1, keepdims=True)
        packed = jnp.where(lane == n, value, packed)
    out[...] = packed
    fetch.wait()


def coefficients(moments):
    zero = jnp.zeros_like(moments[0])

    def inner(s, p, offset):
        total = zero
        for i, a in enumerate(s):
            for j, b in enumerate(p):
                total = total + a * b * moments[i + j + offset]
        return total

    def energy(p):
        return inner(p, p, 1) + HALF * inner(p, p, 0)

    s = [zero + 1.0]
    p = [zero + 1.0]
    x = [zero] * ITERS
    gamma = inner(s, s, 0)
    for sweep in range(ITERS):
        alpha = gamma / energy(p)
        x = [x[i] + (alpha * p[i] if i < len(p) else 0.0) for i in range(ITERS)]
        if sweep < ITERS - 1:
            image = [(p[i - 1] if i else 0.0) + (HALF * p[i] if i < len(p) else 0.0) for i in range(len(p) + 1)]
            s = [(s[i] if i < len(s) else 0.0) - alpha * image[i] for i in range(len(image))]
            gamma_new = inner(s, s, 0)
            beta = gamma_new / gamma
            p = [s[i] + (beta * p[i] if i < len(p) else 0.0) for i in range(len(s))]
            gamma = gamma_new
    return [value * (1.0 / SPAN) for value in x]


def finish_kernel(flags, counts_ref, sums, v0, v1, v2, v3, n0, n1, n2, n3, kept, affines, residual_hbm, residual, sems):
    stores = []
    total = jnp.sum(sums[...], axis=0, keepdims=True)
    lane = lax.broadcasted_iota(jnp.int32, (1, 128), 1)
    moments = [jnp.sum(jnp.where(lane == n, total, 0.0), axis=1, keepdims=True) for n in range(8)]
    weights = coefficients(moments)
    at = flags[2]
    alive = live_counts(flags, counts_ref)
    row_zero, sec_zero = lane_bits((1, 128))

    def mix(refs, i, dev):
        return sum(w * ref[i, pl.ds(dev, 1), :] for w, ref in zip(weights, refs))

    vs = (v0, v1, v2, v3)
    x = [mix(vs, i, at) for i in range(6)]
    above = [mix(vs, i, at + 1) for i in range(6)]
    beside = [mix((n0, n1, n2, n3), i, at) for i in range(6)]
    for i in range(6):
        for sec in range(2):
            for row in range(2):
                start = 64 * sec + 32 * row
                affines[i, sec, row : row + 1, :] = x[i][:, start : start + 32]
    for kind in range(4):
        if kind == 0:
            b = [roll(z, -1, 1) for z in x]
        elif kind == 1:
            b = [jnp.where(row_zero, roll(z, -32, 1), roll(w, 32, 1)) for z, w in zip(x, beside)]
        elif kind == 2:
            b = [jnp.where(sec_zero, roll(z, 64, 1), roll(w, 64, 1)) for z, w in zip(x, above)]
        else:
            b = above
        u, v, p, q = (kept[4 * kind + i] for i in range(4))
        live = live_points(alive[kind])
        for comp in range(2):
            o = 3 * comp
            r = (p - u) if comp == 0 else (q - v)
            r = r - (x[o] * u + x[o + 1] * v) + (b[o] * p + b[o + 1] * q) - live * (x[o + 2] - b[o + 2])
            residual[pl.ds(kind * 256 + comp, 128, stride=2), :] = r.T
        part = pl.ds(kind * 256, 256)
        stores.append(pltpu.make_async_copy(residual.at[part], residual_hbm.at[part], sems.at[kind]))
        stores[-1].start()
    for store in stores:
        store.wait()


def shape_of(*shape):
    return jax.ShapeDtypeStruct(shape, jnp.float32)


def call(interpret, kernel, outs, *args, scalars=0, anywhere=(), copies=0, buffers=(), results=None):
    spaces = []
    args = list(args)
    shapes = [shape_of(*out) for out in outs]
    for n, arg in enumerate(args):
        if n < scalars:
            spaces.append(pl.BlockSpec(memory_space=pltpu.SMEM))
        elif n in anywhere:
            spaces.append(pl.BlockSpec(memory_space=pl.ANY))
        else:
            spaces.append(pl.BlockSpec(memory_space=pltpu.VMEM))
            if arg.dtype == jnp.float32 and not interpret:
                args[n] = pltpu.with_memory_space_constraint(arg, pltpu.VMEM)
    if not results and not interpret:
        shapes = [pltpu.VMEM(out, jnp.float32) for out in outs]
    results = results or [pltpu.VMEM] * len(outs)
    return pl.pallas_call(
        kernel,
        out_shape=shapes,
        in_specs=spaces,
        out_specs=[pl.BlockSpec(memory_space=space) for space in results],
        scratch_shapes=[pltpu.VMEM(b, jnp.float32) for b in buffers]
        + ([pltpu.SemaphoreType.DMA((copies,))] if copies else []),
        interpret=interpret,
    )(*args)


def shifted(value, axes, steps):
    count = lax.axis_size(axes)
    pairs = [(i, i + steps) for i in range(count) if 0 <= i + steps < count]
    return lax.ppermute(value, axes, pairs)


def pack_up(run, g):
    return run(pack_up_kernel, [(192, 128), (192, 128)], g, anywhere=(0,), copies=3)


def pack_rows(run, f, g, counts):
    return run(pack_rows_kernel, [(128, 128), (136, 128)], f, g, counts, anywhere=(0, 1), copies=4)


def per_device(interpret, first_pts, second_pts, counts):
    run = functools.partial(call, interpret)
    n_sec = lax.axis_size(SEC_AXES)
    n_dev = lax.axis_size(GROUP)
    n_group = n_sec // n_dev
    sec = lax.axis_index(SEC_AXES)
    f = first_pts.reshape(1024, 128)
    g = second_pts.reshape(1024, 128)
    flags = jnp.stack(
        [
            (lax.axis_index("row") == lax.axis_size("row") - 1).astype(jnp.int32),
            (sec == n_sec - 1).astype(jnp.int32),
            lax.axis_index(GROUP).astype(jnp.int32),
        ]
    )

    up, rest = pack_up(run, g)
    up = shifted(up, SEC_AXES, -1)
    relay = n_dev - 2
    inside = [(i + 1, i) for i in range(n_sec - 1) if (i + 1) % n_dev]
    to_relay = [(group * n_dev, group * n_dev + relay) for group in range(1, n_group)]
    from_relay = [(group * n_dev + relay, group * n_dev - 1) for group in range(1, n_group)]
    relayed = lax.ppermute(rest, SEC_AXES, to_relay)
    relayed, f_later, g_later = lax.optimization_barrier((relayed, f, g))
    outside = lax.ppermute(relayed, SEC_AXES, from_relay)
    beside, odd, rest = lax.optimization_barrier((*pack_rows(run, f_later, g_later, counts), rest))
    rest = lax.ppermute(rest, SEC_AXES, inside)
    beside = shifted(beside, "row", -1)
    low = shifted(odd, "row", 1)
    packet, kept = run(gram_kernel, [(ROWS, 128), (16, 128, 128)], flags, f, g, counts, up, rest, outside, beside, low, scalars=1)

    half = n_dev // 2
    pairs = []
    for group in range(n_group):
        for dev in range(n_dev):
            source = group + (1 if dev < half else -1)
            if 0 <= source < n_group:
                pairs.append((source * n_dev + dev, group * n_dev + dev))
    other = lax.ppermute(packet, SEC_AXES, pairs)
    both = jnp.concatenate([packet, other], axis=0)
    (mine,) = run(merge_kernel, [(2 * DOUBLE, 128)], both, shifted(both, "row", -1), shifted(both, "row", 1))
    got = lax.all_to_all(jnp.broadcast_to(mine[None], (n_dev, 2 * DOUBLE, 128)), GROUP, 0, 0, tiled=False)
    wide = (6, 2 * n_dev, 128)
    blocks, v0, e0, v1, e1, v2 = run(
        window_kernel, [(93, 2 * n_dev, 128)] + [wide] * 5, got.reshape(n_dev * 2 * DOUBLE, 128)
    )
    e2, v3, e3, part, kept = run(
        moments_kernel,
        [wide, wide, wide, (1, 128), (16, 128, 128)],
        blocks,
        v0,
        v1,
        v2,
        shifted(v2, "row", -1),
        shifted(v2, "row", 1),
        kept,
        anywhere=(6,),
        copies=1,
    )
    n_other = lax.axis_size(OTHERS)
    sums = lax.all_to_all(jnp.broadcast_to(part[None], (n_other, 1, 128)), OTHERS, 0, 0, tiled=False)
    affines, residual = run(
        finish_kernel,
        [(6,) + counts.shape[1:], (1024, 128)],
        flags,
        counts,
        sums.reshape(n_other, 128),
        v0,
        v1,
        v2,
        v3,
        e0,
        e1,
        e2,
        e3,
        kept,
        scalars=1,
        copies=4,
        buffers=[(1024, 128)],
        results=[pltpu.VMEM, pl.ANY],
    )
    return affines, residual.reshape(first_pts.shape)


def split_mesh(mesh):
    n_row = mesh.shape["row"]
    return Mesh(mesh.devices.reshape(4, 4, 4, 2, n_row), SEC_AXES + ("row",))


def solution(mesh, inner=None, interpret=False):
    inner = inner or split_mesh(mesh)
    in_specs = (
        P(None, SEC_AXES, "row", None, None, None),
        P(None, SEC_AXES, "row", None, None, None),
        P(None, SEC_AXES, "row", None),
    )
    out_specs = (P(None, SEC_AXES, "row", None), P(None, SEC_AXES, "row", None, None, None))
    return jax.shard_map(
        functools.partial(per_device, interpret), mesh=inner, in_specs=in_specs, out_specs=out_specs, check_vma=False
    )
```

```python
import functools

import jax
import jax.numpy as jnp
from jax import lax
from jax.experimental import pallas as pl
from jax.experimental.pallas import tpu as pltpu
from jax.sharding import Mesh
from jax.sharding import PartitionSpec as P

ITERS = 4
SPAN = 1024.0
SHIFT = 512.0
HALF = SHIFT / SPAN
SQUARES = (0.49, 0.49, 0.09)
SYM = ((0, 0), (0, 1), (0, 2), (1, 1), (1, 2), (2, 2))
SEC_AXES = ("y", "zhi", "x", "core")
GROUP = ("x", "core")
OTHERS = ("y", "zhi", "row")
EVERY = SEC_AXES + ("row",)

ROWS = 64
AT_C = 12
AT_THREE = 48
AT_TWO = 57
USED = 62
AT_E = 62
AT_E2 = 124
DOUBLE = 144
BEYOND = [6 + i for i in range(6)] + [AT_THREE + 3 + i for i in range(6)] + [AT_TWO + i for i in range(3)]


def sym_at(a, b):
    return SYM.index((min(a, b), max(a, b)))


def roll(value, shift, axis):
    size = value.shape[axis]
    return pltpu.roll(value, shift % size, axis)


def lane_bits(shape):
    lane = lax.broadcasted_iota(jnp.int32, shape, len(shape) - 1)
    return (lane // 32) % 2 == 0, lane < 64


def counts_row(ref, kind):
    cells = [ref[kind, sec, row : row + 1, :] for sec in range(2) for row in range(2)]
    return jnp.concatenate(cells, axis=1).astype(jnp.float32)


def live_counts(flags, counts_ref):
    row_zero, sec_zero = lane_bits((1, 128))
    lane = lax.broadcasted_iota(jnp.int32, (1, 128), 1)
    last_row = flags[0] == 1
    last_sec = flags[1] == 1
    zero = jnp.zeros((1, 128), jnp.float32)
    counts = [counts_row(counts_ref, kind) for kind in range(4)]
    return [
        jnp.where(lane % 32 == 31, zero, counts[0]),
        jnp.where(jnp.logical_and(jnp.logical_not(row_zero), last_row), zero, counts[1]),
        jnp.where(jnp.logical_and(jnp.logical_not(sec_zero), last_sec), zero, counts[2]),
        jnp.where(last_sec, zero, counts[3]),
    ]


def live_points(count):
    point = lax.broadcasted_iota(jnp.int32, (128, 128), 0).astype(jnp.float32)
    return jnp.where(point < count, 1.0, 0.0)


def block_sums(first, second, live):
    u, v = first
    p, q = second
    dx = p - u
    dy = q - v

    def red(z):
        return jnp.sum(z, axis=0, keepdims=True)

    su, sv, sp, sq, n = red(u), red(v), red(p), red(q), red(live)
    F = [red(u * u), red(u * v), su, red(v * v), sv, n]
    G = [red(p * p), red(p * q), sp, red(q * q), sq, n]
    C = [red(u * p), red(u * q), su, red(v * p), red(v * q), sv, sp, sq, n]
    tx, ty = red(dx), red(dy)
    s1 = [red(dx * u), red(dx * v), tx, red(dy * u), red(dy * v), ty]
    s2 = [red(dx * p), red(dx * q), tx, red(dy * p), red(dy * q), ty]
    return F, G, C, s1, s2


def gram_kernel(flags, f_ref, g_ref, counts_ref, up_ref, rest_ref, outside_ref, next_ref, low_ref, packet, kept):
    row_zero, sec_zero = lane_bits((1, 128))

    def pair_rows(ref, start, count, comp):
        return ref[pl.ds(2 * start + comp, count, stride=2), :]

    def own(ref, kind):
        return [pair_rows(ref, kind * 128, 128, comp).T for comp in range(2)]

    zero = jnp.zeros((1, 128), jnp.float32)
    alive = live_counts(flags, counts_ref)

    def masked(points, count):
        live = live_points(count)
        return [z * live for z in points], live

    def second_of(kind):
        if kind == 0:
            return [roll(z, -1, 1) for z in own(g_ref, 0)]
        out = []
        for comp in range(2):
            if kind == 1:
                parts = [
                    pair_rows(g_ref, 128 + 32, 32, comp),
                    pair_rows(next_ref, 0, 32, comp),
                    pair_rows(g_ref, 128 + 96, 32, comp),
                    pair_rows(next_ref, 32, 32, comp),
                ]
            elif kind == 2:
                parts = [pair_rows(g_ref, 256 + 64, 64, comp), pair_rows(up_ref, 0, 64, comp)]
            else:
                rest = pair_rows(rest_ref, 0, 96, comp) + pair_rows(outside_ref, 0, 96, comp)
                parts = [pair_rows(up_ref, 64, 32, comp), rest]
            out.append(jnp.concatenate(parts, axis=0).T)
        return out

    D = [zero] * 6
    S = [zero] * 6
    unit = 1.0 / SPAN

    def put(row, value):
        packet[row : row + 1, :] = value

    for kind in range(4):
        first, live = masked(own(f_ref, kind), alive[kind])
        second, _ = masked(second_of(kind), alive[kind])
        for i, points in enumerate(first + second):
            kept[4 * kind + i] = points
        F, G, C, s1, s2 = block_sums(first, second, live)
        D = [a + b for a, b in zip(D, F)]
        S = [a + b for a, b in zip(S, s1)]
        for i in range(9):
            put(AT_C + 9 * kind + i, C[i] * unit)
        if kind == 0:
            D = [a + roll(b, 1, 1) for a, b in zip(D, G)]
            S = [a - roll(b, 1, 1) for a, b in zip(S, s2)]
        elif kind == 1:
            D = [a + jnp.where(row_zero, zero, roll(b, 32, 1)) for a, b in zip(D, G)]
            S = [a - jnp.where(row_zero, zero, roll(b, 32, 1)) for a, b in zip(S, s2)]
        elif kind == 2:
            D = [a + jnp.where(sec_zero, zero, roll(b, 64, 1)) for a, b in zip(D, G)]
            S = [a - jnp.where(sec_zero, zero, roll(b, 64, 1)) for a, b in zip(S, s2)]
            for i in range(3):
                put(AT_TWO + i, jnp.where(sec_zero, roll(s2[3 + i], 64, 1), s2[i]))
            put(AT_TWO + 3, jnp.where(sec_zero, roll(G[1], 64, 1), G[0]) * unit)
            put(AT_TWO + 4, G[3] * unit)
        else:
            put(AT_THREE, G[0] * unit)
            put(AT_THREE + 1, G[1] * unit)
            put(AT_THREE + 2, G[3] * unit)
            for i in range(6):
                put(AT_THREE + 3 + i, s2[i])

    low_count = jnp.where(row_zero, zero, low_ref[128:129, :])
    first = []
    second = []
    for comp in range(2):
        low = [pair_rows(low_ref, 32 * sec, 32, comp) for sec in range(2)]
        first.append(jnp.concatenate([low[0], low[0], low[1], low[1]], axis=0).T)
        mine = [pair_rows(g_ref, 128 + 64 * sec, 32, comp) for sec in range(2)]
        second.append(jnp.concatenate([mine[0], mine[0], mine[1], mine[1]], axis=0).T)
    first, live = masked(first, low_count)
    second, _ = masked(second, low_count)
    F, G, C, s1, s2 = block_sums(first, second, live)
    D = [a + jnp.where(row_zero, roll(b, -32, 1), zero) for a, b in zip(D, G)]
    S = [a - jnp.where(row_zero, roll(b, -32, 1), zero) for a, b in zip(S, s2)]

    for i in range(6):
        a, b = SYM[i]
        put(i, D[i] * unit + ((SQUARES[a] - SHIFT) * unit if a == b else 0.0))
        put(6 + i, S[i])
    for row in range(USED, ROWS):
        put(row, zero)


def from_above(value):
    return roll(value, -1, 0)


def from_below(value):
    return roll(value, 1, 0)


def pack_up_kernel(g_ref, up, rest, sems):
    copies = [
        pltpu.make_async_copy(g_ref.at[pl.ds(512, 128)], up.at[pl.ds(0, 128)], sems.at[0]),
        pltpu.make_async_copy(g_ref.at[pl.ds(768, 64)], up.at[pl.ds(128, 64)], sems.at[1]),
        pltpu.make_async_copy(g_ref.at[pl.ds(832, 192)], rest, sems.at[2]),
    ]
    for copy in copies:
        copy.start()
    for copy in copies:
        copy.wait()


def pack_rows_kernel(f_ref, g_ref, counts_ref, beside, odd, sems):
    copies = [
        pltpu.make_async_copy(g_ref.at[pl.ds(256, 64)], beside.at[pl.ds(0, 64)], sems.at[0]),
        pltpu.make_async_copy(g_ref.at[pl.ds(384, 64)], beside.at[pl.ds(64, 64)], sems.at[1]),
        pltpu.make_async_copy(f_ref.at[pl.ds(320, 64)], odd.at[pl.ds(0, 64)], sems.at[2]),
        pltpu.make_async_copy(f_ref.at[pl.ds(448, 64)], odd.at[pl.ds(64, 64)], sems.at[3]),
    ]
    for copy in copies:
        copy.start()
    odd[128:136, :] = jnp.broadcast_to(counts_row(counts_ref, 1), (8, 128))
    for copy in copies:
        copy.wait()


def merge_kernel(both, above, below, out):
    row_zero, _ = lane_bits((1, 128))
    for part in range(2):
        at = part * ROWS
        to = part * DOUBLE
        out[to : to + USED, :] = both[at : at + USED, :]
        a = above[at : at + USED, :]
        b = below[at : at + USED, :]
        out[to + AT_E : to + AT_E + USED, :] = jnp.where(row_zero, a, b)
        first = AT_C + 9
        for i in range(5):
            one, two = b[first + i : first + i + 1], b[first + min(5 + i, 8) : first + min(5 + i, 8) + 1]
            out[to + AT_E2 + i : to + AT_E2 + i + 1, :] = jnp.where(row_zero, one, roll(two, 32, 1))
        for i, source in enumerate(BEYOND):
            out[to + AT_E2 + 5 + i : to + AT_E2 + 6 + i, :] = jnp.where(
                row_zero, b[source : source + 1], a[source : source + 1]
            )


class Window:
    def __init__(self, load, n_dev):
        self.load = load
        self.bits = lane_bits((2 * n_dev, 128))

    def seconds(self, v, row_values):
        row_zero, sec_zero = self.bits
        half = roll(v, 64, 1)
        return [
            roll(v, -1, 1),
            row_values,
            jnp.where(sec_zero, half, from_above(half)),
            from_above(v),
        ]

    def row_pairs(self, v, e, e2):
        row_zero, _ = self.bits
        forth, back = roll(v, 32, 1), roll(v, -32, 1)
        own = jnp.where(row_zero, back, roll(e, 32, 1))
        side = jnp.where(row_zero, roll(e2, -32, 1), forth)
        return own, side

    def c(self, side, kind, i, j):
        return self.load(side * 42 + 6 + 9 * kind + 3 * i + j)

    def d(self, side, i, j):
        return self.load(side * 42 + sym_at(i, j))

    def c_e2(self, i, j):
        return self.load(84 + 3 * i + j)

    def transposed(self, c, a):
        return [c(0, j) * a[0] + c(1, j) * a[1] + c(2, j) * a[2] for j in range(3)]

    def apply(self, v, e, e2, sides):
        row_zero, sec_zero = self.bits
        outs = ([None] * 6, [None] * 6)
        for half in range(2):
            span = slice(3 * half, 3 * half + 3)
            sets = (v[span], e[span])
            beyond = e2[span]
            pairs = [self.row_pairs(*z) for z in zip(v[span], e[span], beyond)]
            t_row = [self.transposed(functools.partial(self.c, side, 1), sets[side]) for side in range(2)]
            for side in sides:
                a = sets[side]
                after = [self.seconds(a[j], pairs[j][side]) for j in range(3)]
                total = []
                for i in range(3):
                    y = sum(self.d(side, i, j) * a[j] for j in range(3))
                    for kind in range(4):
                        y = y - sum(self.c(side, kind, i, j) * after[j][kind] for j in range(3))
                    total.append(y)
                col = self.transposed(functools.partial(self.c, side, 0), a)
                one = self.transposed(functools.partial(self.c, side, 2), a)
                two = self.transposed(functools.partial(self.c, side, 3), a)
                if side == 1:
                    outer = self.transposed(self.c_e2, beyond)
                for j in range(3):
                    t = roll(one[j], 64, 1)
                    y = total[j] - roll(col[j], 1, 1) - jnp.where(sec_zero, from_below(t), t) - from_below(two[j])
                    if side == 0:
                        y = y - jnp.where(row_zero, roll(t_row[1][j], -32, 1), roll(t_row[0][j], 32, 1))
                    else:
                        y = y - jnp.where(row_zero, roll(t_row[0][j], -32, 1), roll(outer[j], 32, 1))
                    outs[side][3 * half + j] = y
        return outs


def window_kernel(got, blocks, v0, e0, v1, e1, v2):
    n_dev = got.shape[0] // (2 * DOUBLE)
    row_zero, sec_zero = lane_bits((2 * n_dev, 128))
    zero = jnp.zeros((2 * n_dev, 128), jnp.float32)

    def row(i):
        return jnp.concatenate(
            [got[pl.ds(slot * DOUBLE + i, n_dev, stride=2 * DOUBLE), :] for slot in range(2)], axis=0
        )

    def from_two(value, packed_second=False):
        if not packed_second:
            value = roll(value, 64, 1)
        return from_below(jnp.where(sec_zero, value, zero))

    def s_terms(three, two):
        return [
            from_below(row(three + i)) + from_two(row(two + i % 3), packed_second=i >= 3) for i in range(6)
        ]

    starts = []
    for side, at in enumerate((0, AT_E)):
        base = side * 42
        for i in range(36):
            blocks[base + 6 + i] = row(at + AT_C + i)
        two = [blocks[base + 24 + i] for i in (6, 7, 8)]
        three = [blocks[base + 33 + i] for i in (6, 7, 8)]
        pair, last = row(at + AT_TWO + 3), row(at + AT_TWO + 4)
        G_two = [from_two(z) for z in (pair, pair, two[0], last, two[1], two[2])]
        G_two[1] = from_two(pair, packed_second=True)
        G_three = [row(at + AT_THREE), row(at + AT_THREE + 1), three[0], row(at + AT_THREE + 2), three[1], three[2]]
        for i in range(6):
            blocks[base + i] = row(at + i) + G_two[i] + from_below(G_three[i])
        terms = s_terms(at + AT_THREE + 3, at + AT_TWO)
        starts.append([row(at + 6 + i) - terms[i] for i in range(6)])
    for i in range(5):
        packed = row(AT_E2 + i)
        blocks[84 + i] = packed
        if i < 4:
            blocks[89 + i] = roll(packed, -32, 1)
    terms = s_terms(AT_E2 + 11, AT_E2 + 17)
    outer = [row(AT_E2 + 5 + i) - terms[i] for i in range(6)]
    window = Window(lambda i: blocks[i], n_dev)
    v, e = starts
    w, f = window.apply(v, e, outer, (0, 1))
    last, _ = window.apply(w, f, f, (0,))
    for i in range(6):
        v0[i] = v[i]
        e0[i] = e[i]
        v1[i] = w[i]
        e1[i] = f[i]
        v2[i] = last[i]


def moments_kernel(blocks, v0, v1, v2, above, below, kept_hbm, e2, v3, e3, out, kept, sems):
    fetch = pltpu.make_async_copy(kept_hbm, kept, sems.at[0])
    fetch.start()
    shape = v2.shape[1:]
    n_dev = shape[0] // 2
    bits = lane_bits(shape)
    row_zero, _ = bits
    window = Window(lambda i: blocks[i], n_dev)
    v = [v2[i] for i in range(6)]
    side = [jnp.where(row_zero, above[i], below[i]) for i in range(6)]
    outer = [jnp.where(row_zero, below[i], above[i]) for i in range(6)]
    w, f = window.apply(v, side, outer, (0, 1))
    for i in range(6):
        e2[i] = side[i]
        v3[i] = w[i]
        e3[i] = f[i]
    vs = [[v0[i] for i in range(6)], [v1[i] for i in range(6)], v, w]

    def dot(left, right):
        return sum(a[:n_dev] * b[:n_dev] for a, b in zip(left, right))

    products = [dot(vs[n // 2], vs[n - n // 2]) for n in range(7)]
    energy = 0.0
    for half in range(2):
        a = w[3 * half : 3 * half + 3]
        b = f[3 * half : 3 * half + 3]
        after = [window.seconds(a[j], jnp.where(row_zero, roll(a[j], -32, 1), roll(b[j], 32, 1))) for j in range(3)]
        for i in range(3):
            inner = sum(window.d(0, i, j) * a[j] for j in range(3))
            for kind in range(4):
                inner = inner - 2.0 * sum(window.c(0, kind, i, j) * after[j][kind] for j in range(3))
            energy = energy + a[i][:n_dev] * inner[:n_dev]
    products.append(energy)
    lane = lax.broadcasted_iota(jnp.int32, (1, 128), 1)
    packed = jnp.zeros((1, 128), jnp.float32)
    for n, value in enumerate(products):
        value = jnp.sum(jnp.sum(value, axis=0, keepdims=True), axis=1, keepdims=True)
        packed = jnp.where(lane == n, value, packed)
    out[...] = packed
    fetch.wait()


def coefficients(moments):
    zero = jnp.zeros_like(moments[0])

    def inner(s, p, offset):
        total = zero
        for i, a in enumerate(s):
            for j, b in enumerate(p):
                total = total + a * b * moments[i + j + offset]
        return total

    def energy(p):
        return inner(p, p, 1) + HALF * inner(p, p, 0)

    s = [zero + 1.0]
    p = [zero + 1.0]
    x = [zero] * ITERS
    gamma = inner(s, s, 0)
    for sweep in range(ITERS):
        alpha = gamma / energy(p)
        x = [x[i] + (alpha * p[i] if i < len(p) else 0.0) for i in range(ITERS)]
        if sweep < ITERS - 1:
            image = [(p[i - 1] if i else 0.0) + (HALF * p[i] if i < len(p) else 0.0) for i in range(len(p) + 1)]
            s = [(s[i] if i < len(s) else 0.0) - alpha * image[i] for i in range(len(image))]
            gamma_new = inner(s, s, 0)
            beta = gamma_new / gamma
            p = [s[i] + (beta * p[i] if i < len(p) else 0.0) for i in range(len(s))]
            gamma = gamma_new
    return [value * (1.0 / SPAN) for value in x]


def finish_kernel(flags, counts_ref, sums, v0, v1, v2, v3, n0, n1, n2, n3, kept, affines, residual_hbm, residual, sems):
    stores = []
    total = jnp.sum(sums[...], axis=0, keepdims=True)
    lane = lax.broadcasted_iota(jnp.int32, (1, 128), 1)
    moments = [jnp.sum(jnp.where(lane == n, total, 0.0), axis=1, keepdims=True) for n in range(8)]
    weights = coefficients(moments)
    at = flags[2]
    alive = live_counts(flags, counts_ref)
    row_zero, sec_zero = lane_bits((1, 128))

    def mix(refs, i, dev):
        return sum(w * ref[i, pl.ds(dev, 1), :] for w, ref in zip(weights, refs))

    vs = (v0, v1, v2, v3)
    x = [mix(vs, i, at) for i in range(6)]
    above = [mix(vs, i, at + 1) for i in range(6)]
    beside = [mix((n0, n1, n2, n3), i, at) for i in range(6)]
    for i in range(6):
        for sec in range(2):
            for row in range(2):
                start = 64 * sec + 32 * row
                affines[i, sec, row : row + 1, :] = x[i][:, start : start + 32]
    for kind in range(4):
        if kind == 0:
            b = [roll(z, -1, 1) for z in x]
        elif kind == 1:
            b = [jnp.where(row_zero, roll(z, -32, 1), roll(w, 32, 1)) for z, w in zip(x, beside)]
        elif kind == 2:
            b = [jnp.where(sec_zero, roll(z, 64, 1), roll(w, 64, 1)) for z, w in zip(x, above)]
        else:
            b = above
        u, v, p, q = (kept[4 * kind + i] for i in range(4))
        live = live_points(alive[kind])
        for comp in range(2):
            o = 3 * comp
            r = (p - u) if comp == 0 else (q - v)
            r = r - (x[o] * u + x[o + 1] * v) + (b[o] * p + b[o + 1] * q) - live * (x[o + 2] - b[o + 2])
            residual[pl.ds(kind * 256 + comp, 128, stride=2), :] = r.T
        part = pl.ds(kind * 256, 256)
        stores.append(pltpu.make_async_copy(residual.at[part], residual_hbm.at[part], sems.at[kind]))
        stores[-1].start()
    for store in stores:
        store.wait()


def shape_of(*shape):
    return jax.ShapeDtypeStruct(shape, jnp.float32)


def call(interpret, kernel, outs, *args, scalars=0, anywhere=(), copies=0, buffers=(), results=None):
    spaces = []
    args = list(args)
    shapes = [shape_of(*out) for out in outs]
    for n, arg in enumerate(args):
        if n < scalars:
            spaces.append(pl.BlockSpec(memory_space=pltpu.SMEM))
        elif n in anywhere:
            spaces.append(pl.BlockSpec(memory_space=pl.ANY))
        else:
            spaces.append(pl.BlockSpec(memory_space=pltpu.VMEM))
            if arg.dtype == jnp.float32 and not interpret:
                args[n] = pltpu.with_memory_space_constraint(arg, pltpu.VMEM)
    if not results and not interpret:
        shapes = [pltpu.VMEM(out, jnp.float32) for out in outs]
    results = results or [pltpu.VMEM] * len(outs)
    return pl.pallas_call(
        kernel,
        out_shape=shapes,
        in_specs=spaces,
        out_specs=[pl.BlockSpec(memory_space=space) for space in results],
        scratch_shapes=[pltpu.VMEM(b, jnp.float32) for b in buffers]
        + ([pltpu.SemaphoreType.DMA((copies,))] if copies else []),
        interpret=interpret,
    )(*args)


def shifted(value, axes, steps):
    count = lax.axis_size(axes)
    pairs = [(i, i + steps) for i in range(count) if 0 <= i + steps < count]
    return lax.ppermute(value, axes, pairs)


def pack_up(run, g):
    return run(pack_up_kernel, [(192, 128), (192, 128)], g, anywhere=(0,), copies=3)


def pack_rows(run, f, g, counts):
    return run(pack_rows_kernel, [(128, 128), (136, 128)], f, g, counts, anywhere=(0, 1), copies=4)


def per_device(interpret, first_pts, second_pts, counts):
    run = functools.partial(call, interpret)
    n_sec = lax.axis_size(SEC_AXES)
    n_dev = lax.axis_size(GROUP)
    n_group = n_sec // n_dev
    sec = lax.axis_index(SEC_AXES)
    f = first_pts.reshape(1024, 128)
    g = second_pts.reshape(1024, 128)
    flags = jnp.stack(
        [
            (lax.axis_index("row") == lax.axis_size("row") - 1).astype(jnp.int32),
            (sec == n_sec - 1).astype(jnp.int32),
            lax.axis_index(GROUP).astype(jnp.int32),
        ]
    )

    up, rest = pack_up(run, g)
    up = shifted(up, SEC_AXES, -1)
    relay = n_dev - 2
    inside = [(i + 1, i) for i in range(n_sec - 1) if (i + 1) % n_dev]
    to_relay = [(group * n_dev, group * n_dev + relay) for group in range(1, n_group)]
    from_relay = [(group * n_dev + relay, group * n_dev - 1) for group in range(1, n_group)]
    relayed = lax.ppermute(rest, SEC_AXES, to_relay)
    relayed, f_later, g_later = lax.optimization_barrier((relayed, f, g))
    outside = lax.ppermute(relayed, SEC_AXES, from_relay)
    beside, odd, rest = lax.optimization_barrier((*pack_rows(run, f_later, g_later, counts), rest))
    rest = lax.ppermute(rest, SEC_AXES, inside)
    beside = shifted(beside, "row", -1)
    low = shifted(odd, "row", 1)
    packet, kept = run(gram_kernel, [(ROWS, 128), (16, 128, 128)], flags, f, g, counts, up, rest, outside, beside, low, scalars=1)

    half = n_dev // 2
    pairs = []
    for group in range(n_group):
        for dev in range(n_dev):
            source = group + (1 if dev < half else -1)
            if 0 <= source < n_group:
                pairs.append((source * n_dev + dev, group * n_dev + dev))
    other = lax.ppermute(packet, SEC_AXES, pairs)
    both = jnp.concatenate([packet, other], axis=0)
    (mine,) = run(merge_kernel, [(2 * DOUBLE, 128)], both, shifted(both, "row", -1), shifted(both, "row", 1))
    got = lax.all_to_all(jnp.broadcast_to(mine[None], (n_dev, 2 * DOUBLE, 128)), GROUP, 0, 0, tiled=False)
    wide = (6, 2 * n_dev, 128)
    blocks, v0, e0, v1, e1, v2 = run(
        window_kernel, [(93, 2 * n_dev, 128)] + [wide] * 5, got.reshape(n_dev * 2 * DOUBLE, 128)
    )
    e2, v3, e3, part, kept = run(
        moments_kernel,
        [wide, wide, wide, (1, 128), (16, 128, 128)],
        blocks,
        v0,
        v1,
        v2,
        shifted(v2, "row", -1),
        shifted(v2, "row", 1),
        kept,
        anywhere=(6,),
        copies=1,
    )
    n_other = lax.axis_size(OTHERS)
    groups = sum_groups([lax.axis_size(axis) for axis in EVERY])
    sums = lax.all_to_all(
        jnp.broadcast_to(part[None], (n_other, 1, 128)), EVERY, 0, 0, axis_index_groups=groups, tiled=False
    )
    affines, residual = run(
        finish_kernel,
        [(6,) + counts.shape[1:], (1024, 128)],
        flags,
        counts,
        sums.reshape(n_other, 128),
        v0,
        v1,
        v2,
        v3,
        e0,
        e1,
        e2,
        e3,
        kept,
        scalars=1,
        copies=4,
        buffers=[(1024, 128)],
        results=[pltpu.VMEM, pl.ANY],
    )
    return affines, residual.reshape(first_pts.shape)


def sum_groups(sizes):
    n_y, n_zhi, n_x, n_core, n_row = sizes
    groups = []
    for place in range(n_x * n_core):
        order = [((n_zhi - 1 + step) % n_zhi, y, row) for step in range(n_zhi) for y in range(n_y) for row in range(n_row)]
        groups.append([((y * n_zhi + zhi) * n_x * n_core + place) * n_row + row for zhi, y, row in order])
    return groups


def split_mesh(mesh):
    n_row = mesh.shape["row"]
    return Mesh(mesh.devices.reshape(4, 4, 4, 2, n_row), SEC_AXES + ("row",))


def solution(mesh, inner=None, interpret=False):
    inner = inner or split_mesh(mesh)
    in_specs = (
        P(None, SEC_AXES, "row", None, None, None),
        P(None, SEC_AXES, "row", None, None, None),
        P(None, SEC_AXES, "row", None),
    )
    out_specs = (P(None, SEC_AXES, "row", None), P(None, SEC_AXES, "row", None, None, None))
    return jax.shard_map(
        functools.partial(per_device, interpret), mesh=inner, in_specs=in_specs, out_specs=out_specs, check_vma=False
    )
```

```python
import functools

import jax
import jax.numpy as jnp
from jax import lax
from jax.experimental import pallas as pl
from jax.experimental.pallas import tpu as pltpu
from jax.sharding import Mesh
from jax.sharding import PartitionSpec as P

ITERS = 4
SPAN = 1024.0
SHIFT = 512.0
HALF = SHIFT / SPAN
SQUARES = (0.49, 0.49, 0.09)
SYM = ((0, 0), (0, 1), (0, 2), (1, 1), (1, 2), (2, 2))
SEC_AXES = ("y", "zhi", "x", "core")
GROUP = ("x", "core")
OTHERS = ("y", "zhi", "row")
EVERY = SEC_AXES + ("row",)

ROWS = 64
AT_C = 12
AT_THREE = 48
AT_TWO = 57
USED = 62
AT_E = 62
AT_E2 = 124
DOUBLE = 144
BEYOND = [6 + i for i in range(6)] + [AT_THREE + 3 + i for i in range(6)] + [AT_TWO + i for i in range(3)]


def sym_at(a, b):
    return SYM.index((min(a, b), max(a, b)))


def roll(value, shift, axis):
    size = value.shape[axis]
    return pltpu.roll(value, shift % size, axis)


def lane_bits(shape):
    lane = lax.broadcasted_iota(jnp.int32, shape, len(shape) - 1)
    return (lane // 32) % 2 == 0, lane < 64


def counts_row(ref, kind):
    cells = [ref[kind, sec, row : row + 1, :] for sec in range(2) for row in range(2)]
    return jnp.concatenate(cells, axis=1).astype(jnp.float32)


def live_counts(counts_ref, sizes):
    n_sec, n_row = sizes
    row_zero, sec_zero = lane_bits((1, 128))
    lane = lax.broadcasted_iota(jnp.int32, (1, 128), 1)
    section = 0
    for axis in SEC_AXES:
        section = section * lax.axis_size(axis) + lax.axis_index(axis)
    last_row = lax.axis_index("row") == n_row - 1
    last_sec = section == n_sec - 1
    zero = jnp.zeros((1, 128), jnp.float32)
    counts = [counts_row(counts_ref, kind) for kind in range(4)]
    return [
        jnp.where(lane % 32 == 31, zero, counts[0]),
        jnp.where(jnp.logical_and(jnp.logical_not(row_zero), last_row), zero, counts[1]),
        jnp.where(jnp.logical_and(jnp.logical_not(sec_zero), last_sec), zero, counts[2]),
        jnp.where(last_sec, zero, counts[3]),
    ]


def live_points(count):
    point = lax.broadcasted_iota(jnp.int32, (128, 128), 0).astype(jnp.float32)
    return jnp.where(point < count, 1.0, 0.0)


def block_sums(first, second, live):
    u, v = first
    p, q = second
    dx = p - u
    dy = q - v

    def red(z):
        return jnp.sum(z, axis=0, keepdims=True)

    su, sv, sp, sq, n = red(u), red(v), red(p), red(q), red(live)
    F = [red(u * u), red(u * v), su, red(v * v), sv, n]
    G = [red(p * p), red(p * q), sp, red(q * q), sq, n]
    C = [red(u * p), red(u * q), su, red(v * p), red(v * q), sv, sp, sq, n]
    tx, ty = red(dx), red(dy)
    s1 = [red(dx * u), red(dx * v), tx, red(dy * u), red(dy * v), ty]
    s2 = [red(dx * p), red(dx * q), tx, red(dy * p), red(dy * q), ty]
    return F, G, C, s1, s2


def gram_kernel(f_ref, g_ref, alive_ref, up_ref, rest_ref, outside_ref, next_ref, low_ref, packet, kept):
    row_zero, sec_zero = lane_bits((1, 128))

    def pair_rows(ref, start, count, comp):
        return ref[pl.ds(2 * start + comp, count, stride=2), :]

    def own(ref, kind):
        return [pair_rows(ref, kind * 128, 128, comp).T for comp in range(2)]

    zero = jnp.zeros((1, 128), jnp.float32)
    alive = [alive_ref[kind : kind + 1, :] for kind in range(4)]

    def masked(points, count):
        live = live_points(count)
        return [z * live for z in points], live

    def second_of(kind):
        if kind == 0:
            return [roll(z, -1, 1) for z in own(g_ref, 0)]
        out = []
        for comp in range(2):
            if kind == 1:
                parts = [
                    pair_rows(g_ref, 128 + 32, 32, comp),
                    pair_rows(next_ref, 0, 32, comp),
                    pair_rows(g_ref, 128 + 96, 32, comp),
                    pair_rows(next_ref, 32, 32, comp),
                ]
            elif kind == 2:
                parts = [pair_rows(g_ref, 256 + 64, 64, comp), pair_rows(up_ref, 0, 64, comp)]
            else:
                rest = pair_rows(rest_ref, 0, 96, comp) + pair_rows(outside_ref, 0, 96, comp)
                parts = [pair_rows(up_ref, 64, 32, comp), rest]
            out.append(jnp.concatenate(parts, axis=0).T)
        return out

    D = [zero] * 6
    S = [zero] * 6
    unit = 1.0 / SPAN

    def put(row, value):
        packet[row : row + 1, :] = value

    for kind in range(4):
        first, live = masked(own(f_ref, kind), alive[kind])
        second, _ = masked(second_of(kind), alive[kind])
        for i, points in enumerate(first + second):
            kept[4 * kind + i] = points
        F, G, C, s1, s2 = block_sums(first, second, live)
        D = [a + b for a, b in zip(D, F)]
        S = [a + b for a, b in zip(S, s1)]
        for i in range(9):
            put(AT_C + 9 * kind + i, C[i] * unit)
        if kind == 0:
            D = [a + roll(b, 1, 1) for a, b in zip(D, G)]
            S = [a - roll(b, 1, 1) for a, b in zip(S, s2)]
        elif kind == 1:
            D = [a + jnp.where(row_zero, zero, roll(b, 32, 1)) for a, b in zip(D, G)]
            S = [a - jnp.where(row_zero, zero, roll(b, 32, 1)) for a, b in zip(S, s2)]
        elif kind == 2:
            D = [a + jnp.where(sec_zero, zero, roll(b, 64, 1)) for a, b in zip(D, G)]
            S = [a - jnp.where(sec_zero, zero, roll(b, 64, 1)) for a, b in zip(S, s2)]
            for i in range(3):
                put(AT_TWO + i, jnp.where(sec_zero, roll(s2[3 + i], 64, 1), s2[i]))
            put(AT_TWO + 3, jnp.where(sec_zero, roll(G[1], 64, 1), G[0]) * unit)
            put(AT_TWO + 4, G[3] * unit)
        else:
            put(AT_THREE, G[0] * unit)
            put(AT_THREE + 1, G[1] * unit)
            put(AT_THREE + 2, G[3] * unit)
            for i in range(6):
                put(AT_THREE + 3 + i, s2[i])

    low_count = jnp.where(row_zero, zero, low_ref[128:129, :])
    first = []
    second = []
    for comp in range(2):
        low = [pair_rows(low_ref, 32 * sec, 32, comp) for sec in range(2)]
        first.append(jnp.concatenate([low[0], low[0], low[1], low[1]], axis=0).T)
        mine = [pair_rows(g_ref, 128 + 64 * sec, 32, comp) for sec in range(2)]
        second.append(jnp.concatenate([mine[0], mine[0], mine[1], mine[1]], axis=0).T)
    first, live = masked(first, low_count)
    second, _ = masked(second, low_count)
    F, G, C, s1, s2 = block_sums(first, second, live)
    D = [a + jnp.where(row_zero, roll(b, -32, 1), zero) for a, b in zip(D, G)]
    S = [a - jnp.where(row_zero, roll(b, -32, 1), zero) for a, b in zip(S, s2)]

    for i in range(6):
        a, b = SYM[i]
        put(i, D[i] * unit + ((SQUARES[a] - SHIFT) * unit if a == b else 0.0))
        put(6 + i, S[i])
    for row in range(USED, ROWS):
        put(row, zero)


def from_above(value):
    return roll(value, -1, 0)


def from_below(value):
    return roll(value, 1, 0)


def pack_up_kernel(g_ref, up, rest, sems):
    copies = [
        pltpu.make_async_copy(g_ref.at[pl.ds(512, 128)], up.at[pl.ds(0, 128)], sems.at[0]),
        pltpu.make_async_copy(g_ref.at[pl.ds(768, 64)], up.at[pl.ds(128, 64)], sems.at[1]),
        pltpu.make_async_copy(g_ref.at[pl.ds(832, 192)], rest, sems.at[2]),
    ]
    for copy in copies:
        copy.start()
    for copy in copies:
        copy.wait()


def pack_rows_kernel(sizes, f_ref, g_ref, counts_ref, beside, odd, alive, sems):
    copies = [
        pltpu.make_async_copy(g_ref.at[pl.ds(256, 64)], beside.at[pl.ds(0, 64)], sems.at[0]),
        pltpu.make_async_copy(g_ref.at[pl.ds(384, 64)], beside.at[pl.ds(64, 64)], sems.at[1]),
        pltpu.make_async_copy(f_ref.at[pl.ds(320, 64)], odd.at[pl.ds(0, 64)], sems.at[2]),
        pltpu.make_async_copy(f_ref.at[pl.ds(448, 64)], odd.at[pl.ds(64, 64)], sems.at[3]),
    ]
    for copy in copies:
        copy.start()
    odd[128:136, :] = jnp.broadcast_to(counts_row(counts_ref, 1), (8, 128))
    for kind, row in enumerate(live_counts(counts_ref, sizes)):
        alive[kind : kind + 1, :] = row
    alive[4:8, :] = jnp.zeros((4, 128), jnp.float32)
    for copy in copies:
        copy.wait()


def merge_kernel(both, above, below, out):
    row_zero, _ = lane_bits((1, 128))
    for part in range(2):
        at = part * ROWS
        to = part * DOUBLE
        out[to : to + USED, :] = both[at : at + USED, :]
        a = above[at : at + USED, :]
        b = below[at : at + USED, :]
        out[to + AT_E : to + AT_E + USED, :] = jnp.where(row_zero, a, b)
        first = AT_C + 9
        for i in range(5):
            one, two = b[first + i : first + i + 1], b[first + min(5 + i, 8) : first + min(5 + i, 8) + 1]
            out[to + AT_E2 + i : to + AT_E2 + i + 1, :] = jnp.where(row_zero, one, roll(two, 32, 1))
        for i, source in enumerate(BEYOND):
            out[to + AT_E2 + 5 + i : to + AT_E2 + 6 + i, :] = jnp.where(
                row_zero, b[source : source + 1], a[source : source + 1]
            )


class Window:
    def __init__(self, load, n_dev):
        self.load = load
        self.bits = lane_bits((2 * n_dev, 128))

    def seconds(self, v, row_values):
        row_zero, sec_zero = self.bits
        half = roll(v, 64, 1)
        return [
            roll(v, -1, 1),
            row_values,
            jnp.where(sec_zero, half, from_above(half)),
            from_above(v),
        ]

    def row_pairs(self, v, e, e2):
        row_zero, _ = self.bits
        forth, back = roll(v, 32, 1), roll(v, -32, 1)
        own = jnp.where(row_zero, back, roll(e, 32, 1))
        side = jnp.where(row_zero, roll(e2, -32, 1), forth)
        return own, side

    def c(self, side, kind, i, j):
        return self.load(side * 42 + 6 + 9 * kind + 3 * i + j)

    def d(self, side, i, j):
        return self.load(side * 42 + sym_at(i, j))

    def c_e2(self, i, j):
        return self.load(84 + 3 * i + j)

    def transposed(self, c, a):
        return [c(0, j) * a[0] + c(1, j) * a[1] + c(2, j) * a[2] for j in range(3)]

    def apply(self, v, e, e2, sides):
        row_zero, sec_zero = self.bits
        outs = ([None] * 6, [None] * 6)
        for half in range(2):
            span = slice(3 * half, 3 * half + 3)
            sets = (v[span], e[span])
            beyond = e2[span]
            pairs = [self.row_pairs(*z) for z in zip(v[span], e[span], beyond)]
            t_row = [self.transposed(functools.partial(self.c, side, 1), sets[side]) for side in range(2)]
            for side in sides:
                a = sets[side]
                after = [self.seconds(a[j], pairs[j][side]) for j in range(3)]
                total = []
                for i in range(3):
                    y = sum(self.d(side, i, j) * a[j] for j in range(3))
                    for kind in range(4):
                        y = y - sum(self.c(side, kind, i, j) * after[j][kind] for j in range(3))
                    total.append(y)
                col = self.transposed(functools.partial(self.c, side, 0), a)
                one = self.transposed(functools.partial(self.c, side, 2), a)
                two = self.transposed(functools.partial(self.c, side, 3), a)
                if side == 1:
                    outer = self.transposed(self.c_e2, beyond)
                for j in range(3):
                    t = roll(one[j], 64, 1)
                    y = total[j] - roll(col[j], 1, 1) - jnp.where(sec_zero, from_below(t), t) - from_below(two[j])
                    if side == 0:
                        y = y - jnp.where(row_zero, roll(t_row[1][j], -32, 1), roll(t_row[0][j], 32, 1))
                    else:
                        y = y - jnp.where(row_zero, roll(t_row[0][j], -32, 1), roll(outer[j], 32, 1))
                    outs[side][3 * half + j] = y
        return outs


def window_kernel(got, blocks, v0, e0, v1, e1, v2):
    n_dev = got.shape[0] // (2 * DOUBLE)
    row_zero, sec_zero = lane_bits((2 * n_dev, 128))
    zero = jnp.zeros((2 * n_dev, 128), jnp.float32)

    def row(i):
        return jnp.concatenate(
            [got[pl.ds(slot * DOUBLE + i, n_dev, stride=2 * DOUBLE), :] for slot in range(2)], axis=0
        )

    def from_two(value, packed_second=False):
        if not packed_second:
            value = roll(value, 64, 1)
        return from_below(jnp.where(sec_zero, value, zero))

    def s_terms(three, two):
        return [
            from_below(row(three + i)) + from_two(row(two + i % 3), packed_second=i >= 3) for i in range(6)
        ]

    starts = []
    for side, at in enumerate((0, AT_E)):
        base = side * 42
        for i in range(36):
            blocks[base + 6 + i] = row(at + AT_C + i)
        two = [blocks[base + 24 + i] for i in (6, 7, 8)]
        three = [blocks[base + 33 + i] for i in (6, 7, 8)]
        pair, last = row(at + AT_TWO + 3), row(at + AT_TWO + 4)
        G_two = [from_two(z) for z in (pair, pair, two[0], last, two[1], two[2])]
        G_two[1] = from_two(pair, packed_second=True)
        G_three = [row(at + AT_THREE), row(at + AT_THREE + 1), three[0], row(at + AT_THREE + 2), three[1], three[2]]
        for i in range(6):
            blocks[base + i] = row(at + i) + G_two[i] + from_below(G_three[i])
        terms = s_terms(at + AT_THREE + 3, at + AT_TWO)
        starts.append([row(at + 6 + i) - terms[i] for i in range(6)])
    for i in range(5):
        packed = row(AT_E2 + i)
        blocks[84 + i] = packed
        if i < 4:
            blocks[89 + i] = roll(packed, -32, 1)
    terms = s_terms(AT_E2 + 11, AT_E2 + 17)
    outer = [row(AT_E2 + 5 + i) - terms[i] for i in range(6)]
    window = Window(lambda i: blocks[i], n_dev)
    v, e = starts
    w, f = window.apply(v, e, outer, (0, 1))
    last, _ = window.apply(w, f, f, (0,))
    for i in range(6):
        v0[i] = v[i]
        e0[i] = e[i]
        v1[i] = w[i]
        e1[i] = f[i]
        v2[i] = last[i]


def moments_kernel(blocks, v0, v1, v2, above, below, kept_hbm, e2, v3, e3, out, kept, sems):
    fetch = pltpu.make_async_copy(kept_hbm, kept, sems.at[0])
    fetch.start()
    shape = v2.shape[1:]
    n_dev = shape[0] // 2
    bits = lane_bits(shape)
    row_zero, _ = bits
    window = Window(lambda i: blocks[i], n_dev)
    v = [v2[i] for i in range(6)]
    side = [jnp.where(row_zero, above[i], below[i]) for i in range(6)]
    outer = [jnp.where(row_zero, below[i], above[i]) for i in range(6)]
    w, f = window.apply(v, side, outer, (0, 1))
    for i in range(6):
        e2[i] = side[i]
        v3[i] = w[i]
        e3[i] = f[i]
    vs = [[v0[i] for i in range(6)], [v1[i] for i in range(6)], v, w]

    def dot(left, right):
        return sum(a[:n_dev] * b[:n_dev] for a, b in zip(left, right))

    products = [dot(vs[n // 2], vs[n - n // 2]) for n in range(7)]
    energy = 0.0
    for half in range(2):
        a = w[3 * half : 3 * half + 3]
        b = f[3 * half : 3 * half + 3]
        after = [window.seconds(a[j], jnp.where(row_zero, roll(a[j], -32, 1), roll(b[j], 32, 1))) for j in range(3)]
        for i in range(3):
            inner = sum(window.d(0, i, j) * a[j] for j in range(3))
            for kind in range(4):
                inner = inner - 2.0 * sum(window.c(0, kind, i, j) * after[j][kind] for j in range(3))
            energy = energy + a[i][:n_dev] * inner[:n_dev]
    products.append(energy)
    lane = lax.broadcasted_iota(jnp.int32, (1, 128), 1)
    packed = jnp.zeros((1, 128), jnp.float32)
    for n, value in enumerate(products):
        value = jnp.sum(jnp.sum(value, axis=0, keepdims=True), axis=1, keepdims=True)
        packed = jnp.where(lane == n, value, packed)
    out[...] = packed
    fetch.wait()


def coefficients(moments):
    zero = jnp.zeros_like(moments[0])

    def inner(s, p, offset):
        total = zero
        for i, a in enumerate(s):
            for j, b in enumerate(p):
                total = total + a * b * moments[i + j + offset]
        return total

    def energy(p):
        return inner(p, p, 1) + HALF * inner(p, p, 0)

    s = [zero + 1.0]
    p = [zero + 1.0]
    x = [zero] * ITERS
    gamma = inner(s, s, 0)
    for sweep in range(ITERS):
        alpha = gamma / energy(p)
        x = [x[i] + (alpha * p[i] if i < len(p) else 0.0) for i in range(ITERS)]
        if sweep < ITERS - 1:
            image = [(p[i - 1] if i else 0.0) + (HALF * p[i] if i < len(p) else 0.0) for i in range(len(p) + 1)]
            s = [(s[i] if i < len(s) else 0.0) - alpha * image[i] for i in range(len(image))]
            gamma_new = inner(s, s, 0)
            beta = gamma_new / gamma
            p = [s[i] + (beta * p[i] if i < len(p) else 0.0) for i in range(len(s))]
            gamma = gamma_new
    return [value * (1.0 / SPAN) for value in x]


def finish_kernel(alive_ref, sums, v0, v1, v2, v3, n0, n1, n2, n3, kept, affines_hbm, residual_hbm, affines, residual, sems):
    stores = []
    total = jnp.sum(sums[...], axis=0, keepdims=True)
    lane = lax.broadcasted_iota(jnp.int32, (1, 128), 1)
    moments = [jnp.sum(jnp.where(lane == n, total, 0.0), axis=1, keepdims=True) for n in range(8)]
    weights = coefficients(moments)
    at = lax.axis_index("x") * lax.axis_size("core") + lax.axis_index("core")
    alive = [alive_ref[kind : kind + 1, :] for kind in range(4)]
    row_zero, sec_zero = lane_bits((1, 128))

    def mix(refs, i, dev):
        return sum(w * ref[i, pl.ds(dev, 1), :] for w, ref in zip(weights, refs))

    vs = (v0, v1, v2, v3)
    x = [mix(vs, i, at) for i in range(6)]
    above = [mix(vs, i, at + 1) for i in range(6)]
    beside = [mix((n0, n1, n2, n3), i, at) for i in range(6)]
    for i in range(6):
        for sec in range(2):
            for row in range(2):
                start = 64 * sec + 32 * row
                affines[i, sec, row : row + 1, :] = x[i][:, start : start + 32]
    stores.append(pltpu.make_async_copy(affines, affines_hbm, sems.at[4]))
    stores[-1].start()
    for kind in range(4):
        if kind == 0:
            b = [roll(z, -1, 1) for z in x]
        elif kind == 1:
            b = [jnp.where(row_zero, roll(z, -32, 1), roll(w, 32, 1)) for z, w in zip(x, beside)]
        elif kind == 2:
            b = [jnp.where(sec_zero, roll(z, 64, 1), roll(w, 64, 1)) for z, w in zip(x, above)]
        else:
            b = above
        u, v, p, q = (kept[4 * kind + i] for i in range(4))
        live = live_points(alive[kind])
        for comp in range(2):
            o = 3 * comp
            r = (p - u) if comp == 0 else (q - v)
            r = r - (x[o] * u + x[o + 1] * v) + (b[o] * p + b[o + 1] * q) - live * (x[o + 2] - b[o + 2])
            residual[pl.ds(kind * 256 + comp, 128, stride=2), :] = r.T
        part = pl.ds(kind * 256, 256)
        stores.append(pltpu.make_async_copy(residual.at[part], residual_hbm.at[part], sems.at[kind]))
        stores[-1].start()
    for store in stores:
        store.wait()


def shape_of(*shape):
    return jax.ShapeDtypeStruct(shape, jnp.float32)


def call(interpret, kernel, outs, *args, scalars=0, anywhere=(), copies=0, buffers=(), results=None):
    spaces = []
    args = list(args)
    shapes = [shape_of(*out) for out in outs]
    for n, arg in enumerate(args):
        if n < scalars:
            spaces.append(pl.BlockSpec(memory_space=pltpu.SMEM))
        elif n in anywhere:
            spaces.append(pl.BlockSpec(memory_space=pl.ANY))
        else:
            spaces.append(pl.BlockSpec(memory_space=pltpu.VMEM))
            if arg.dtype == jnp.float32 and not interpret:
                args[n] = pltpu.with_memory_space_constraint(arg, pltpu.VMEM)
    if not results and not interpret:
        shapes = [pltpu.VMEM(out, jnp.float32) for out in outs]
    results = results or [pltpu.VMEM] * len(outs)
    return pl.pallas_call(
        kernel,
        out_shape=shapes,
        in_specs=spaces,
        out_specs=[pl.BlockSpec(memory_space=space) for space in results],
        scratch_shapes=[pltpu.VMEM(b, jnp.float32) for b in buffers]
        + ([pltpu.SemaphoreType.DMA((copies,))] if copies else []),
        interpret=interpret,
    )(*args)


def shifted(value, axes, steps):
    count = lax.axis_size(axes)
    pairs = [(i, i + steps) for i in range(count) if 0 <= i + steps < count]
    return lax.ppermute(value, axes, pairs)


def pack_up(run, g):
    return run(pack_up_kernel, [(192, 128), (192, 128)], g, anywhere=(0,), copies=3)


def pack_rows(run, f, g, counts, sizes):
    kernel = functools.partial(pack_rows_kernel, sizes)
    return run(kernel, [(128, 128), (136, 128), (8, 128)], f, g, counts, anywhere=(0, 1), copies=4)


def per_device(interpret, first_pts, second_pts, counts):
    run = functools.partial(call, interpret)
    n_sec = lax.axis_size(SEC_AXES)
    n_dev = lax.axis_size(GROUP)
    n_group = n_sec // n_dev
    f = first_pts.reshape(1024, 128)
    g = second_pts.reshape(1024, 128)
    up, rest = pack_up(run, g)
    up = shifted(up, SEC_AXES, -1)
    relay = n_dev - 2
    inside = [(i + 1, i) for i in range(n_sec - 1) if (i + 1) % n_dev]
    to_relay = [(group * n_dev, group * n_dev + relay) for group in range(1, n_group)]
    from_relay = [(group * n_dev + relay, group * n_dev - 1) for group in range(1, n_group)]
    relayed = lax.ppermute(rest, SEC_AXES, to_relay)
    relayed, f_later, g_later = lax.optimization_barrier((relayed, f, g))
    outside = lax.ppermute(relayed, SEC_AXES, from_relay)
    sizes = (n_sec, lax.axis_size("row"))
    beside, odd, alive, rest = lax.optimization_barrier((*pack_rows(run, f_later, g_later, counts, sizes), rest))
    beside = shifted(beside, "row", -1)
    low = shifted(odd, "row", 1)
    rest = lax.ppermute(rest, SEC_AXES, inside)
    packet, kept = run(gram_kernel, [(ROWS, 128), (16, 128, 128)], f, g, alive, up, rest, outside, beside, low)

    half = n_dev // 2
    pairs = []
    for group in range(n_group):
        for dev in range(n_dev):
            source = group + (1 if dev < half else -1)
            if 0 <= source < n_group:
                pairs.append((source * n_dev + dev, group * n_dev + dev))
    other = lax.ppermute(packet, SEC_AXES, pairs)
    both = jnp.concatenate([packet, other], axis=0)
    (mine,) = run(merge_kernel, [(2 * DOUBLE, 128)], both, shifted(both, "row", -1), shifted(both, "row", 1))
    got = lax.all_to_all(jnp.broadcast_to(mine[None], (n_dev, 2 * DOUBLE, 128)), GROUP, 0, 0, tiled=False)
    wide = (6, 2 * n_dev, 128)
    blocks, v0, e0, v1, e1, v2 = run(
        window_kernel, [(93, 2 * n_dev, 128)] + [wide] * 5, got.reshape(n_dev * 2 * DOUBLE, 128)
    )
    e2, v3, e3, part, kept = run(
        moments_kernel,
        [wide, wide, wide, (1, 128), (16, 128, 128)],
        blocks,
        v0,
        v1,
        v2,
        shifted(v2, "row", -1),
        shifted(v2, "row", 1),
        kept,
        anywhere=(6,),
        copies=1,
    )
    n_other = lax.axis_size(OTHERS)
    groups = sum_groups([lax.axis_size(axis) for axis in EVERY])
    sums = lax.all_to_all(
        jnp.broadcast_to(part[None], (n_other, 1, 128)), EVERY, 0, 0, axis_index_groups=groups, tiled=False
    )
    affines, residual = run(
        finish_kernel,
        [(6,) + counts.shape[1:], (1024, 128)],
        alive,
        sums.reshape(n_other, 128),
        v0,
        v1,
        v2,
        v3,
        e0,
        e1,
        e2,
        e3,
        kept,
        copies=5,
        buffers=[(6,) + counts.shape[1:], (1024, 128)],
        results=[pl.ANY, pl.ANY],
    )
    return affines, residual.reshape(first_pts.shape)


def sum_groups(sizes):
    n_y, n_zhi, n_x, n_core, n_row = sizes
    n_z = n_zhi * n_row
    first = 5 * n_z // 8
    groups = []
    for place in range(n_x * n_core):
        order = [((first + step) % n_z, y) for step in range(n_z) for y in reversed(range(n_y))]
        groups.append([((y * n_zhi + z // n_row) * n_x * n_core + place) * n_row + z % n_row for z, y in order])
    return groups


def split_mesh(mesh):
    n_row = mesh.shape["row"]
    return Mesh(mesh.devices.reshape(4, 4, 4, 2, n_row), SEC_AXES + ("row",))


def solution(mesh, inner=None, interpret=False):
    inner = inner or split_mesh(mesh)
    in_specs = (
        P(None, SEC_AXES, "row", None, None, None),
        P(None, SEC_AXES, "row", None, None, None),
        P(None, SEC_AXES, "row", None),
    )
    out_specs = (P(None, SEC_AXES, "row", None), P(None, SEC_AXES, "row", None, None, None))
    return jax.shard_map(
        functools.partial(per_device, interpret), mesh=inner, in_specs=in_specs, out_specs=out_specs, check_vma=False
    )
```

```python
import functools

import jax
import jax.numpy as jnp
from jax import lax
from jax.experimental import pallas as pl
from jax.experimental.pallas import tpu as pltpu
from jax.sharding import Mesh
from jax.sharding import PartitionSpec as P

ITERS = 4
SPAN = 1024.0
SHIFT = 512.0
HALF = SHIFT / SPAN
SQUARES = (0.49, 0.49, 0.09)
SYM = ((0, 0), (0, 1), (0, 2), (1, 1), (1, 2), (2, 2))
SEC_AXES = ("y", "zhi", "x", "core")
GROUP = ("x", "core")
OTHERS = ("y", "zhi", "row")
EVERY = SEC_AXES + ("row",)

ROWS = 64
AT_C = 12
AT_THREE = 48
AT_TWO = 57
USED = 62
AT_E = 62
AT_E2 = 124
DOUBLE = 144
BEYOND = [6 + i for i in range(6)] + [AT_THREE + 3 + i for i in range(6)] + [AT_TWO + i for i in range(3)]


def sym_at(a, b):
    return SYM.index((min(a, b), max(a, b)))


def roll(value, shift, axis):
    size = value.shape[axis]
    return pltpu.roll(value, shift % size, axis)


def lane_bits(shape):
    lane = lax.broadcasted_iota(jnp.int32, shape, len(shape) - 1)
    return (lane // 32) % 2 == 0, lane < 64


def counts_row(ref, kind):
    cells = [ref[kind, sec, row : row + 1, :] for sec in range(2) for row in range(2)]
    return jnp.concatenate(cells, axis=1).astype(jnp.float32)


def live_counts(counts_ref, sizes):
    n_sec, n_row = sizes
    row_zero, sec_zero = lane_bits((1, 128))
    lane = lax.broadcasted_iota(jnp.int32, (1, 128), 1)
    section = 0
    for axis in SEC_AXES:
        section = section * lax.axis_size(axis) + lax.axis_index(axis)
    last_row = lax.axis_index("row") == n_row - 1
    last_sec = section == n_sec - 1
    zero = jnp.zeros((1, 128), jnp.float32)
    counts = [counts_row(counts_ref, kind) for kind in range(4)]
    return [
        jnp.where(lane % 32 == 31, zero, counts[0]),
        jnp.where(jnp.logical_and(jnp.logical_not(row_zero), last_row), zero, counts[1]),
        jnp.where(jnp.logical_and(jnp.logical_not(sec_zero), last_sec), zero, counts[2]),
        jnp.where(last_sec, zero, counts[3]),
    ]


def live_points(count):
    point = lax.broadcasted_iota(jnp.int32, (128, 128), 0).astype(jnp.float32)
    return jnp.where(point < count, 1.0, 0.0)


def block_sums(first, second, live):
    u, v = first
    p, q = second
    dx = p - u
    dy = q - v

    def red(z):
        return jnp.sum(z, axis=0, keepdims=True)

    su, sv, sp, sq, n = red(u), red(v), red(p), red(q), red(live)
    F = [red(u * u), red(u * v), su, red(v * v), sv, n]
    G = [red(p * p), red(p * q), sp, red(q * q), sq, n]
    C = [red(u * p), red(u * q), su, red(v * p), red(v * q), sv, sp, sq, n]
    tx, ty = red(dx), red(dy)
    s1 = [red(dx * u), red(dx * v), tx, red(dy * u), red(dy * v), ty]
    s2 = [red(dx * p), red(dx * q), tx, red(dy * p), red(dy * q), ty]
    return F, G, C, s1, s2


def gram_kernel(f_ref, g_ref, alive_ref, up_ref, rest_ref, outside_ref, next_ref, low_ref, packet, kept):
    row_zero, sec_zero = lane_bits((1, 128))

    def pair_rows(ref, start, count, comp):
        return ref[pl.ds(2 * start + comp, count, stride=2), :]

    def own(ref, kind):
        return [pair_rows(ref, kind * 128, 128, comp).T for comp in range(2)]

    zero = jnp.zeros((1, 128), jnp.float32)
    alive = [alive_ref[kind : kind + 1, :] for kind in range(4)]

    def masked(points, count):
        live = live_points(count)
        return [z * live for z in points], live

    def second_of(kind):
        if kind == 0:
            return [roll(z, -1, 1) for z in own(g_ref, 0)]
        out = []
        for comp in range(2):
            if kind == 1:
                parts = [
                    pair_rows(g_ref, 128 + 32, 32, comp),
                    pair_rows(next_ref, 0, 32, comp),
                    pair_rows(g_ref, 128 + 96, 32, comp),
                    pair_rows(next_ref, 32, 32, comp),
                ]
            elif kind == 2:
                parts = [pair_rows(g_ref, 256 + 64, 64, comp), pair_rows(up_ref, 0, 64, comp)]
            else:
                rest = pair_rows(rest_ref, 0, 96, comp) + pair_rows(outside_ref, 0, 96, comp)
                parts = [pair_rows(up_ref, 64, 32, comp), rest]
            out.append(jnp.concatenate(parts, axis=0).T)
        return out

    D = [zero] * 6
    S = [zero] * 6
    unit = 1.0 / SPAN

    def put(row, value):
        packet[row : row + 1, :] = value

    for kind in range(4):
        first, live = masked(own(f_ref, kind), alive[kind])
        second, _ = masked(second_of(kind), alive[kind])
        for i, points in enumerate(first + second):
            kept[4 * kind + i] = points
        F, G, C, s1, s2 = block_sums(first, second, live)
        D = [a + b for a, b in zip(D, F)]
        S = [a + b for a, b in zip(S, s1)]
        for i in range(9):
            put(AT_C + 9 * kind + i, C[i] * unit)
        if kind == 0:
            D = [a + roll(b, 1, 1) for a, b in zip(D, G)]
            S = [a - roll(b, 1, 1) for a, b in zip(S, s2)]
        elif kind == 1:
            D = [a + jnp.where(row_zero, zero, roll(b, 32, 1)) for a, b in zip(D, G)]
            S = [a - jnp.where(row_zero, zero, roll(b, 32, 1)) for a, b in zip(S, s2)]
        elif kind == 2:
            D = [a + jnp.where(sec_zero, zero, roll(b, 64, 1)) for a, b in zip(D, G)]
            S = [a - jnp.where(sec_zero, zero, roll(b, 64, 1)) for a, b in zip(S, s2)]
            for i in range(3):
                put(AT_TWO + i, jnp.where(sec_zero, roll(s2[3 + i], 64, 1), s2[i]))
            put(AT_TWO + 3, jnp.where(sec_zero, roll(G[1], 64, 1), G[0]) * unit)
            put(AT_TWO + 4, G[3] * unit)
        else:
            put(AT_THREE, G[0] * unit)
            put(AT_THREE + 1, G[1] * unit)
            put(AT_THREE + 2, G[3] * unit)
            for i in range(6):
                put(AT_THREE + 3 + i, s2[i])

    low_count = jnp.where(row_zero, zero, low_ref[128:129, :])
    first = []
    second = []
    for comp in range(2):
        low = [pair_rows(low_ref, 32 * sec, 32, comp) for sec in range(2)]
        first.append(jnp.concatenate([low[0], low[0], low[1], low[1]], axis=0).T)
        mine = [pair_rows(g_ref, 128 + 64 * sec, 32, comp) for sec in range(2)]
        second.append(jnp.concatenate([mine[0], mine[0], mine[1], mine[1]], axis=0).T)
    first, live = masked(first, low_count)
    second, _ = masked(second, low_count)
    F, G, C, s1, s2 = block_sums(first, second, live)
    D = [a + jnp.where(row_zero, roll(b, -32, 1), zero) for a, b in zip(D, G)]
    S = [a - jnp.where(row_zero, roll(b, -32, 1), zero) for a, b in zip(S, s2)]

    for i in range(6):
        a, b = SYM[i]
        put(i, D[i] * unit + ((SQUARES[a] - SHIFT) * unit if a == b else 0.0))
        put(6 + i, S[i])
    for row in range(USED, ROWS):
        put(row, zero)


def from_above(value):
    return roll(value, -1, 0)


def from_below(value):
    return roll(value, 1, 0)


def pack_up_kernel(g_ref, up, rest, sems):
    copies = [
        pltpu.make_async_copy(g_ref.at[pl.ds(512, 128)], up.at[pl.ds(0, 128)], sems.at[0]),
        pltpu.make_async_copy(g_ref.at[pl.ds(768, 64)], up.at[pl.ds(128, 64)], sems.at[1]),
        pltpu.make_async_copy(g_ref.at[pl.ds(832, 192)], rest, sems.at[2]),
    ]
    for copy in copies:
        copy.start()
    for copy in copies:
        copy.wait()


def pack_rows_kernel(sizes, f_ref, g_ref, counts_hbm, beside, odd, alive, counts_ref, sems):
    copies = [
        pltpu.make_async_copy(g_ref.at[pl.ds(256, 64)], beside.at[pl.ds(0, 64)], sems.at[0]),
        pltpu.make_async_copy(g_ref.at[pl.ds(384, 64)], beside.at[pl.ds(64, 64)], sems.at[1]),
        pltpu.make_async_copy(f_ref.at[pl.ds(320, 64)], odd.at[pl.ds(0, 64)], sems.at[2]),
        pltpu.make_async_copy(f_ref.at[pl.ds(448, 64)], odd.at[pl.ds(64, 64)], sems.at[3]),
    ]
    fetch = pltpu.make_async_copy(counts_hbm, counts_ref, sems.at[4])
    fetch.start()
    for copy in copies:
        copy.start()
    fetch.wait()
    for kind, row in enumerate(live_counts(counts_ref, sizes)):
        alive[kind : kind + 1, :] = row
    alive[4:8, :] = jnp.zeros((4, 128), jnp.float32)
    odd[128:136, :] = jnp.broadcast_to(counts_row(counts_ref, 1), (8, 128))
    for copy in copies:
        copy.wait()


def merge_kernel(both, above, below, out):
    row_zero, _ = lane_bits((1, 128))
    for part in range(2):
        at = part * ROWS
        to = part * DOUBLE
        out[to : to + USED, :] = both[at : at + USED, :]
        a = above[at : at + USED, :]
        b = below[at : at + USED, :]
        out[to + AT_E : to + AT_E + USED, :] = jnp.where(row_zero, a, b)
        first = AT_C + 9
        for i in range(5):
            one, two = b[first + i : first + i + 1], b[first + min(5 + i, 8) : first + min(5 + i, 8) + 1]
            out[to + AT_E2 + i : to + AT_E2 + i + 1, :] = jnp.where(row_zero, one, roll(two, 32, 1))
        for i, source in enumerate(BEYOND):
            out[to + AT_E2 + 5 + i : to + AT_E2 + 6 + i, :] = jnp.where(
                row_zero, b[source : source + 1], a[source : source + 1]
            )


class Window:
    def __init__(self, load, n_dev):
        self.load = load
        self.bits = lane_bits((2 * n_dev, 128))

    def seconds(self, v, row_values):
        row_zero, sec_zero = self.bits
        half = roll(v, 64, 1)
        return [
            roll(v, -1, 1),
            row_values,
            jnp.where(sec_zero, half, from_above(half)),
            from_above(v),
        ]

    def row_pairs(self, v, e, e2):
        row_zero, _ = self.bits
        forth, back = roll(v, 32, 1), roll(v, -32, 1)
        own = jnp.where(row_zero, back, roll(e, 32, 1))
        side = jnp.where(row_zero, roll(e2, -32, 1), forth)
        return own, side

    def c(self, side, kind, i, j):
        return self.load(side * 42 + 6 + 9 * kind + 3 * i + j)

    def d(self, side, i, j):
        return self.load(side * 42 + sym_at(i, j))

    def c_e2(self, i, j):
        return self.load(84 + 3 * i + j)

    def transposed(self, c, a):
        return [c(0, j) * a[0] + c(1, j) * a[1] + c(2, j) * a[2] for j in range(3)]

    def apply(self, v, e, e2, sides):
        row_zero, sec_zero = self.bits
        outs = ([None] * 6, [None] * 6)
        for half in range(2):
            span = slice(3 * half, 3 * half + 3)
            sets = (v[span], e[span])
            beyond = e2[span]
            pairs = [self.row_pairs(*z) for z in zip(v[span], e[span], beyond)]
            t_row = [self.transposed(functools.partial(self.c, side, 1), sets[side]) for side in range(2)]
            for side in sides:
                a = sets[side]
                after = [self.seconds(a[j], pairs[j][side]) for j in range(3)]
                total = []
                for i in range(3):
                    y = sum(self.d(side, i, j) * a[j] for j in range(3))
                    for kind in range(4):
                        y = y - sum(self.c(side, kind, i, j) * after[j][kind] for j in range(3))
                    total.append(y)
                col = self.transposed(functools.partial(self.c, side, 0), a)
                one = self.transposed(functools.partial(self.c, side, 2), a)
                two = self.transposed(functools.partial(self.c, side, 3), a)
                if side == 1:
                    outer = self.transposed(self.c_e2, beyond)
                for j in range(3):
                    t = roll(one[j], 64, 1)
                    y = total[j] - roll(col[j], 1, 1) - jnp.where(sec_zero, from_below(t), t) - from_below(two[j])
                    if side == 0:
                        y = y - jnp.where(row_zero, roll(t_row[1][j], -32, 1), roll(t_row[0][j], 32, 1))
                    else:
                        y = y - jnp.where(row_zero, roll(t_row[0][j], -32, 1), roll(outer[j], 32, 1))
                    outs[side][3 * half + j] = y
        return outs


def window_kernel(got, kept_hbm, blocks, v0, e0, v1, e1, v2, kept, sems):
    fetch = pltpu.make_async_copy(kept_hbm, kept, sems.at[0])
    fetch.start()
    n_dev = got.shape[0] // (2 * DOUBLE)
    row_zero, sec_zero = lane_bits((2 * n_dev, 128))
    zero = jnp.zeros((2 * n_dev, 128), jnp.float32)

    def row(i):
        return jnp.concatenate(
            [got[pl.ds(slot * DOUBLE + i, n_dev, stride=2 * DOUBLE), :] for slot in range(2)], axis=0
        )

    def from_two(value, packed_second=False):
        if not packed_second:
            value = roll(value, 64, 1)
        return from_below(jnp.where(sec_zero, value, zero))

    def s_terms(three, two):
        return [
            from_below(row(three + i)) + from_two(row(two + i % 3), packed_second=i >= 3) for i in range(6)
        ]

    starts = []
    for side, at in enumerate((0, AT_E)):
        base = side * 42
        for i in range(36):
            blocks[base + 6 + i] = row(at + AT_C + i)
        two = [blocks[base + 24 + i] for i in (6, 7, 8)]
        three = [blocks[base + 33 + i] for i in (6, 7, 8)]
        pair, last = row(at + AT_TWO + 3), row(at + AT_TWO + 4)
        G_two = [from_two(z) for z in (pair, pair, two[0], last, two[1], two[2])]
        G_two[1] = from_two(pair, packed_second=True)
        G_three = [row(at + AT_THREE), row(at + AT_THREE + 1), three[0], row(at + AT_THREE + 2), three[1], three[2]]
        for i in range(6):
            blocks[base + i] = row(at + i) + G_two[i] + from_below(G_three[i])
        terms = s_terms(at + AT_THREE + 3, at + AT_TWO)
        starts.append([row(at + 6 + i) - terms[i] for i in range(6)])
    for i in range(5):
        packed = row(AT_E2 + i)
        blocks[84 + i] = packed
        if i < 4:
            blocks[89 + i] = roll(packed, -32, 1)
    terms = s_terms(AT_E2 + 11, AT_E2 + 17)
    outer = [row(AT_E2 + 5 + i) - terms[i] for i in range(6)]
    window = Window(lambda i: blocks[i], n_dev)
    v, e = starts
    w, f = window.apply(v, e, outer, (0, 1))
    last, _ = window.apply(w, f, f, (0,))
    for i in range(6):
        v0[i] = v[i]
        e0[i] = e[i]
        v1[i] = w[i]
        e1[i] = f[i]
        v2[i] = last[i]
    fetch.wait()


def moments_kernel(blocks, v0, v1, v2, above, below, e2, v3, e3, out):
    shape = v2.shape[1:]
    n_dev = shape[0] // 2
    bits = lane_bits(shape)
    row_zero, _ = bits
    window = Window(lambda i: blocks[i], n_dev)
    v = [v2[i] for i in range(6)]
    side = [jnp.where(row_zero, above[i], below[i]) for i in range(6)]
    outer = [jnp.where(row_zero, below[i], above[i]) for i in range(6)]
    w, f = window.apply(v, side, outer, (0, 1))
    for i in range(6):
        e2[i] = side[i]
        v3[i] = w[i]
        e3[i] = f[i]
    vs = [[v0[i] for i in range(6)], [v1[i] for i in range(6)], v, w]

    def dot(left, right):
        return sum(a[:n_dev] * b[:n_dev] for a, b in zip(left, right))

    products = [dot(vs[n // 2], vs[n - n // 2]) for n in range(7)]
    energy = 0.0
    for half in range(2):
        a = w[3 * half : 3 * half + 3]
        b = f[3 * half : 3 * half + 3]
        after = [window.seconds(a[j], jnp.where(row_zero, roll(a[j], -32, 1), roll(b[j], 32, 1))) for j in range(3)]
        for i in range(3):
            inner = sum(window.d(0, i, j) * a[j] for j in range(3))
            for kind in range(4):
                inner = inner - 2.0 * sum(window.c(0, kind, i, j) * after[j][kind] for j in range(3))
            energy = energy + a[i][:n_dev] * inner[:n_dev]
    products.append(energy)
    lane = lax.broadcasted_iota(jnp.int32, (1, 128), 1)
    packed = jnp.zeros((1, 128), jnp.float32)
    for n, value in enumerate(products):
        value = jnp.sum(jnp.sum(value, axis=0, keepdims=True), axis=1, keepdims=True)
        packed = jnp.where(lane == n, value, packed)
    out[...] = packed


def coefficients(moments):
    zero = jnp.zeros_like(moments[0])

    def inner(s, p, offset):
        total = zero
        for i, a in enumerate(s):
            for j, b in enumerate(p):
                total = total + a * b * moments[i + j + offset]
        return total

    def energy(p):
        return inner(p, p, 1) + HALF * inner(p, p, 0)

    s = [zero + 1.0]
    p = [zero + 1.0]
    x = [zero] * ITERS
    gamma = inner(s, s, 0)
    for sweep in range(ITERS):
        alpha = gamma / energy(p)
        x = [x[i] + (alpha * p[i] if i < len(p) else 0.0) for i in range(ITERS)]
        if sweep < ITERS - 1:
            image = [(p[i - 1] if i else 0.0) + (HALF * p[i] if i < len(p) else 0.0) for i in range(len(p) + 1)]
            s = [(s[i] if i < len(s) else 0.0) - alpha * image[i] for i in range(len(image))]
            gamma_new = inner(s, s, 0)
            beta = gamma_new / gamma
            p = [s[i] + (beta * p[i] if i < len(p) else 0.0) for i in range(len(s))]
            gamma = gamma_new
    return [value * (1.0 / SPAN) for value in x]


def finish_kernel(alive_ref, sums, v0, v1, v2, v3, n0, n1, n2, n3, kept, affines_hbm, residual_hbm, affines, residual, sems):
    stores = []
    total = jnp.sum(sums[...], axis=0, keepdims=True)
    lane = lax.broadcasted_iota(jnp.int32, (1, 128), 1)
    moments = [jnp.sum(jnp.where(lane == n, total, 0.0), axis=1, keepdims=True) for n in range(8)]
    weights = coefficients(moments)
    at = lax.axis_index("x") * lax.axis_size("core") + lax.axis_index("core")
    alive = [alive_ref[kind : kind + 1, :] for kind in range(4)]
    row_zero, sec_zero = lane_bits((1, 128))

    def mix(refs, i, dev):
        return sum(w * ref[i, pl.ds(dev, 1), :] for w, ref in zip(weights, refs))

    vs = (v0, v1, v2, v3)
    x = [mix(vs, i, at) for i in range(6)]
    above = [mix(vs, i, at + 1) for i in range(6)]
    beside = [mix((n0, n1, n2, n3), i, at) for i in range(6)]
    for i in range(6):
        for sec in range(2):
            for row in range(2):
                start = 64 * sec + 32 * row
                affines[i, sec, row : row + 1, :] = x[i][:, start : start + 32]
    stores.append(pltpu.make_async_copy(affines, affines_hbm, sems.at[4]))
    stores[-1].start()
    for kind in range(4):
        if kind == 0:
            b = [roll(z, -1, 1) for z in x]
        elif kind == 1:
            b = [jnp.where(row_zero, roll(z, -32, 1), roll(w, 32, 1)) for z, w in zip(x, beside)]
        elif kind == 2:
            b = [jnp.where(sec_zero, roll(z, 64, 1), roll(w, 64, 1)) for z, w in zip(x, above)]
        else:
            b = above
        u, v, p, q = (kept[4 * kind + i] for i in range(4))
        live = live_points(alive[kind])
        for comp in range(2):
            o = 3 * comp
            r = (p - u) if comp == 0 else (q - v)
            r = r - (x[o] * u + x[o + 1] * v) + (b[o] * p + b[o + 1] * q) - live * (x[o + 2] - b[o + 2])
            residual[pl.ds(kind * 256 + comp, 128, stride=2), :] = r.T
        part = pl.ds(kind * 256, 256)
        stores.append(pltpu.make_async_copy(residual.at[part], residual_hbm.at[part], sems.at[kind]))
        stores[-1].start()
    for store in stores:
        store.wait()


def shape_of(*shape):
    return jax.ShapeDtypeStruct(shape, jnp.float32)


def call(interpret, kernel, outs, *args, scalars=0, anywhere=(), copies=0, buffers=(), results=None):
    spaces = []
    args = list(args)
    shapes = [shape_of(*out) for out in outs]
    for n, arg in enumerate(args):
        if n < scalars:
            spaces.append(pl.BlockSpec(memory_space=pltpu.SMEM))
        elif n in anywhere:
            spaces.append(pl.BlockSpec(memory_space=pl.ANY))
        else:
            spaces.append(pl.BlockSpec(memory_space=pltpu.VMEM))
            if arg.dtype == jnp.float32 and not interpret:
                args[n] = pltpu.with_memory_space_constraint(arg, pltpu.VMEM)
    if not results and not interpret:
        shapes = [pltpu.VMEM(out, jnp.float32) for out in outs]
    results = results or [pltpu.VMEM] * len(outs)
    return pl.pallas_call(
        kernel,
        out_shape=shapes,
        in_specs=spaces,
        out_specs=[pl.BlockSpec(memory_space=space) for space in results],
        scratch_shapes=list(buffers)
        + ([pltpu.SemaphoreType.DMA((copies,))] if copies else []),
        interpret=interpret,
    )(*args)


def shifted(value, axes, steps):
    count = lax.axis_size(axes)
    pairs = [(i, i + steps) for i in range(count) if 0 <= i + steps < count]
    return lax.ppermute(value, axes, pairs)


def pack_up(run, g):
    return run(pack_up_kernel, [(192, 128), (192, 128)], g, anywhere=(0,), copies=3)


def pack_rows(run, f, g, counts, sizes):
    return run(
        functools.partial(pack_rows_kernel, sizes),
        [(128, 128), (136, 128), (8, 128)],
        f,
        g,
        counts,
        anywhere=(0, 1, 2),
        copies=5,
        buffers=[pltpu.VMEM(counts.shape, jnp.int32)],
    )


def per_device(interpret, first_pts, second_pts, counts):
    run = functools.partial(call, interpret)
    n_sec = lax.axis_size(SEC_AXES)
    n_dev = lax.axis_size(GROUP)
    n_group = n_sec // n_dev
    f = first_pts.reshape(1024, 128)
    g = second_pts.reshape(1024, 128)
    up, rest = pack_up(run, g)
    up = shifted(up, SEC_AXES, -1)
    relay = n_dev - 2
    inside = [(i + 1, i) for i in range(n_sec - 1) if (i + 1) % n_dev]
    to_relay = [(group * n_dev, group * n_dev + relay) for group in range(1, n_group)]
    from_relay = [(group * n_dev + relay, group * n_dev - 1) for group in range(1, n_group)]
    relayed = lax.ppermute(rest, SEC_AXES, to_relay)
    relayed, f_later, g_later = lax.optimization_barrier((relayed, f, g))
    outside = lax.ppermute(relayed, SEC_AXES, from_relay)
    sizes = (n_sec, lax.axis_size("row"))
    beside, odd, alive, rest = lax.optimization_barrier((*pack_rows(run, f_later, g_later, counts, sizes), rest))
    beside = shifted(beside, "row", -1)
    low = shifted(odd, "row", 1)
    rest = lax.ppermute(rest, SEC_AXES, inside)
    packet, kept = run(gram_kernel, [(ROWS, 128), (16, 128, 128)], f, g, alive, up, rest, outside, beside, low)

    half = n_dev // 2
    pairs = []
    for group in range(n_group):
        for dev in range(n_dev):
            source = group + (1 if dev < half else -1)
            if 0 <= source < n_group:
                pairs.append((source * n_dev + dev, group * n_dev + dev))
    other = lax.ppermute(packet, SEC_AXES, pairs)
    both = jnp.concatenate([packet, other], axis=0)
    (mine,) = run(merge_kernel, [(2 * DOUBLE, 128)], both, shifted(both, "row", -1), shifted(both, "row", 1))
    got = lax.all_to_all(jnp.broadcast_to(mine[None], (n_dev, 2 * DOUBLE, 128)), GROUP, 0, 0, tiled=False)
    wide = (6, 2 * n_dev, 128)
    blocks, v0, e0, v1, e1, v2, kept = run(
        window_kernel,
        [(93, 2 * n_dev, 128)] + [wide] * 5 + [(16, 128, 128)],
        got.reshape(n_dev * 2 * DOUBLE, 128),
        kept,
        anywhere=(1,),
        copies=1,
    )
    e2, v3, e3, part = run(
        moments_kernel,
        [wide, wide, wide, (1, 128)],
        blocks,
        v0,
        v1,
        v2,
        shifted(v2, "row", -1),
        shifted(v2, "row", 1),
    )
    n_other = lax.axis_size(OTHERS)
    groups = sum_groups([lax.axis_size(axis) for axis in EVERY])
    sums = lax.all_to_all(
        jnp.broadcast_to(part[None], (n_other, 1, 128)), EVERY, 0, 0, axis_index_groups=groups, tiled=False
    )
    affines, residual = run(
        finish_kernel,
        [(6,) + counts.shape[1:], (1024, 128)],
        alive,
        sums.reshape(n_other, 128),
        v0,
        v1,
        v2,
        v3,
        e0,
        e1,
        e2,
        e3,
        kept,
        copies=5,
        buffers=[pltpu.VMEM((6,) + counts.shape[1:], jnp.float32), pltpu.VMEM((1024, 128), jnp.float32)],
        results=[pl.ANY, pl.ANY],
    )
    return affines, residual.reshape(first_pts.shape)


def sum_groups(sizes):
    n_y, n_zhi, n_x, n_core, n_row = sizes
    n_z = n_zhi * n_row
    first = 5 * n_z // 8
    groups = []
    for place in range(n_x * n_core):
        order = [((first + step) % n_z, y) for step in range(n_z) for y in reversed(range(n_y))]
        groups.append([((y * n_zhi + z // n_row) * n_x * n_core + place) * n_row + z % n_row for z, y in order])
    return groups


def split_mesh(mesh):
    n_row = mesh.shape["row"]
    return Mesh(mesh.devices.reshape(4, 4, 4, 2, n_row), SEC_AXES + ("row",))


def solution(mesh, inner=None, interpret=False):
    inner = inner or split_mesh(mesh)
    in_specs = (
        P(None, SEC_AXES, "row", None, None, None),
        P(None, SEC_AXES, "row", None, None, None),
        P(None, SEC_AXES, "row", None),
    )
    out_specs = (P(None, SEC_AXES, "row", None), P(None, SEC_AXES, "row", None, None, None))
    return jax.shard_map(
        functools.partial(per_device, interpret), mesh=inner, in_specs=in_specs, out_specs=out_specs, check_vma=False
    )
```

```python
import functools

import jax
import jax.numpy as jnp
from jax import lax
from jax.experimental import pallas as pl
from jax.experimental.pallas import tpu as pltpu
from jax.sharding import Mesh
from jax.sharding import PartitionSpec as P

ITERS = 4
SPAN = 1024.0
SHIFT = 512.0
HALF = SHIFT / SPAN
SQUARES = (0.49, 0.49, 0.09)
SYM = ((0, 0), (0, 1), (0, 2), (1, 1), (1, 2), (2, 2))
SEC_AXES = ("y", "zhi", "x", "core")
GROUP = ("x", "core")
OTHERS = ("y", "zhi", "row")
EVERY = SEC_AXES + ("row",)

ROWS = 64
AT_C = 12
AT_THREE = 48
AT_TWO = 57
USED = 62
AT_E = 62
AT_E2 = 124
DOUBLE = 144
BEYOND = [6 + i for i in range(6)] + [AT_THREE + 3 + i for i in range(6)] + [AT_TWO + i for i in range(3)]


def sym_at(a, b):
    return SYM.index((min(a, b), max(a, b)))


def roll(value, shift, axis):
    size = value.shape[axis]
    return pltpu.roll(value, shift % size, axis)


def lane_bits(shape):
    lane = lax.broadcasted_iota(jnp.int32, shape, len(shape) - 1)
    return (lane // 32) % 2 == 0, lane < 64


def counts_row(ref, kind):
    cells = [ref[kind, sec, row : row + 1, :] for sec in range(2) for row in range(2)]
    return jnp.concatenate(cells, axis=1).astype(jnp.float32)


def live_counts(counts_ref, sizes):
    n_sec, n_row = sizes
    row_zero, sec_zero = lane_bits((1, 128))
    lane = lax.broadcasted_iota(jnp.int32, (1, 128), 1)
    section = 0
    for axis in SEC_AXES:
        section = section * lax.axis_size(axis) + lax.axis_index(axis)
    last_row = lax.axis_index("row") == n_row - 1
    last_sec = section == n_sec - 1
    zero = jnp.zeros((1, 128), jnp.float32)
    counts = [counts_row(counts_ref, kind) for kind in range(4)]
    return [
        jnp.where(lane % 32 == 31, zero, counts[0]),
        jnp.where(jnp.logical_and(jnp.logical_not(row_zero), last_row), zero, counts[1]),
        jnp.where(jnp.logical_and(jnp.logical_not(sec_zero), last_sec), zero, counts[2]),
        jnp.where(last_sec, zero, counts[3]),
    ]


def live_points(count):
    point = lax.broadcasted_iota(jnp.int32, (128, 128), 0).astype(jnp.float32)
    return jnp.where(point < count, 1.0, 0.0)


def block_sums(first, second, live):
    u, v = first
    p, q = second
    dx = p - u
    dy = q - v

    def red(z):
        return jnp.sum(z, axis=0, keepdims=True)

    su, sv, sp, sq, n = red(u), red(v), red(p), red(q), red(live)
    F = [red(u * u), red(u * v), su, red(v * v), sv, n]
    G = [red(p * p), red(p * q), sp, red(q * q), sq, n]
    C = [red(u * p), red(u * q), su, red(v * p), red(v * q), sv, sp, sq, n]
    tx, ty = red(dx), red(dy)
    s1 = [red(dx * u), red(dx * v), tx, red(dy * u), red(dy * v), ty]
    s2 = [red(dx * p), red(dx * q), tx, red(dy * p), red(dy * q), ty]
    return F, G, C, s1, s2


def gram_kernel(f_ref, g_ref, alive_ref, up_ref, rest_ref, outside_ref, next_ref, low_ref, packet, kept):
    row_zero, sec_zero = lane_bits((1, 128))

    def pair_rows(ref, start, count, comp):
        return ref[pl.ds(2 * start + comp, count, stride=2), :]

    def own(ref, kind):
        return [pair_rows(ref, kind * 128, 128, comp).T for comp in range(2)]

    zero = jnp.zeros((1, 128), jnp.float32)
    alive = [alive_ref[kind : kind + 1, :] for kind in range(4)]

    def masked(points, count):
        live = live_points(count)
        return [z * live for z in points], live

    def second_of(kind):
        if kind == 0:
            return [roll(z, -1, 1) for z in own(g_ref, 0)]
        out = []
        for comp in range(2):
            if kind == 1:
                parts = [
                    pair_rows(g_ref, 128 + 32, 32, comp),
                    pair_rows(next_ref, 0, 32, comp),
                    pair_rows(g_ref, 128 + 96, 32, comp),
                    pair_rows(next_ref, 32, 32, comp),
                ]
            elif kind == 2:
                parts = [pair_rows(g_ref, 256 + 64, 64, comp), pair_rows(up_ref, 0, 64, comp)]
            else:
                rest = pair_rows(rest_ref, 0, 96, comp) + pair_rows(outside_ref, 0, 96, comp)
                parts = [pair_rows(up_ref, 64, 32, comp), rest]
            out.append(jnp.concatenate(parts, axis=0).T)
        return out

    D = [zero] * 6
    S = [zero] * 6
    unit = 1.0 / SPAN

    def put(row, value):
        packet[row : row + 1, :] = value

    for kind in range(4):
        first, live = masked(own(f_ref, kind), alive[kind])
        second, _ = masked(second_of(kind), alive[kind])
        for i, points in enumerate(first + second):
            kept[4 * kind + i] = points
        F, G, C, s1, s2 = block_sums(first, second, live)
        D = [a + b for a, b in zip(D, F)]
        S = [a + b for a, b in zip(S, s1)]
        for i in range(9):
            put(AT_C + 9 * kind + i, C[i] * unit)
        if kind == 0:
            D = [a + roll(b, 1, 1) for a, b in zip(D, G)]
            S = [a - roll(b, 1, 1) for a, b in zip(S, s2)]
        elif kind == 1:
            D = [a + jnp.where(row_zero, zero, roll(b, 32, 1)) for a, b in zip(D, G)]
            S = [a - jnp.where(row_zero, zero, roll(b, 32, 1)) for a, b in zip(S, s2)]
        elif kind == 2:
            D = [a + jnp.where(sec_zero, zero, roll(b, 64, 1)) for a, b in zip(D, G)]
            S = [a - jnp.where(sec_zero, zero, roll(b, 64, 1)) for a, b in zip(S, s2)]
            for i in range(3):
                put(AT_TWO + i, jnp.where(sec_zero, roll(s2[3 + i], 64, 1), s2[i]))
            put(AT_TWO + 3, jnp.where(sec_zero, roll(G[1], 64, 1), G[0]) * unit)
            put(AT_TWO + 4, G[3] * unit)
        else:
            put(AT_THREE, G[0] * unit)
            put(AT_THREE + 1, G[1] * unit)
            put(AT_THREE + 2, G[3] * unit)
            for i in range(6):
                put(AT_THREE + 3 + i, s2[i])

    low_count = jnp.where(row_zero, zero, low_ref[128:129, :])
    first = []
    second = []
    for comp in range(2):
        low = [pair_rows(low_ref, 32 * sec, 32, comp) for sec in range(2)]
        first.append(jnp.concatenate([low[0], low[0], low[1], low[1]], axis=0).T)
        mine = [pair_rows(g_ref, 128 + 64 * sec, 32, comp) for sec in range(2)]
        second.append(jnp.concatenate([mine[0], mine[0], mine[1], mine[1]], axis=0).T)
    first, live = masked(first, low_count)
    second, _ = masked(second, low_count)
    F, G, C, s1, s2 = block_sums(first, second, live)
    D = [a + jnp.where(row_zero, roll(b, -32, 1), zero) for a, b in zip(D, G)]
    S = [a - jnp.where(row_zero, roll(b, -32, 1), zero) for a, b in zip(S, s2)]

    for i in range(6):
        a, b = SYM[i]
        put(i, D[i] * unit + ((SQUARES[a] - SHIFT) * unit if a == b else 0.0))
        put(6 + i, S[i])
    for row in range(USED, ROWS):
        put(row, zero)


def from_above(value):
    return roll(value, -1, 0)


def from_below(value):
    return roll(value, 1, 0)


def pack_up_kernel(g_ref, up, rest, sems):
    copies = [
        pltpu.make_async_copy(g_ref.at[pl.ds(512, 128)], up.at[pl.ds(0, 128)], sems.at[0]),
        pltpu.make_async_copy(g_ref.at[pl.ds(768, 64)], up.at[pl.ds(128, 64)], sems.at[1]),
        pltpu.make_async_copy(g_ref.at[pl.ds(832, 192)], rest, sems.at[2]),
    ]
    for copy in copies:
        copy.start()
    for copy in copies:
        copy.wait()


def pack_rows_kernel(sizes, f_ref, g_ref, counts_hbm, beside, odd, alive, counts_ref, sems):
    copies = [
        pltpu.make_async_copy(g_ref.at[pl.ds(256, 64)], beside.at[pl.ds(0, 64)], sems.at[0]),
        pltpu.make_async_copy(g_ref.at[pl.ds(384, 64)], beside.at[pl.ds(64, 64)], sems.at[1]),
        pltpu.make_async_copy(f_ref.at[pl.ds(320, 64)], odd.at[pl.ds(0, 64)], sems.at[2]),
        pltpu.make_async_copy(f_ref.at[pl.ds(448, 64)], odd.at[pl.ds(64, 64)], sems.at[3]),
    ]
    fetch = pltpu.make_async_copy(counts_hbm, counts_ref, sems.at[4])
    fetch.start()
    for copy in copies:
        copy.start()
    fetch.wait()
    for kind, row in enumerate(live_counts(counts_ref, sizes)):
        alive[kind : kind + 1, :] = row
    alive[4:8, :] = jnp.zeros((4, 128), jnp.float32)
    odd[128:136, :] = jnp.broadcast_to(counts_row(counts_ref, 1), (8, 128))
    for copy in copies:
        copy.wait()


def merge_kernel(both, above, below, out):
    row_zero, _ = lane_bits((1, 128))
    for part in range(2):
        at = part * ROWS
        to = part * DOUBLE
        out[to : to + USED, :] = both[at : at + USED, :]
        a = above[at : at + USED, :]
        b = below[at : at + USED, :]
        out[to + AT_E : to + AT_E + USED, :] = jnp.where(row_zero, a, b)
        first = AT_C + 9
        for i in range(5):
            one, two = b[first + i : first + i + 1], b[first + min(5 + i, 8) : first + min(5 + i, 8) + 1]
            out[to + AT_E2 + i : to + AT_E2 + i + 1, :] = jnp.where(row_zero, one, roll(two, 32, 1))
        for i, source in enumerate(BEYOND):
            out[to + AT_E2 + 5 + i : to + AT_E2 + 6 + i, :] = jnp.where(
                row_zero, b[source : source + 1], a[source : source + 1]
            )


class Window:
    def __init__(self, load, n_dev):
        self.load = load
        self.bits = lane_bits((2 * n_dev, 128))

    def seconds(self, v, row_values):
        row_zero, sec_zero = self.bits
        half = roll(v, 64, 1)
        return [
            roll(v, -1, 1),
            row_values,
            jnp.where(sec_zero, half, from_above(half)),
            from_above(v),
        ]

    def row_pairs(self, v, e, e2):
        row_zero, _ = self.bits
        forth, back = roll(v, 32, 1), roll(v, -32, 1)
        own = jnp.where(row_zero, back, roll(e, 32, 1))
        side = jnp.where(row_zero, roll(e2, -32, 1), forth)
        return own, side

    def c(self, side, kind, i, j):
        return self.load(side * 42 + 6 + 9 * kind + 3 * i + j)

    def d(self, side, i, j):
        return self.load(side * 42 + sym_at(i, j))

    def c_e2(self, i, j):
        return self.load(84 + 3 * i + j)

    def transposed(self, c, a):
        return [c(0, j) * a[0] + c(1, j) * a[1] + c(2, j) * a[2] for j in range(3)]

    def apply(self, v, e, e2, sides):
        row_zero, sec_zero = self.bits
        outs = ([None] * 6, [None] * 6)
        for half in range(2):
            span = slice(3 * half, 3 * half + 3)
            sets = (v[span], e[span])
            beyond = e2[span]
            pairs = [self.row_pairs(*z) for z in zip(v[span], e[span], beyond)]
            t_row = [self.transposed(functools.partial(self.c, side, 1), sets[side]) for side in range(2)]
            for side in sides:
                a = sets[side]
                after = [self.seconds(a[j], pairs[j][side]) for j in range(3)]
                total = []
                for i in range(3):
                    y = sum(self.d(side, i, j) * a[j] for j in range(3))
                    for kind in range(4):
                        y = y - sum(self.c(side, kind, i, j) * after[j][kind] for j in range(3))
                    total.append(y)
                col = self.transposed(functools.partial(self.c, side, 0), a)
                one = self.transposed(functools.partial(self.c, side, 2), a)
                two = self.transposed(functools.partial(self.c, side, 3), a)
                if side == 1:
                    outer = self.transposed(self.c_e2, beyond)
                for j in range(3):
                    t = roll(one[j], 64, 1)
                    y = total[j] - roll(col[j], 1, 1) - jnp.where(sec_zero, from_below(t), t) - from_below(two[j])
                    if side == 0:
                        y = y - jnp.where(row_zero, roll(t_row[1][j], -32, 1), roll(t_row[0][j], 32, 1))
                    else:
                        y = y - jnp.where(row_zero, roll(t_row[0][j], -32, 1), roll(outer[j], 32, 1))
                    outs[side][3 * half + j] = y
        return outs


def window_kernel(got, blocks, v0, e0, v1, e1, v2):
    n_dev = got.shape[0] // (2 * DOUBLE)
    row_zero, sec_zero = lane_bits((2 * n_dev, 128))
    zero = jnp.zeros((2 * n_dev, 128), jnp.float32)

    def row(i):
        return jnp.concatenate(
            [got[pl.ds(slot * DOUBLE + i, n_dev, stride=2 * DOUBLE), :] for slot in range(2)], axis=0
        )

    def from_two(value, packed_second=False):
        if not packed_second:
            value = roll(value, 64, 1)
        return from_below(jnp.where(sec_zero, value, zero))

    def s_terms(three, two):
        return [
            from_below(row(three + i)) + from_two(row(two + i % 3), packed_second=i >= 3) for i in range(6)
        ]

    starts = []
    for side, at in enumerate((0, AT_E)):
        base = side * 42
        for i in range(36):
            blocks[base + 6 + i] = row(at + AT_C + i)
        two = [blocks[base + 24 + i] for i in (6, 7, 8)]
        three = [blocks[base + 33 + i] for i in (6, 7, 8)]
        pair, last = row(at + AT_TWO + 3), row(at + AT_TWO + 4)
        G_two = [from_two(z) for z in (pair, pair, two[0], last, two[1], two[2])]
        G_two[1] = from_two(pair, packed_second=True)
        G_three = [row(at + AT_THREE), row(at + AT_THREE + 1), three[0], row(at + AT_THREE + 2), three[1], three[2]]
        for i in range(6):
            blocks[base + i] = row(at + i) + G_two[i] + from_below(G_three[i])
        terms = s_terms(at + AT_THREE + 3, at + AT_TWO)
        starts.append([row(at + 6 + i) - terms[i] for i in range(6)])
    for i in range(5):
        packed = row(AT_E2 + i)
        blocks[84 + i] = packed
        if i < 4:
            blocks[89 + i] = roll(packed, -32, 1)
    terms = s_terms(AT_E2 + 11, AT_E2 + 17)
    outer = [row(AT_E2 + 5 + i) - terms[i] for i in range(6)]
    window = Window(lambda i: blocks[i], n_dev)
    v, e = starts
    w, f = window.apply(v, e, outer, (0, 1))
    last, _ = window.apply(w, f, f, (0,))
    for i in range(6):
        v0[i] = v[i]
        e0[i] = e[i]
        v1[i] = w[i]
        e1[i] = f[i]
        v2[i] = last[i]


def moments_kernel(blocks, v0, v1, v2, above, below, kept_hbm, e2, v3, e3, out, kept, sems):
    fetches = [
        pltpu.make_async_copy(kept_hbm.at[pl.ds(2 * i, 2)], kept.at[pl.ds(2 * i, 2)], sems.at[i]) for i in range(8)
    ]
    for fetch in fetches:
        fetch.start()
    shape = v2.shape[1:]
    n_dev = shape[0] // 2
    bits = lane_bits(shape)
    row_zero, _ = bits
    window = Window(lambda i: blocks[i], n_dev)
    v = [v2[i] for i in range(6)]
    side = [jnp.where(row_zero, above[i], below[i]) for i in range(6)]
    outer = [jnp.where(row_zero, below[i], above[i]) for i in range(6)]
    w, f = window.apply(v, side, outer, (0, 1))
    for i in range(6):
        e2[i] = side[i]
        v3[i] = w[i]
        e3[i] = f[i]
    vs = [[v0[i] for i in range(6)], [v1[i] for i in range(6)], v, w]

    def dot(left, right):
        return sum(a[:n_dev] * b[:n_dev] for a, b in zip(left, right))

    products = [dot(vs[n // 2], vs[n - n // 2]) for n in range(7)]
    energy = 0.0
    for half in range(2):
        a = w[3 * half : 3 * half + 3]
        b = f[3 * half : 3 * half + 3]
        after = [window.seconds(a[j], jnp.where(row_zero, roll(a[j], -32, 1), roll(b[j], 32, 1))) for j in range(3)]
        for i in range(3):
            inner = sum(window.d(0, i, j) * a[j] for j in range(3))
            for kind in range(4):
                inner = inner - 2.0 * sum(window.c(0, kind, i, j) * after[j][kind] for j in range(3))
            energy = energy + a[i][:n_dev] * inner[:n_dev]
    products.append(energy)
    lane = lax.broadcasted_iota(jnp.int32, (1, 128), 1)
    packed = jnp.zeros((1, 128), jnp.float32)
    for n, value in enumerate(products):
        value = jnp.sum(jnp.sum(value, axis=0, keepdims=True), axis=1, keepdims=True)
        packed = jnp.where(lane == n, value, packed)
    out[...] = packed
    for fetch in fetches:
        fetch.wait()


def coefficients(moments):
    zero = jnp.zeros_like(moments[0])

    def inner(s, p, offset):
        total = zero
        for i, a in enumerate(s):
            for j, b in enumerate(p):
                total = total + a * b * moments[i + j + offset]
        return total

    def energy(p):
        return inner(p, p, 1) + HALF * inner(p, p, 0)

    s = [zero + 1.0]
    p = [zero + 1.0]
    x = [zero] * ITERS
    gamma = inner(s, s, 0)
    for sweep in range(ITERS):
        alpha = gamma / energy(p)
        x = [x[i] + (alpha * p[i] if i < len(p) else 0.0) for i in range(ITERS)]
        if sweep < ITERS - 1:
            image = [(p[i - 1] if i else 0.0) + (HALF * p[i] if i < len(p) else 0.0) for i in range(len(p) + 1)]
            s = [(s[i] if i < len(s) else 0.0) - alpha * image[i] for i in range(len(image))]
            gamma_new = inner(s, s, 0)
            beta = gamma_new / gamma
            p = [s[i] + (beta * p[i] if i < len(p) else 0.0) for i in range(len(s))]
            gamma = gamma_new
    return [value * (1.0 / SPAN) for value in x]


def finish_kernel(alive_ref, sums, v0, v1, v2, v3, n0, n1, n2, n3, kept, affines_hbm, residual_hbm, affines, residual, sems):
    stores = []
    total = jnp.sum(sums[...], axis=0, keepdims=True)
    lane = lax.broadcasted_iota(jnp.int32, (1, 128), 1)
    moments = [jnp.sum(jnp.where(lane == n, total, 0.0), axis=1, keepdims=True) for n in range(8)]
    weights = coefficients(moments)
    at = lax.axis_index("x") * lax.axis_size("core") + lax.axis_index("core")
    alive = [alive_ref[kind : kind + 1, :] for kind in range(4)]
    row_zero, sec_zero = lane_bits((1, 128))

    def mix(refs, i, dev):
        return sum(w * ref[i, pl.ds(dev, 1), :] for w, ref in zip(weights, refs))

    vs = (v0, v1, v2, v3)
    x = [mix(vs, i, at) for i in range(6)]
    above = [mix(vs, i, at + 1) for i in range(6)]
    beside = [mix((n0, n1, n2, n3), i, at) for i in range(6)]
    for i in range(6):
        for sec in range(2):
            for row in range(2):
                start = 64 * sec + 32 * row
                affines[i, sec, row : row + 1, :] = x[i][:, start : start + 32]
    stores.append(pltpu.make_async_copy(affines, affines_hbm, sems.at[4]))
    stores[-1].start()
    for kind in range(4):
        if kind == 0:
            b = [roll(z, -1, 1) for z in x]
        elif kind == 1:
            b = [jnp.where(row_zero, roll(z, -32, 1), roll(w, 32, 1)) for z, w in zip(x, beside)]
        elif kind == 2:
            b = [jnp.where(sec_zero, roll(z, 64, 1), roll(w, 64, 1)) for z, w in zip(x, above)]
        else:
            b = above
        u, v, p, q = (kept[4 * kind + i] for i in range(4))
        live = live_points(alive[kind])
        for comp in range(2):
            o = 3 * comp
            r = (p - u) if comp == 0 else (q - v)
            r = r - (x[o] * u + x[o + 1] * v) + (b[o] * p + b[o + 1] * q) - live * (x[o + 2] - b[o + 2])
            residual[pl.ds(kind * 256 + comp, 128, stride=2), :] = r.T
        part = pl.ds(kind * 256, 256)
        stores.append(pltpu.make_async_copy(residual.at[part], residual_hbm.at[part], sems.at[kind]))
        stores[-1].start()
    for store in stores:
        store.wait()


def shape_of(*shape):
    return jax.ShapeDtypeStruct(shape, jnp.float32)


def call(interpret, kernel, outs, *args, scalars=0, anywhere=(), copies=0, buffers=(), results=None):
    spaces = []
    args = list(args)
    shapes = [shape_of(*out) for out in outs]
    for n, arg in enumerate(args):
        if n < scalars:
            spaces.append(pl.BlockSpec(memory_space=pltpu.SMEM))
        elif n in anywhere:
            spaces.append(pl.BlockSpec(memory_space=pl.ANY))
        else:
            spaces.append(pl.BlockSpec(memory_space=pltpu.VMEM))
            if arg.dtype == jnp.float32 and not interpret:
                args[n] = pltpu.with_memory_space_constraint(arg, pltpu.VMEM)
    if not results and not interpret:
        shapes = [pltpu.VMEM(out, jnp.float32) for out in outs]
    results = results or [pltpu.VMEM] * len(outs)
    return pl.pallas_call(
        kernel,
        out_shape=shapes,
        in_specs=spaces,
        out_specs=[pl.BlockSpec(memory_space=space) for space in results],
        scratch_shapes=list(buffers)
        + ([pltpu.SemaphoreType.DMA((copies,))] if copies else []),
        interpret=interpret,
    )(*args)


def shifted(value, axes, steps):
    count = lax.axis_size(axes)
    pairs = [(i, i + steps) for i in range(count) if 0 <= i + steps < count]
    return lax.ppermute(value, axes, pairs)


def pack_up(run, g):
    return run(pack_up_kernel, [(192, 128), (192, 128)], g, anywhere=(0,), copies=3)


def pack_rows(run, f, g, counts, sizes):
    return run(
        functools.partial(pack_rows_kernel, sizes),
        [(128, 128), (136, 128), (8, 128)],
        f,
        g,
        counts,
        anywhere=(0, 1, 2),
        copies=5,
        buffers=[pltpu.VMEM(counts.shape, jnp.int32)],
    )


def per_device(interpret, first_pts, second_pts, counts):
    run = functools.partial(call, interpret)
    n_sec = lax.axis_size(SEC_AXES)
    n_dev = lax.axis_size(GROUP)
    n_group = n_sec // n_dev
    f = first_pts.reshape(1024, 128)
    g = second_pts.reshape(1024, 128)
    up, rest = pack_up(run, g)
    up = shifted(up, SEC_AXES, -1)
    relay = n_dev - 2
    inside = [(i + 1, i) for i in range(n_sec - 1) if (i + 1) % n_dev]
    to_relay = [(group * n_dev, group * n_dev + relay) for group in range(1, n_group)]
    from_relay = [(group * n_dev + relay, group * n_dev - 1) for group in range(1, n_group)]
    relayed = lax.ppermute(rest, SEC_AXES, to_relay)
    relayed, f_later, g_later = lax.optimization_barrier((relayed, f, g))
    outside = lax.ppermute(relayed, SEC_AXES, from_relay)
    sizes = (n_sec, lax.axis_size("row"))
    beside, odd, alive, rest = lax.optimization_barrier((*pack_rows(run, f_later, g_later, counts, sizes), rest))
    beside = shifted(beside, "row", -1)
    low = shifted(odd, "row", 1)
    rest = lax.ppermute(rest, SEC_AXES, inside)
    packet, kept = run(gram_kernel, [(ROWS, 128), (16, 128, 128)], f, g, alive, up, rest, outside, beside, low)

    half = n_dev // 2
    pairs = []
    for group in range(n_group):
        for dev in range(n_dev):
            source = group + (1 if dev < half else -1)
            if 0 <= source < n_group:
                pairs.append((source * n_dev + dev, group * n_dev + dev))
    other = lax.ppermute(packet, SEC_AXES, pairs)
    both = jnp.concatenate([packet, other], axis=0)
    (mine,) = run(merge_kernel, [(2 * DOUBLE, 128)], both, shifted(both, "row", -1), shifted(both, "row", 1))
    got = lax.all_to_all(jnp.broadcast_to(mine[None], (n_dev, 2 * DOUBLE, 128)), GROUP, 0, 0, tiled=False)
    wide = (6, 2 * n_dev, 128)
    blocks, v0, e0, v1, e1, v2 = run(
        window_kernel, [(93, 2 * n_dev, 128)] + [wide] * 5, got.reshape(n_dev * 2 * DOUBLE, 128)
    )
    e2, v3, e3, part, kept = run(
        moments_kernel,
        [wide, wide, wide, (1, 128), (16, 128, 128)],
        blocks,
        v0,
        v1,
        v2,
        shifted(v2, "row", -1),
        shifted(v2, "row", 1),
        kept,
        anywhere=(6,),
        copies=8,
    )
    n_other = lax.axis_size(OTHERS)
    groups = sum_groups([lax.axis_size(axis) for axis in EVERY])
    sums = lax.all_to_all(
        jnp.broadcast_to(part[None], (n_other, 1, 128)), EVERY, 0, 0, axis_index_groups=groups, tiled=False
    )
    affines, residual = run(
        finish_kernel,
        [(6,) + counts.shape[1:], (1024, 128)],
        alive,
        sums.reshape(n_other, 128),
        v0,
        v1,
        v2,
        v3,
        e0,
        e1,
        e2,
        e3,
        kept,
        copies=5,
        buffers=[pltpu.VMEM((6,) + counts.shape[1:], jnp.float32), pltpu.VMEM((1024, 128), jnp.float32)],
        results=[pl.ANY, pl.ANY],
    )
    return affines, residual.reshape(first_pts.shape)


def sum_groups(sizes):
    n_y, n_zhi, n_x, n_core, n_row = sizes
    n_z = n_zhi * n_row
    first = 5 * n_z // 8
    groups = []
    for place in range(n_x * n_core):
        order = [((first + step) % n_z, y) for step in range(n_z) for y in reversed(range(n_y))]
        groups.append([((y * n_zhi + z // n_row) * n_x * n_core + place) * n_row + z % n_row for z, y in order])
    return groups


def split_mesh(mesh):
    n_row = mesh.shape["row"]
    return Mesh(mesh.devices.reshape(4, 4, 4, 2, n_row), SEC_AXES + ("row",))


def solution(mesh, inner=None, interpret=False):
    inner = inner or split_mesh(mesh)
    in_specs = (
        P(None, SEC_AXES, "row", None, None, None),
        P(None, SEC_AXES, "row", None, None, None),
        P(None, SEC_AXES, "row", None),
    )
    out_specs = (P(None, SEC_AXES, "row", None), P(None, SEC_AXES, "row", None, None, None))
    return jax.shard_map(
        functools.partial(per_device, interpret), mesh=inner, in_specs=in_specs, out_specs=out_specs, check_vma=False
    )
```

```python
import functools

import jax
import jax.numpy as jnp
from jax import lax
from jax.experimental import pallas as pl
from jax.experimental.pallas import tpu as pltpu
from jax.sharding import Mesh
from jax.sharding import PartitionSpec as P

ITERS = 4
SPAN = 1024.0
SHIFT = 512.0
HALF = SHIFT / SPAN
SQUARES = (0.49, 0.49, 0.09)
SYM = ((0, 0), (0, 1), (0, 2), (1, 1), (1, 2), (2, 2))
SEC_AXES = ("y", "zhi", "x", "core")
GROUP = ("x", "core")
OTHERS = ("y", "zhi", "row")
EVERY = SEC_AXES + ("row",)

ROWS = 64
AT_C = 12
AT_THREE = 48
AT_TWO = 57
USED = 62
AT_E = 62
AT_E2 = 124
DOUBLE = 144
BEYOND = [6 + i for i in range(6)] + [AT_THREE + 3 + i for i in range(6)] + [AT_TWO + i for i in range(3)]


def sym_at(a, b):
    return SYM.index((min(a, b), max(a, b)))


def roll(value, shift, axis):
    size = value.shape[axis]
    return pltpu.roll(value, shift % size, axis)


def lane_bits(shape):
    lane = lax.broadcasted_iota(jnp.int32, shape, len(shape) - 1)
    return (lane // 32) % 2 == 0, lane < 64


def counts_row(ref, kind):
    cells = [ref[kind, sec, row : row + 1, :] for sec in range(2) for row in range(2)]
    return jnp.concatenate(cells, axis=1).astype(jnp.float32)


def live_counts(counts_ref, sizes):
    n_sec, n_row = sizes
    row_zero, sec_zero = lane_bits((1, 128))
    lane = lax.broadcasted_iota(jnp.int32, (1, 128), 1)
    section = 0
    for axis in SEC_AXES:
        section = section * lax.axis_size(axis) + lax.axis_index(axis)
    last_row = lax.axis_index("row") == n_row - 1
    last_sec = section == n_sec - 1
    zero = jnp.zeros((1, 128), jnp.float32)
    counts = [counts_row(counts_ref, kind) for kind in range(4)]
    return [
        jnp.where(lane % 32 == 31, zero, counts[0]),
        jnp.where(jnp.logical_and(jnp.logical_not(row_zero), last_row), zero, counts[1]),
        jnp.where(jnp.logical_and(jnp.logical_not(sec_zero), last_sec), zero, counts[2]),
        jnp.where(last_sec, zero, counts[3]),
    ]


def live_points(count):
    point = lax.broadcasted_iota(jnp.int32, (128, 128), 0).astype(jnp.float32)
    return jnp.where(point < count, 1.0, 0.0)


def block_sums(first, second, live):
    u, v = first
    p, q = second
    dx = p - u
    dy = q - v

    def red(z):
        return jnp.sum(z, axis=0, keepdims=True)

    su, sv, sp, sq, n = red(u), red(v), red(p), red(q), red(live)
    F = [red(u * u), red(u * v), su, red(v * v), sv, n]
    G = [red(p * p), red(p * q), sp, red(q * q), sq, n]
    C = [red(u * p), red(u * q), su, red(v * p), red(v * q), sv, sp, sq, n]
    tx, ty = red(dx), red(dy)
    s1 = [red(dx * u), red(dx * v), tx, red(dy * u), red(dy * v), ty]
    s2 = [red(dx * p), red(dx * q), tx, red(dy * p), red(dy * q), ty]
    return F, G, C, s1, s2


def gram_kernel(f_ref, g_ref, alive_ref, up_ref, rest_ref, outside_ref, next_ref, low_ref, packet, kept):
    row_zero, sec_zero = lane_bits((1, 128))

    def pair_rows(ref, start, count, comp):
        return ref[pl.ds(2 * start + comp, count, stride=2), :]

    def own(ref, kind):
        return [pair_rows(ref, kind * 128, 128, comp).T for comp in range(2)]

    zero = jnp.zeros((1, 128), jnp.float32)
    alive = [alive_ref[kind : kind + 1, :] for kind in range(4)]

    def masked(points, count):
        live = live_points(count)
        return [z * live for z in points], live

    def second_of(kind):
        if kind == 0:
            return [roll(z, -1, 1) for z in own(g_ref, 0)]
        out = []
        for comp in range(2):
            if kind == 1:
                parts = [
                    pair_rows(g_ref, 128 + 32, 32, comp),
                    pair_rows(next_ref, 0, 32, comp),
                    pair_rows(g_ref, 128 + 96, 32, comp),
                    pair_rows(next_ref, 32, 32, comp),
                ]
            elif kind == 2:
                parts = [pair_rows(g_ref, 256 + 64, 64, comp), pair_rows(up_ref, 0, 64, comp)]
            else:
                rest = pair_rows(rest_ref, 0, 96, comp) + pair_rows(outside_ref, 0, 96, comp)
                parts = [pair_rows(up_ref, 64, 32, comp), rest]
            out.append(jnp.concatenate(parts, axis=0).T)
        return out

    D = [zero] * 6
    S = [zero] * 6
    unit = 1.0 / SPAN

    def put(row, value):
        packet[row : row + 1, :] = value

    for kind in range(4):
        first, live = masked(own(f_ref, kind), alive[kind])
        second, _ = masked(second_of(kind), alive[kind])
        for i, points in enumerate(first + second):
            kept[4 * kind + i] = points
        F, G, C, s1, s2 = block_sums(first, second, live)
        D = [a + b for a, b in zip(D, F)]
        S = [a + b for a, b in zip(S, s1)]
        for i in range(9):
            put(AT_C + 9 * kind + i, C[i] * unit)
        if kind == 0:
            D = [a + roll(b, 1, 1) for a, b in zip(D, G)]
            S = [a - roll(b, 1, 1) for a, b in zip(S, s2)]
        elif kind == 1:
            D = [a + jnp.where(row_zero, zero, roll(b, 32, 1)) for a, b in zip(D, G)]
            S = [a - jnp.where(row_zero, zero, roll(b, 32, 1)) for a, b in zip(S, s2)]
        elif kind == 2:
            D = [a + jnp.where(sec_zero, zero, roll(b, 64, 1)) for a, b in zip(D, G)]
            S = [a - jnp.where(sec_zero, zero, roll(b, 64, 1)) for a, b in zip(S, s2)]
            for i in range(3):
                put(AT_TWO + i, jnp.where(sec_zero, roll(s2[3 + i], 64, 1), s2[i]))
            put(AT_TWO + 3, jnp.where(sec_zero, roll(G[1], 64, 1), G[0]) * unit)
            put(AT_TWO + 4, G[3] * unit)
        else:
            put(AT_THREE, G[0] * unit)
            put(AT_THREE + 1, G[1] * unit)
            put(AT_THREE + 2, G[3] * unit)
            for i in range(6):
                put(AT_THREE + 3 + i, s2[i])

    low_count = jnp.where(row_zero, zero, low_ref[128:129, :])
    first = []
    second = []
    for comp in range(2):
        low = [pair_rows(low_ref, 32 * sec, 32, comp) for sec in range(2)]
        first.append(jnp.concatenate([low[0], low[0], low[1], low[1]], axis=0).T)
        mine = [pair_rows(g_ref, 128 + 64 * sec, 32, comp) for sec in range(2)]
        second.append(jnp.concatenate([mine[0], mine[0], mine[1], mine[1]], axis=0).T)
    first, live = masked(first, low_count)
    second, _ = masked(second, low_count)
    F, G, C, s1, s2 = block_sums(first, second, live)
    D = [a + jnp.where(row_zero, roll(b, -32, 1), zero) for a, b in zip(D, G)]
    S = [a - jnp.where(row_zero, roll(b, -32, 1), zero) for a, b in zip(S, s2)]

    for i in range(6):
        a, b = SYM[i]
        put(i, D[i] * unit + ((SQUARES[a] - SHIFT) * unit if a == b else 0.0))
        put(6 + i, S[i])
    for row in range(USED, ROWS):
        put(row, zero)


def from_above(value):
    return roll(value, -1, 0)


def from_below(value):
    return roll(value, 1, 0)


def pack_up_kernel(g_ref, up, rest, sems):
    copies = [
        pltpu.make_async_copy(g_ref.at[pl.ds(512, 128)], up.at[pl.ds(0, 128)], sems.at[0]),
        pltpu.make_async_copy(g_ref.at[pl.ds(768, 64)], up.at[pl.ds(128, 64)], sems.at[1]),
        pltpu.make_async_copy(g_ref.at[pl.ds(832, 192)], rest, sems.at[2]),
    ]
    for copy in copies:
        copy.start()
    for copy in copies:
        copy.wait()


def pack_rows_kernel(sizes, f_ref, g_ref, counts_hbm, beside, odd, alive, counts_ref, sems):
    copies = [
        pltpu.make_async_copy(g_ref.at[pl.ds(256, 64)], beside.at[pl.ds(0, 64)], sems.at[0]),
        pltpu.make_async_copy(g_ref.at[pl.ds(384, 64)], beside.at[pl.ds(64, 64)], sems.at[1]),
        pltpu.make_async_copy(f_ref.at[pl.ds(320, 64)], odd.at[pl.ds(0, 64)], sems.at[2]),
        pltpu.make_async_copy(f_ref.at[pl.ds(448, 64)], odd.at[pl.ds(64, 64)], sems.at[3]),
    ]
    fetch = pltpu.make_async_copy(counts_hbm, counts_ref, sems.at[4])
    fetch.start()
    for copy in copies:
        copy.start()
    fetch.wait()
    for kind, row in enumerate(live_counts(counts_ref, sizes)):
        alive[kind : kind + 1, :] = row
    alive[4:8, :] = jnp.zeros((4, 128), jnp.float32)
    odd[128:136, :] = jnp.broadcast_to(counts_row(counts_ref, 1), (8, 128))
    for copy in copies:
        copy.wait()


def merge_kernel(both, above, below, out):
    row_zero, _ = lane_bits((1, 128))
    for part in range(2):
        at = part * ROWS
        to = part * DOUBLE
        out[to : to + USED, :] = both[at : at + USED, :]
        a = above[at : at + USED, :]
        b = below[at : at + USED, :]
        out[to + AT_E : to + AT_E + USED, :] = jnp.where(row_zero, a, b)
        first = AT_C + 9
        for i in range(5):
            one, two = b[first + i : first + i + 1], b[first + min(5 + i, 8) : first + min(5 + i, 8) + 1]
            out[to + AT_E2 + i : to + AT_E2 + i + 1, :] = jnp.where(row_zero, one, roll(two, 32, 1))
        for i, source in enumerate(BEYOND):
            out[to + AT_E2 + 5 + i : to + AT_E2 + 6 + i, :] = jnp.where(
                row_zero, b[source : source + 1], a[source : source + 1]
            )


class Window:
    def __init__(self, load, n_dev):
        self.load = load
        self.bits = lane_bits((2 * n_dev, 128))

    def seconds(self, v, row_values):
        row_zero, sec_zero = self.bits
        half = roll(v, 64, 1)
        return [
            roll(v, -1, 1),
            row_values,
            jnp.where(sec_zero, half, from_above(half)),
            from_above(v),
        ]

    def row_pairs(self, v, e, e2):
        row_zero, _ = self.bits
        forth, back = roll(v, 32, 1), roll(v, -32, 1)
        own = jnp.where(row_zero, back, roll(e, 32, 1))
        side = jnp.where(row_zero, roll(e2, -32, 1), forth)
        return own, side

    def c(self, side, kind, i, j):
        return self.load(side * 42 + 6 + 9 * kind + 3 * i + j)

    def d(self, side, i, j):
        return self.load(side * 42 + sym_at(i, j))

    def c_e2(self, i, j):
        return self.load(84 + 3 * i + j)

    def transposed(self, c, a):
        return [c(0, j) * a[0] + c(1, j) * a[1] + c(2, j) * a[2] for j in range(3)]

    def apply(self, v, e, e2, sides):
        row_zero, sec_zero = self.bits
        outs = ([None] * 6, [None] * 6)
        for half in range(2):
            span = slice(3 * half, 3 * half + 3)
            sets = (v[span], e[span])
            beyond = e2[span]
            pairs = [self.row_pairs(*z) for z in zip(v[span], e[span], beyond)]
            t_row = [self.transposed(functools.partial(self.c, side, 1), sets[side]) for side in range(2)]
            for side in sides:
                a = sets[side]
                after = [self.seconds(a[j], pairs[j][side]) for j in range(3)]
                total = []
                for i in range(3):
                    y = sum(self.d(side, i, j) * a[j] for j in range(3))
                    for kind in range(4):
                        y = y - sum(self.c(side, kind, i, j) * after[j][kind] for j in range(3))
                    total.append(y)
                col = self.transposed(functools.partial(self.c, side, 0), a)
                one = self.transposed(functools.partial(self.c, side, 2), a)
                two = self.transposed(functools.partial(self.c, side, 3), a)
                if side == 1:
                    outer = self.transposed(self.c_e2, beyond)
                for j in range(3):
                    t = roll(one[j], 64, 1)
                    y = total[j] - roll(col[j], 1, 1) - jnp.where(sec_zero, from_below(t), t) - from_below(two[j])
                    if side == 0:
                        y = y - jnp.where(row_zero, roll(t_row[1][j], -32, 1), roll(t_row[0][j], 32, 1))
                    else:
                        y = y - jnp.where(row_zero, roll(t_row[0][j], -32, 1), roll(outer[j], 32, 1))
                    outs[side][3 * half + j] = y
        return outs


def window_kernel(got, blocks, v0, e0, v1, e1, v2):
    n_dev = got.shape[0] // (2 * DOUBLE)
    row_zero, sec_zero = lane_bits((2 * n_dev, 128))
    zero = jnp.zeros((2 * n_dev, 128), jnp.float32)

    def row(i):
        return jnp.concatenate(
            [got[pl.ds(slot * DOUBLE + i, n_dev, stride=2 * DOUBLE), :] for slot in range(2)], axis=0
        )

    def from_two(value, packed_second=False):
        if not packed_second:
            value = roll(value, 64, 1)
        return from_below(jnp.where(sec_zero, value, zero))

    def s_terms(three, two):
        return [
            from_below(row(three + i)) + from_two(row(two + i % 3), packed_second=i >= 3) for i in range(6)
        ]

    starts = []
    for side, at in enumerate((0, AT_E)):
        base = side * 42
        for i in range(36):
            blocks[base + 6 + i] = row(at + AT_C + i)
        two = [blocks[base + 24 + i] for i in (6, 7, 8)]
        three = [blocks[base + 33 + i] for i in (6, 7, 8)]
        pair, last = row(at + AT_TWO + 3), row(at + AT_TWO + 4)
        G_two = [from_two(z) for z in (pair, pair, two[0], last, two[1], two[2])]
        G_two[1] = from_two(pair, packed_second=True)
        G_three = [row(at + AT_THREE), row(at + AT_THREE + 1), three[0], row(at + AT_THREE + 2), three[1], three[2]]
        for i in range(6):
            blocks[base + i] = row(at + i) + G_two[i] + from_below(G_three[i])
        terms = s_terms(at + AT_THREE + 3, at + AT_TWO)
        starts.append([row(at + 6 + i) - terms[i] for i in range(6)])
    for i in range(5):
        packed = row(AT_E2 + i)
        blocks[84 + i] = packed
        if i < 4:
            blocks[89 + i] = roll(packed, -32, 1)
    terms = s_terms(AT_E2 + 11, AT_E2 + 17)
    outer = [row(AT_E2 + 5 + i) - terms[i] for i in range(6)]
    window = Window(lambda i: blocks[i], n_dev)
    v, e = starts
    w, f = window.apply(v, e, outer, (0, 1))
    last, _ = window.apply(w, f, f, (0,))
    for i in range(6):
        v0[i] = v[i]
        e0[i] = e[i]
        v1[i] = w[i]
        e1[i] = f[i]
        v2[i] = last[i]


def moments_kernel(blocks, v0, v1, v2, above, below, kept_hbm, e2, v3, e3, out, kept, sems):
    fetches = [pltpu.make_async_copy(kept_hbm, kept, sems.at[0])]
    for fetch in fetches:
        fetch.start()
    shape = v2.shape[1:]
    n_dev = shape[0] // 2
    bits = lane_bits(shape)
    row_zero, _ = bits
    window = Window(lambda i: blocks[i], n_dev)
    v = [v2[i] for i in range(6)]
    side = [jnp.where(row_zero, above[i], below[i]) for i in range(6)]
    outer = [jnp.where(row_zero, below[i], above[i]) for i in range(6)]
    w, f = window.apply(v, side, outer, (0, 1))
    for i in range(6):
        e2[i] = side[i]
        v3[i] = w[i]
        e3[i] = f[i]
    vs = [[v0[i] for i in range(6)], [v1[i] for i in range(6)], v, w]

    def dot(left, right):
        return sum(a[:n_dev] * b[:n_dev] for a, b in zip(left, right))

    products = [dot(vs[n // 2], vs[n - n // 2]) for n in range(7)]
    energy = 0.0
    for half in range(2):
        a = w[3 * half : 3 * half + 3]
        b = f[3 * half : 3 * half + 3]
        after = [window.seconds(a[j], jnp.where(row_zero, roll(a[j], -32, 1), roll(b[j], 32, 1))) for j in range(3)]
        for i in range(3):
            inner = sum(window.d(0, i, j) * a[j] for j in range(3))
            for kind in range(4):
                inner = inner - 2.0 * sum(window.c(0, kind, i, j) * after[j][kind] for j in range(3))
            energy = energy + a[i][:n_dev] * inner[:n_dev]
    products.append(energy)
    lane = lax.broadcasted_iota(jnp.int32, (1, 128), 1)
    packed = jnp.zeros((1, 128), jnp.float32)
    for n, value in enumerate(products):
        value = jnp.sum(jnp.sum(value, axis=0, keepdims=True), axis=1, keepdims=True)
        packed = jnp.where(lane == n, value, packed)
    out[...] = packed
    for fetch in fetches:
        fetch.wait()


def coefficients(moments):
    zero = jnp.zeros_like(moments[0])

    def inner(s, p, offset):
        total = zero
        for i, a in enumerate(s):
            for j, b in enumerate(p):
                total = total + a * b * moments[i + j + offset]
        return total

    def energy(p):
        return inner(p, p, 1) + HALF * inner(p, p, 0)

    s = [zero + 1.0]
    p = [zero + 1.0]
    x = [zero] * ITERS
    gamma = inner(s, s, 0)
    for sweep in range(ITERS):
        alpha = gamma / energy(p)
        x = [x[i] + (alpha * p[i] if i < len(p) else 0.0) for i in range(ITERS)]
        if sweep < ITERS - 1:
            image = [(p[i - 1] if i else 0.0) + (HALF * p[i] if i < len(p) else 0.0) for i in range(len(p) + 1)]
            s = [(s[i] if i < len(s) else 0.0) - alpha * image[i] for i in range(len(image))]
            gamma_new = inner(s, s, 0)
            beta = gamma_new / gamma
            p = [s[i] + (beta * p[i] if i < len(p) else 0.0) for i in range(len(s))]
            gamma = gamma_new
    return [value * (1.0 / SPAN) for value in x]


def finish_kernel(alive_ref, sums, v0, v1, v2, v3, n0, n1, n2, n3, kept, affines_hbm, residual_hbm, affines, residual, sems):
    stores = []
    total = jnp.sum(sums[...], axis=0, keepdims=True)
    lane = lax.broadcasted_iota(jnp.int32, (1, 128), 1)
    moments = [jnp.sum(jnp.where(lane == n, total, 0.0), axis=1, keepdims=True) for n in range(8)]
    weights = coefficients(moments)
    at = lax.axis_index("x") * lax.axis_size("core") + lax.axis_index("core")
    alive = [alive_ref[kind : kind + 1, :] for kind in range(4)]
    row_zero, sec_zero = lane_bits((1, 128))

    def mix(refs, i, dev):
        return sum(w * ref[i, pl.ds(dev, 1), :] for w, ref in zip(weights, refs))

    vs = (v0, v1, v2, v3)
    x = [mix(vs, i, at) for i in range(6)]
    above = [mix(vs, i, at + 1) for i in range(6)]
    beside = [mix((n0, n1, n2, n3), i, at) for i in range(6)]
    for i in range(6):
        for sec in range(2):
            for row in range(2):
                start = 64 * sec + 32 * row
                affines[i, sec, row : row + 1, :] = x[i][:, start : start + 32]
    stores.append(pltpu.make_async_copy(affines, affines_hbm, sems.at[4]))
    stores[-1].start()
    for kind in range(4):
        if kind == 0:
            b = [roll(z, -1, 1) for z in x]
        elif kind == 1:
            b = [jnp.where(row_zero, roll(z, -32, 1), roll(w, 32, 1)) for z, w in zip(x, beside)]
        elif kind == 2:
            b = [jnp.where(sec_zero, roll(z, 64, 1), roll(w, 64, 1)) for z, w in zip(x, above)]
        else:
            b = above
        u, v, p, q = (kept[4 * kind + i] for i in range(4))
        live = live_points(alive[kind])
        for comp in range(2):
            o = 3 * comp
            r = (p - u) if comp == 0 else (q - v)
            r = r - (x[o] * u + x[o + 1] * v) + (b[o] * p + b[o + 1] * q) - live * (x[o + 2] - b[o + 2])
            residual[pl.ds(kind * 256 + comp, 128, stride=2), :] = r.T
        part = pl.ds(kind * 256, 256)
        stores.append(pltpu.make_async_copy(residual.at[part], residual_hbm.at[part], sems.at[kind]))
        stores[-1].start()
    for store in stores:
        store.wait()


def shape_of(*shape):
    return jax.ShapeDtypeStruct(shape, jnp.float32)


def call(interpret, kernel, outs, *args, scalars=0, anywhere=(), copies=0, buffers=(), results=None):
    spaces = []
    args = list(args)
    shapes = [shape_of(*out) for out in outs]
    for n, arg in enumerate(args):
        if n < scalars:
            spaces.append(pl.BlockSpec(memory_space=pltpu.SMEM))
        elif n in anywhere:
            spaces.append(pl.BlockSpec(memory_space=pl.ANY))
        else:
            spaces.append(pl.BlockSpec(memory_space=pltpu.VMEM))
            if arg.dtype == jnp.float32 and not interpret:
                args[n] = pltpu.with_memory_space_constraint(arg, pltpu.VMEM)
    if not results and not interpret:
        shapes = [pltpu.VMEM(out, jnp.float32) for out in outs]
    results = results or [pltpu.VMEM] * len(outs)
    return pl.pallas_call(
        kernel,
        out_shape=shapes,
        in_specs=spaces,
        out_specs=[pl.BlockSpec(memory_space=space) for space in results],
        scratch_shapes=list(buffers)
        + ([pltpu.SemaphoreType.DMA((copies,))] if copies else []),
        interpret=interpret,
    )(*args)


def shifted(value, axes, steps):
    count = lax.axis_size(axes)
    pairs = [(i, i + steps) for i in range(count) if 0 <= i + steps < count]
    return lax.ppermute(value, axes, pairs)


def pack_up(run, g):
    return run(pack_up_kernel, [(192, 128), (192, 128)], g, anywhere=(0,), copies=3)


def pack_rows(run, f, g, counts, sizes):
    return run(
        functools.partial(pack_rows_kernel, sizes),
        [(128, 128), (136, 128), (8, 128)],
        f,
        g,
        counts,
        anywhere=(0, 1, 2),
        copies=5,
        buffers=[pltpu.VMEM(counts.shape, jnp.int32)],
    )


def per_device(interpret, first_pts, second_pts, counts):
    run = functools.partial(call, interpret)
    n_sec = lax.axis_size(SEC_AXES)
    n_dev = lax.axis_size(GROUP)
    n_group = n_sec // n_dev
    f = first_pts.reshape(1024, 128)
    g = second_pts.reshape(1024, 128)
    up, rest = pack_up(run, g)
    up = shifted(up, SEC_AXES, -1)
    relay = n_dev - 2
    inside = [(i + 1, i) for i in range(n_sec - 1) if (i + 1) % n_dev]
    to_relay = [(group * n_dev, group * n_dev + relay) for group in range(1, n_group)]
    from_relay = [(group * n_dev + relay, group * n_dev - 1) for group in range(1, n_group)]
    relayed = lax.ppermute(rest, SEC_AXES, to_relay)
    relayed, f_later, g_later = lax.optimization_barrier((relayed, f, g))
    outside = lax.ppermute(relayed, SEC_AXES, from_relay)
    sizes = (n_sec, lax.axis_size("row"))
    beside, odd, alive, rest = lax.optimization_barrier((*pack_rows(run, f_later, g_later, counts, sizes), rest))
    beside = shifted(beside, "row", -1)
    low = shifted(odd, "row", 1)
    rest = lax.ppermute(rest, SEC_AXES, inside)
    packet, kept = run(gram_kernel, [(ROWS, 128), (16, 128, 128)], f, g, alive, up, rest, outside, beside, low)

    half = n_dev // 2
    pairs = []
    for group in range(n_group):
        for dev in range(n_dev):
            source = group + (1 if dev < half else -1)
            if 0 <= source < n_group:
                pairs.append((source * n_dev + dev, group * n_dev + dev))
    other = lax.ppermute(packet, SEC_AXES, pairs)
    both = jnp.concatenate([packet, other], axis=0)
    (mine,) = run(merge_kernel, [(2 * DOUBLE, 128)], both, shifted(both, "row", -1), shifted(both, "row", 1))
    got = lax.all_to_all(jnp.broadcast_to(mine[None], (n_dev, 2 * DOUBLE, 128)), GROUP, 0, 0, tiled=False)
    wide = (6, 2 * n_dev, 128)
    blocks, v0, e0, v1, e1, v2 = run(
        window_kernel, [(93, 2 * n_dev, 128)] + [wide] * 5, got.reshape(n_dev * 2 * DOUBLE, 128)
    )
    e2, v3, e3, part, kept = run(
        moments_kernel,
        [wide, wide, wide, (1, 128), (16, 128, 128)],
        blocks,
        v0,
        v1,
        v2,
        shifted(v2, "row", -1),
        shifted(v2, "row", 1),
        kept,
        anywhere=(6,),
        copies=1,
    )
    n_other = lax.axis_size(OTHERS)
    groups = sum_groups([lax.axis_size(axis) for axis in EVERY])
    sums = lax.all_to_all(
        jnp.broadcast_to(part[None], (n_other, 1, 128)), EVERY, 0, 0, axis_index_groups=groups, tiled=False
    )
    affines, residual = run(
        finish_kernel,
        [(6,) + counts.shape[1:], (1024, 128)],
        alive,
        sums.reshape(n_other, 128),
        v0,
        v1,
        v2,
        v3,
        e0,
        e1,
        e2,
        e3,
        kept,
        copies=5,
        buffers=[pltpu.VMEM((6,) + counts.shape[1:], jnp.float32), pltpu.VMEM((1024, 128), jnp.float32)],
        results=[pl.ANY, pl.ANY],
    )
    return affines, residual.reshape(first_pts.shape)


def sum_groups(sizes):
    n_y, n_zhi, n_x, n_core, n_row = sizes
    n_z = n_zhi * n_row
    first = 5 * n_z // 8
    groups = []
    for place in range(n_x * n_core):
        order = [((first + step) % n_z, y) for step in range(n_z) for y in reversed(range(n_y))]
        groups.append([((y * n_zhi + z // n_row) * n_x * n_core + place) * n_row + z % n_row for z, y in order])
    return groups


def split_mesh(mesh):
    n_row = mesh.shape["row"]
    return Mesh(mesh.devices.reshape(4, 4, 4, 2, n_row), SEC_AXES + ("row",))


def solution(mesh, inner=None, interpret=False):
    inner = inner or split_mesh(mesh)
    in_specs = (
        P(None, SEC_AXES, "row", None, None, None),
        P(None, SEC_AXES, "row", None, None, None),
        P(None, SEC_AXES, "row", None),
    )
    out_specs = (P(None, SEC_AXES, "row", None), P(None, SEC_AXES, "row", None, None, None))
    return jax.shard_map(
        functools.partial(per_device, interpret), mesh=inner, in_specs=in_specs, out_specs=out_specs, check_vma=False
    )
```
